32 devices in a mesh: rep: 8 (over z, y), grp: 4 (over x, core).
Axes of the slice: x: 2, y: 2, z: 4, core: 2. Of those that a mesh axis runs over, the one named last changes fastest.
Arguments:
- tokens: bfloat16 [3648, 1152], P(('rep', 'grp')), may hold values from -6 to 6
- cotangent: bfloat16 [3648, 1152], P(('rep', 'grp')), may hold values from -6 to 6
- slice_sizes: int32 [32], replicated, may hold values from 113 to 114, as said below
- gain_one: float32 [1152], replicated, may hold values from 0.1 to 1.9
- shift_one: float32 [1152], replicated, may hold values from -3 to 3
- attn_in: bfloat16 [3456, 1152], P('grp')
- attn_bias: float32 [2, 1152], replicated, may hold values from -3 to 3
- attn_out: bfloat16 [1152, 1152], P('grp'), may hold values from -1 to 1
- out_bias: float32 [1152], replicated, may hold values from -3 to 3
- gain_two: float32 [1152], replicated, may hold values from 0.1 to 1.9
- shift_two: float32 [1152], replicated, may hold values from -3 to 3
- mlp_up: bfloat16 [4304, 1152], P('grp'), may hold values from -0.1875 to 0.1875
- up_bias: float32 [4304], replicated, may hold values from -3 to 3
- mlp_down: bfloat16 [4304, 1152], P('grp'), may hold values from -0.09375 to 0.09375
- down_bias: float32 [1152], replicated, may hold values from -3 to 3
Outputs:
- block_output: bfloat16 [3648, 1152], P(('rep', 'grp'))
- input_grad: float32 [3648, 1152], P(('rep', 'grp'))
- dgain_one: float32 [1152], replicated
- dshift_one: float32 [1152], replicated
- dattn_in: float32 [3456, 1152], P('grp', 'rep')
- dattn_bias: float32 [2, 1152], replicated
- dattn_out: float32 [1152, 1152], P('grp', 'rep')
- dout_bias: float32 [1152], replicated
- dgain_two: float32 [1152], replicated
- dshift_two: float32 [1152], replicated
- dmlp_up: float32 [4304, 1152], P('grp', 'rep')
- dup_bias: float32 [4304], replicated
- dmlp_down: float32 [4304, 1152], P('grp', 'rep')
- ddown_bias: float32 [1152], replicated
The draws below stay inside these ranges and needn't reach their ends.
Inputs may be any that keep to these rules, and one draw needn't show every extreme that they name: slice_sizes sums to 3645; every entry is 113 or one more.
All inputs are finite; a program needn't handle non-finite values.
Results may differ from the reference program's by a relative error of at most 0.012.
Values may be sent and summed in bfloat16 or wider, within the bound.
A program may use at most 192 MiB of HBM per device.

```python
import jax
import jax.numpy as jnp
from jax import lax

D = 1152
H = 16
HD = 72
FF = 4304
IMG = 729
SHARDS = 32
NIMG = 5
TOKENS = 3645
SLOTS = 3648


def draw_slice_sizes(key, part):
    ranking = jax.random.permutation(key, SHARDS)
    extra = (ranking < TOKENS % SHARDS).astype(jnp.int32)
    return (TOKENS // SHARDS + extra).astype(jnp.int32)


def draw_attn_in(key, part):
    base = jax.random.normal(key, (3 * D, D), jnp.float32) * D ** (-0.5)
    return base.astype(jnp.bfloat16)


def raised(values, own_key, source, target, shards_of, factor):
    owner, partner = [(jnp.arange(values.shape[axis_at]) // (values.shape[axis_at] // shards_of)).reshape([-1 if axis == axis_at else 1 for axis in range(values.ndim)]) for axis_at in (source, target)]
    chosen = jax.random.permutation(own_key, shards_of)[partner]
    strong = (owner == chosen) | (owner == (partner + shards_of // 2) % shards_of)
    return jnp.where(strong, factor * values, values)


def steps_of(stream_key, dims, pieces, smallest, largest):
    def one(axis_at, blocks):
        heights = jax.random.uniform(jax.random.fold_in(jax.random.fold_in(stream_key, 6), axis_at), (blocks,), jnp.float32, smallest / len(pieces), largest / len(pieces))
        return jnp.repeat(jnp.exp(heights), dims[axis_at] // blocks).reshape((-1,) + (1,) * (len(dims) - axis_at - 1))

    gain = one(*pieces[0])
    for cut in pieces[1:]:
        gain = gain * one(*cut)
    return gain


def normal_values(own_key, extent, scale, reach, cuts=(), held_as=jnp.bfloat16):
    gain = steps_of(own_key, extent, cuts, -0.22, 0.18) if cuts else 1.0
    values = jax.random.normal(own_key, extent, jnp.float32) * scale * gain
    return jnp.minimum(jnp.maximum(values, -reach), reach).astype(held_as)


def noise_with(rng, extent, width, bound, split, heavy, kind=jnp.bfloat16):
    result = width * jax.random.normal(rng, extent, jnp.float32)
    if split:
        result = result * steps_of(rng, extent, split, -0.22, 0.18)
    return jnp.clip(raised(result, jax.random.fold_in(rng, 3), *heavy), -bound, bound).astype(kind)


def setup_inputs(seed: int = 0) -> dict:
    splits = jax.random.split(jax.random.key(seed), 16)
    tokens = noise_with(splits[0], (SLOTS, D), 1.0, 6.0, ((0, 32),), (0, 1, 32, 2.75))
    cotangent = noise_with(splits[1], (SLOTS, D), 1.0, 6.0, ((0, 32),), (0, 1, 32, 2.75))
    slice_sizes = draw_slice_sizes(jax.random.fold_in(splits[15], 71), 0)
    gain_one = jnp.clip(1.0 + 0.18 * jax.random.normal(splits[3], (D,), jnp.float32), 0.1, 1.9)
    shift_one = normal_values(splits[4], (D,), 0.5, 3.0, (), jnp.float32)
    attn_in = draw_attn_in(jax.random.fold_in(splits[15], 71), 0)
    attn_bias = normal_values(splits[6], (2, D), 0.5, 3.0, (), jnp.float32)
    attn_out = normal_values(splits[7], (D, D), (D // 27) ** -0.5, 1.0, ((0, 4),))
    out_bias = normal_values(splits[8], (D,), 0.5, 3.0, (), jnp.float32)
    gain_two = jnp.clip(1.0 + 0.18 * jax.random.normal(splits[9], (D,), jnp.float32), 0.1, 1.9)
    shift_two = normal_values(splits[10], (D,), 0.5, 3.0, (), jnp.float32)
    mlp_up = normal_values(splits[11], (FF, D), D ** -0.5, 0.1875, ((0, 4),))
    up_bias = normal_values(splits[12], (FF,), 0.5, 3.0, (), jnp.float32)
    mlp_down = normal_values(splits[13], (FF, D), FF ** -0.5, 0.09375, ((0, 4),))
    down_bias = normal_values(splits[14], (D,), 0.5, 3.0, (), jnp.float32)
    return {"tokens": tokens, "cotangent": cotangent, "slice_sizes": slice_sizes, "gain_one": gain_one, "shift_one": shift_one, "attn_in": attn_in, "attn_bias": attn_bias, "attn_out": attn_out, "out_bias": out_bias, "gain_two": gain_two, "shift_two": shift_two, "mlp_up": mlp_up, "up_bias": up_bias, "mlp_down": mlp_down, "down_bias": down_bias}


EPSILON = 1e-06
SQRT_TWO_PI = 0.7978845608028654
CUBIC = 0.044715

def norm_forward(rows, gain_row, shift_row):
    centered = rows - lax.optimization_barrier(jnp.mean(rows, axis=-1, keepdims=True))
    inverse = lax.rsqrt(lax.optimization_barrier(jnp.mean(centered * centered, axis=-1, keepdims=True)) + EPSILON)
    normed = centered * inverse
    return (normed, inverse, normed * gain_row + shift_row)

def norm_backward(dscaled, normed, inverse, gain_row):
    dnormed = dscaled * gain_row
    return inverse * (dnormed - lax.optimization_barrier(jnp.mean(dnormed, axis=-1, keepdims=True)) - normed * lax.optimization_barrier(jnp.mean(dnormed * normed, axis=-1, keepdims=True)))

def gelu_parts(before):
    inside = SQRT_TWO_PI * (before + CUBIC * before * before * before)
    tangent = jnp.tanh(inside)
    activated = 0.5 * before * (1.0 + tangent)
    derivative = 0.5 * (1.0 + tangent) + 0.5 * before * (1.0 - tangent * tangent) * SQRT_TWO_PI * (1.0 + 3.0 * CUBIC * before * before)
    return (activated, derivative)

def reference(tokens, cotangent, slice_sizes, gain_one, shift_one, attn_in, attn_bias, attn_out, out_bias, gain_two, shift_two, mlp_up, up_bias, mlp_down, down_bias):
    shards = slice_sizes.shape[0]
    capacity = tokens.shape[0] // shards
    starts = (jnp.cumsum(slice_sizes) - slice_sizes).astype(jnp.int32)
    slot_shard = jnp.repeat(jnp.arange(shards, dtype=jnp.int32), capacity)
    slot_row = jnp.tile(jnp.arange(capacity, dtype=jnp.int32), shards)
    slot_live = slot_row < slice_sizes[slot_shard]
    slot_token = jnp.where(slot_live, starts[slot_shard] + slot_row, TOKENS).astype(jnp.int32)
    stream = jnp.zeros((TOKENS, D), tokens.dtype).at[slot_token].set(tokens, mode='drop')
    cot_stream = jnp.zeros((TOKENS, D), cotangent.dtype).at[slot_token].set(cotangent, mode='drop')
    score_scale = HD ** (-0.5)
    bias_full = jnp.concatenate([attn_bias[0], jnp.zeros((D,), jnp.float32), attn_bias[1]])

    def image_pass(carry, inputs):
        rows, cot_rows = inputs
        tokens_f = rows.astype(jnp.float32)
        normed_one, inverse_one, scaled_one = norm_forward(tokens_f, gain_one, shift_one)
        first = scaled_one.astype(jnp.bfloat16)
        projected = jnp.dot(first, attn_in.T, preferred_element_type=jnp.float32) + bias_full
        queries = projected[:, :D].astype(jnp.bfloat16).reshape(IMG, H, HD)
        keys3 = projected[:, D:2 * D].astype(jnp.bfloat16).reshape(IMG, H, HD)
        values3 = projected[:, 2 * D:].astype(jnp.bfloat16).reshape(IMG, H, HD)
        scores = jnp.einsum('qhd,khd->hqk', queries.astype(jnp.float32), keys3.astype(jnp.float32)) * score_scale
        highest = lax.optimization_barrier(jnp.max(scores, axis=-1, keepdims=True))
        logsum = highest + jnp.log(lax.optimization_barrier(jnp.sum(jnp.exp(scores - highest), axis=-1, keepdims=True)))
        probs = jnp.exp(scores - logsum)
        weights = probs.astype(jnp.bfloat16)
        mixed = jnp.einsum('hqk,khd->qhd', weights.astype(jnp.float32), values3.astype(jnp.float32)).astype(jnp.bfloat16).reshape(IMG, D)
        resid = tokens_f + jnp.dot(mixed, attn_out, preferred_element_type=jnp.float32) + out_bias
        normed_two, inverse_two, scaled_two = norm_forward(resid, gain_two, shift_two)
        second = scaled_two.astype(jnp.bfloat16)
        before = jnp.dot(second, mlp_up.T, preferred_element_type=jnp.float32) + up_bias
        activated, derivative = gelu_parts(before)
        hidden = activated.astype(jnp.bfloat16)
        final = resid + jnp.dot(hidden, mlp_down, preferred_element_type=jnp.float32) + down_bias
        dfinal = cot_rows.astype(jnp.float32)
        dmlp_down = jnp.dot(hidden.T, cot_rows, preferred_element_type=jnp.float32)
        dbefore = jnp.dot(cot_rows, mlp_down.T, preferred_element_type=jnp.float32) * derivative
        dbefore_b = dbefore.astype(jnp.bfloat16)
        dmlp_up = jnp.dot(dbefore_b.T, second, preferred_element_type=jnp.float32)
        dsecond = jnp.dot(dbefore_b, mlp_up, preferred_element_type=jnp.float32)
        dresid = dfinal + norm_backward(dsecond, normed_two, inverse_two, gain_two)
        dresid_b = dresid.astype(jnp.bfloat16)
        dattn_out = jnp.dot(mixed.T, dresid_b, preferred_element_type=jnp.float32)
        dmixed = jnp.dot(dresid_b, attn_out.T, preferred_element_type=jnp.float32).astype(jnp.bfloat16)
        dmixed3 = dmixed.reshape(IMG, H, HD)
        delta = lax.optimization_barrier(jnp.sum(dmixed3.astype(jnp.float32) * mixed.reshape(IMG, H, HD).astype(jnp.float32), axis=-1)).T
        dprob = jnp.einsum('qhd,khd->hqk', dmixed3.astype(jnp.float32), values3.astype(jnp.float32))
        dscore = (probs * (dprob - delta[:, :, None]) * score_scale).astype(jnp.bfloat16)
        dquery = jnp.einsum('hqk,khd->qhd', dscore.astype(jnp.float32), keys3.astype(jnp.float32)).reshape(IMG, D)
        dkey = jnp.einsum('hqk,qhd->khd', dscore.astype(jnp.float32), queries.astype(jnp.float32)).reshape(IMG, D)
        dvalue = jnp.einsum('hqk,qhd->khd', weights.astype(jnp.float32), dmixed3.astype(jnp.float32)).reshape(IMG, D)
        dprojected = jnp.concatenate([dquery, dkey, dvalue], axis=1).astype(jnp.bfloat16)
        dattn_in = jnp.dot(dprojected.T, first, preferred_element_type=jnp.float32)
        dfirst = jnp.dot(dprojected, attn_in, preferred_element_type=jnp.float32)
        input_rows = dresid + norm_backward(dfirst, normed_one, inverse_one, gain_one)
        terms = (lax.optimization_barrier(jnp.sum(dfirst * normed_one, axis=0)), lax.optimization_barrier(jnp.sum(dfirst, axis=0)), dattn_in, jnp.stack([lax.optimization_barrier(jnp.sum(dquery, axis=0)), lax.optimization_barrier(jnp.sum(dvalue, axis=0))]), dattn_out, lax.optimization_barrier(jnp.sum(dresid, axis=0)), lax.optimization_barrier(jnp.sum(dsecond * normed_two, axis=0)), lax.optimization_barrier(jnp.sum(dsecond, axis=0)), dmlp_up, lax.optimization_barrier(jnp.sum(dbefore, axis=0)), dmlp_down, lax.optimization_barrier(jnp.sum(dfinal, axis=0)))
        carry = tuple((total + term for total, term in zip(carry, terms)))
        return (carry, (final.astype(jnp.bfloat16), input_rows))
    zero_f = jnp.float32(0.0)
    init = (jnp.zeros((D,), jnp.float32), jnp.zeros((D,), jnp.float32), jnp.zeros((3 * D, D), jnp.float32), jnp.zeros((2, D), jnp.float32), jnp.zeros((D, D), jnp.float32), jnp.zeros((D,), jnp.float32), jnp.zeros((D,), jnp.float32), jnp.zeros((D,), jnp.float32), jnp.zeros((FF, D), jnp.float32), jnp.zeros((FF,), jnp.float32), jnp.zeros((FF, D), jnp.float32), jnp.zeros((D,), jnp.float32) + zero_f)
    totals, (out_images, grad_images) = lax.scan(image_pass, init, (stream.reshape(NIMG, IMG, D), cot_stream.reshape(NIMG, IMG, D)))
    out_stream = out_images.reshape(TOKENS, D)
    grad_stream = grad_images.reshape(TOKENS, D)
    fetch = jnp.minimum(slot_token, TOKENS - 1).astype(jnp.int32)
    live_col = slot_live[:, None]
    block_output = jnp.where(live_col, out_stream[fetch], jnp.zeros_like(out_stream[fetch]))
    input_grad = jnp.where(live_col, grad_stream[fetch], jnp.zeros_like(grad_stream[fetch]))
    dgain_one, dshift_one, dattn_in, dattn_bias, dattn_out, dout_bias, dgain_two, dshift_two, dmlp_up, dup_bias, dmlp_down, ddown_bias = totals
    return (block_output, input_grad, dgain_one, dshift_one, dattn_in, dattn_bias, dattn_out, dout_bias, dgain_two, dshift_two, dmlp_up, dup_bias, dmlp_down, ddown_bias)
```

```python
import functools

import jax
import jax.numpy as jnp
from jax import lax
from jax.experimental import pallas as pl
from jax.experimental.pallas import tpu as pltpu
from jax.sharding import PartitionSpec as P

H = 16
HD = 72
HP = 80
IMG = 729
GROUP = 4
NEAR_GROUPS = 2
WINDOW = (2 * NEAR_GROUPS + 1) * GROUP
OWN = NEAR_GROUPS * GROUP
OFFSETS = (1, -1, 2, -2)

EPSILON = 1e-06
SQRT_TWO_PI = 0.7978845608028654
CUBIC = 0.044715
NEGATIVE = -1e30
SCALE = HD ** (-0.5)
LOG2E = 1.4426950408889634
BF = jnp.bfloat16
F32 = jnp.float32
MESH = pl.DeviceIdType.MESH


def norm_parts(rows):
    centered = rows - jnp.mean(rows, axis=-1, keepdims=True)
    inverse = lax.rsqrt(jnp.mean(centered * centered, axis=-1, keepdims=True) + EPSILON)
    return centered * inverse, inverse


def norm_backward(dscaled, normed, inverse, gain_row):
    dnormed = dscaled * gain_row
    return inverse * (
        dnormed
        - jnp.mean(dnormed, axis=-1, keepdims=True)
        - normed * jnp.mean(dnormed * normed, axis=-1, keepdims=True)
    )


def gelu_parts(before):
    square = before * before
    tangent = jnp.tanh(SQRT_TWO_PI * before * (1.0 + CUBIC * square))
    half = 0.5 * (1.0 + tangent)
    derivative = half + 0.5 * before * (1.0 - tangent * tangent) * (
        SQRT_TWO_PI + SQRT_TWO_PI * 3.0 * CUBIC * square
    )
    return before * half, derivative


def dot_over(left, right, left_axis, right_axis):
    return lax.dot_general(
        left, right, (((left_axis,), (right_axis,)), ((), ())), preferred_element_type=F32
    )


class Place:
    def __init__(self, capacity, reps):
        self.capacity, self.reps = capacity, reps
        self.devices = reps * GROUP
        self.images = capacity * self.devices // IMG
        self.short = capacity * self.devices - self.images * IMG
        self.rep, self.member = lax.axis_index("rep"), lax.axis_index("grp")
        low = lax.rem(self.member, 2)
        self.near = self.member + 1 - 2 * low
        self.far = lax.rem(self.member + 2, GROUP)
        self.diagonal = lax.rem(self.near + 2, GROUP)
        self.pair = lax.div(self.member, 2)

    def first_image(self, block):
        return lax.div(
            block * self.capacity - jnp.minimum(block, self.short), jnp.int32(IMG)
        )

    def last_image(self, block):
        end = block + 1
        full = self.devices - self.short
        token = end * self.capacity - jnp.maximum(end - full, 0) - 1
        return jnp.minimum(lax.div(token, jnp.int32(IMG)), self.images - 1)

    def shares(self, block, group):
        inside = (block >= 0) & (block < self.devices) & (group >= 0) & (group < self.reps)
        block = jnp.clip(block, 0, self.devices - 1)
        group = jnp.clip(group, 0, self.reps - 1)
        return (
            inside
            & (self.first_image(block) <= self.last_image(group * GROUP + GROUP - 1))
            & (self.first_image(group * GROUP) <= self.last_image(block))
        )

    def group_barrier(self):
        barrier = pltpu.get_barrier_semaphore()
        for other in (self.near, self.far):
            pl.semaphore_signal(
                barrier, inc=1, device_id=(self.rep, other), device_id_type=MESH
            )
        return barrier, 2

    def wide_barrier(self):
        barrier, count = self.group_barrier()
        count = jnp.int32(count)
        for offset in OFFSETS:
            there = self.rep + offset
            valid = (there >= 0) & (there < self.reps)

            @pl.when(valid)
            def _():
                pl.semaphore_signal(
                    barrier, inc=1, device_id=(there, self.member), device_id_type=MESH
                )

            count = count + jnp.where(valid, 1, 0)
        return barrier, count


def remote(source, target, send, recv, place):
    return pltpu.make_async_remote_copy(
        src_ref=source,
        dst_ref=target,
        send_sem=send,
        recv_sem=recv,
        device_id=place,
        device_id_type=MESH,
    )


class Gather:
    def __init__(self, place, ref, rows, send, recv):
        self.place, self.ref, self.rows, self.send, self.recv = place, ref, rows, send, recv
        self.half = rows // 2

    def copy(self, owner, part, slot, target):
        if part is None:
            piece = self.ref.at[pl.ds(pl.multiple_of(owner * self.rows, self.rows), self.rows), :]
        else:
            start = pl.multiple_of(owner * self.rows + part * self.half, self.half)
            piece = self.ref.at[pl.ds(start, self.half), :]
        return remote(
            piece, piece, self.send.at[slot], self.recv.at[slot], (self.place.rep, target)
        )

    def start(self):
        p = self.place
        for part in range(2):
            self.copy(p.member, part, 1 + part, p.far).start()
        self.copy(p.member, None, 0, p.near).start()

    def wait_near(self):
        p = self.place
        self.copy(p.near, None, 0, p.near).wait_recv()

    def forward(self, part):
        p = self.place
        self.copy(p.far, part, 1 + part, p.far).wait_recv()
        self.copy(p.far, part, 3 + part, p.near).start()

    def wait_rest(self):
        p = self.place
        for part in range(2):
            self.copy(p.diagonal, part, 3 + part, p.near).wait_recv()

    def drain(self):
        p = self.place
        self.copy(p.member, None, 0, p.near).wait_send()
        for part in range(2):
            self.copy(p.member, part, 1 + part, p.far).wait_send()
            self.copy(p.far, part, 3 + part, p.near).wait_send()


class Scatter:
    def __init__(self, place, ref, held, stage, rows, send, recv):
        self.place, self.ref, self.held, self.stage = place, ref, held, stage
        self.rows, self.send, self.recv = rows, send, recv

    def block(self, owner):
        return pl.ds(pl.multiple_of(owner * self.rows, self.rows), self.rows)

    def ahead(self):
        p = self.place
        return remote(
            self.ref.at[self.block(p.diagonal), :], self.held.at[0],
            self.send.at[0], self.recv.at[0], (p.rep, p.near),
        )

    def own(self):
        p = self.place
        return remote(
            self.ref.at[self.block(p.near), :], self.held.at[1],
            self.send.at[1], self.recv.at[1], (p.rep, p.near),
        )

    def across(self):
        p = self.place
        return remote(
            self.stage, self.held.at[2], self.send.at[2], self.recv.at[2], (p.rep, p.far)
        )

    def pass_on(self):
        p = self.place
        self.ahead().wait_recv()
        self.stage[...] = (
            self.ref[self.block(p.far), :].astype(F32) + self.held[0].astype(F32)
        ).astype(BF)
        self.across().start()

    def result(self):
        p = self.place
        self.own().wait_recv()
        total = self.ref[self.block(p.member), :].astype(F32) + self.held[1].astype(F32)
        self.across().wait_recv()
        total = total + self.held[2].astype(F32)
        self.ahead().wait_send()
        self.own().wait_send()
        self.across().wait_send()
        return total


def exchange_copy(place, ref, kinds, offset, index, send, recv):
    slot_there = OWN - offset * GROUP + index
    return remote(
        ref.at[kinds, OWN + index],
        ref.at[kinds, slot_there],
        send.at[OFFSETS.index(offset) * GROUP + index],
        recv.at[slot_there],
        (place.rep + offset, place.member),
    )


def for_sent(place, act):
    for offset in OFFSETS:
        for index in range(GROUP):

            @pl.when(place.shares(place.rep * GROUP + index, place.rep + offset))
            def _():
                act(offset, index)


def for_received(place, act):
    for offset in OFFSETS:
        for index in range(GROUP):
            block = (place.rep + offset) * GROUP + index

            @pl.when(place.shares(block, place.rep))
            def _():
                act(offset, index)


def window_wait(place, ref, kinds, offset, index, send, recv):
    slot = OWN + offset * GROUP + index
    remote(
        ref.at[kinds, slot],
        ref.at[kinds, slot],
        send.at[0],
        recv.at[slot],
        (place.rep, place.near),
    ).wait_recv()


def front_kernel(
    capacity, reps, rows, tok_ref, cot_ref, gain_ref, shift_ref, w_ref, bias_ref,
    first_ref, win_ref, cotall_ref,
    xall, sbuf, gsend, grecv, csend, crecv, ssend, srecv, ksend, krecv,
):
    p = Place(capacity, reps)
    barrier, count = p.wide_barrier()
    own = pl.ds(pl.multiple_of(p.member * rows, rows), rows)
    xall[own, :] = tok_ref[...]
    cotall_ref[own, :] = cot_ref[...]
    pl.semaphore_wait(barrier, count)
    tokens = Gather(p, xall, rows, gsend, grecv)
    tokens.start()

    def normalize(owner):
        block = pl.ds(pl.multiple_of(owner * rows, rows), rows)
        normed, _ = norm_parts(xall[block, :].astype(F32))
        first_ref[block, :] = (normed * gain_ref[...] + shift_ref[...]).astype(BF)

    odd = lax.rem(p.member, 2)
    cross = 2 - 2 * odd
    kept = 2 * odd
    kind_of = lambda i: lax.div(3 * p.member + i, GROUP)

    def project(i, pair):
        block = first_ref[pl.ds(pl.multiple_of(pair * 2 * rows, 2 * rows), 2 * rows), :]
        part = dot_over(w_ref[i], block, 1, 1) + bias_ref[i]
        for b in range(2):
            sbuf[i, pair * 2 + b] = part[:, b * rows : (b + 1) * rows].astype(BF)

    def shuffle(i, pair, way, target):
        slot = way * 2 + pair
        return remote(
            sbuf.at[i, pl.ds(pair * 2, 2)],
            win_ref.at[kind_of(i), pl.ds(OWN + pair * 2, 2)],
            ssend.at[slot], srecv.at[slot], (p.rep, target),
        )

    normalize(p.member)
    tokens.wait_near()
    normalize(p.near)
    tokens.forward(0)
    project(cross, p.pair)
    shuffle(cross, p.pair, 0, p.far).start()
    tokens.forward(1)
    project(1, p.pair)
    shuffle(1, p.pair, 1, p.near).start()
    project(kept, p.pair)
    other = 1 - p.pair
    normalize(p.far)
    tokens.wait_rest()
    normalize(p.diagonal)
    project(cross, other)
    shuffle(cross, other, 0, p.far).start()
    project(1, other)
    shuffle(1, other, 1, p.near).start()
    project(kept, other)
    win_ref[kind_of(kept), pl.ds(OWN, GROUP)] = sbuf[kept]
    for pair in (p.pair, other):
        shuffle(cross, pair, 0, p.far).wait_recv()
        shuffle(1, pair, 1, p.near).wait_recv()
    cotangents = Gather(p, cotall_ref, rows, csend, crecv)
    cotangents.start()
    kinds = pl.ds(0, 3)
    for_sent(p, lambda o, i: exchange_copy(p, win_ref, kinds, o, i, ksend, krecv).start())
    cotangents.wait_near()
    cotangents.forward(0)
    cotangents.forward(1)
    cotangents.wait_rest()
    for_received(p, lambda o, i: window_wait(p, win_ref, kinds, o, i, ksend, krecv))
    for_sent(p, lambda o, i: exchange_copy(p, win_ref, kinds, o, i, ksend, krecv).wait_send())
    for pair in (p.pair, other):
        shuffle(cross, pair, 0, p.far).wait_send()
        shuffle(1, pair, 1, p.near).wait_send()
    tokens.drain()
    cotangents.drain()


def image_of(meta_ref, device, index):
    base, turn, size = meta_ref[0, device], meta_ref[1, device], meta_ref[2, device]
    image = jnp.where(index >= turn, base + 1, base)
    return jnp.where(index < size, image, -2)


def own_image_row(meta_ref, place, rows):
    index = lax.broadcasted_iota(jnp.int32, (1, rows), 1)
    return jnp.concatenate(
        [image_of(meta_ref, place.rep * GROUP + b, index) for b in range(GROUP)], axis=1
    )


def window_image_col(meta_ref, place, slot, rows):
    index = lax.broadcasted_iota(jnp.int32, (rows, 1), 0)
    block = jnp.clip(place.rep * GROUP + slot - OWN, 0, place.devices - 1)
    return image_of(meta_ref, block, index)


def attend_kernel(
    capacity, reps, rows, meta_ref, win_ref, mixed_ref, lse_ref, sbuf, best, total, acc
):
    p = Place(capacity, reps)
    query_image = own_image_row(meta_ref, p, rows)
    query_image = jnp.where(query_image < 0, -1, query_image)
    width = GROUP * rows

    def one_head(h, carry):
        head = pl.ds(pl.multiple_of(h * HP, HP), HP)
        best[...] = jnp.full_like(best, NEGATIVE)
        total[...] = jnp.zeros_like(total)
        acc[...] = jnp.zeros_like(acc)
        query = jnp.concatenate([win_ref[0, OWN + b, head, :] for b in range(GROUP)], axis=1)

        def scores(slot, carry):
            @pl.when(p.shares(p.rep * GROUP + slot - OWN, p.rep))
            def _():
                raw = dot_over(win_ref[1, slot, head, :], query, 0, 0)
                raw = jnp.where(
                    window_image_col(meta_ref, p, slot, rows) == query_image, raw, NEGATIVE
                )
                sbuf[slot] = raw
                best[...] = jnp.maximum(
                    best[...], jnp.max(raw.reshape(rows // 8, 8, width), axis=0)
                )

            return carry

        lax.fori_loop(0, WINDOW, scores, 0)
        top = jnp.max(best[...], axis=0, keepdims=True)

        def weigh(slot, carry):
            @pl.when(p.shares(p.rep * GROUP + slot - OWN, p.rep))
            def _():
                powers = jnp.exp2((sbuf[slot] - top) * (SCALE * LOG2E))
                total[...] += jnp.sum(powers.reshape(rows // 8, 8, width), axis=0)
                acc[...] += dot_over(win_ref[2, slot, head, :], powers.astype(BF), 1, 0)

            return carry

        lax.fori_loop(0, WINDOW, weigh, 0)
        whole = jnp.sum(total[...], axis=0, keepdims=True)
        mixed_ref[head, :] = (acc[...] / whole).astype(BF)
        lse_ref[pl.ds(h, 1), :] = top * SCALE + jnp.log(whole)
        return carry

    lax.fori_loop(0, GROUP, one_head, 0)


def middle_kernel(
    capacity, reps, rows, tok_ref, cot_ref, mixed_ref, lse_ref, wo_ref, wup_ref, wdn_ref,
    upb_ref, vec_ref,
    out_ref, dres_ref, dmix_ref, stats_ref, dresall_ref, dwup_ref, dwdn_ref, sums_ref, dupb_ref,
    part, part2, part3, second, hidden, dbefore, dact, res_scr, norm_scr, held, stage,
    asend, arecv, bsend, brecv, csend, crecv, dsend, drecv, esend, erecv,
):
    p = Place(capacity, reps)
    barrier, count = p.group_barrier()
    out_bias, gain, shift, down_bias = (vec_ref[pl.ds(i, 1), :] for i in range(4))
    block_of = lambda owner: pl.ds(pl.multiple_of(owner * rows, rows), rows)
    pair_of = lambda pair: pl.ds(pl.multiple_of(pair * 2 * rows, 2 * rows), 2 * rows)
    other = 1 - p.pair

    def attn_partial(owner):
        part[block_of(owner), :] = dot_over(
            mixed_ref[:, block_of(owner)], wo_ref[...], 0, 0
        ).astype(BF)

    attn_partial(p.diagonal)
    pl.semaphore_wait(barrier, count)
    one = Scatter(p, part, held.at[0], stage.at[0], rows, asend, arecv)
    one.ahead().start()
    attn_partial(p.near)
    one.own().start()
    attn_partial(p.far)
    one.pass_on()
    attn_partial(p.member)
    for pair in (0, 1):
        at = pl.ds(pair * 2 * rows, 2 * rows)
        dact[at, :] = dot_over(cot_ref[at, :], wdn_ref[...], 1, 1)
    resid = tok_ref[...].astype(F32) + one.result() + out_bias
    res_scr[...] = resid
    normed, inverse = norm_parts(resid)
    norm_scr[...] = normed
    second[block_of(p.member), :] = (normed * gain + shift).astype(BF)
    gather = Gather(p, second, rows, bsend, brecv)
    gather.start()

    def mlp(pair):
        at = pair_of(pair)
        before = dot_over(second[at, :], wup_ref[...], 1, 1) + upb_ref[...]
        activated, derivative = gelu_parts(before)
        hidden[at, :] = activated.astype(BF)
        grad = dact[at, :] * derivative
        dact[at, :] = grad
        dbefore[at, :] = grad.astype(BF)
        part2[at, :] = dot_over(dbefore[at, :], wup_ref[...], 1, 0).astype(BF)

    gather.wait_near()
    gather.forward(0)
    mlp(p.pair)
    gather.forward(1)
    two = Scatter(p, part2, held.at[1], stage.at[1], rows, csend, crecv)
    two.own().start()
    gather.wait_rest()
    mlp(other)
    two.ahead().start()

    def down(pair):
        at = pair_of(pair)
        part3[at, :] = dot_over(hidden[at, :], wdn_ref[...], 1, 0).astype(BF)

    down(other)
    two.pass_on()
    down(p.pair)
    three = Scatter(p, part3, held.at[2], stage.at[2], rows, esend, erecv)
    three.ahead().start()
    three.own().start()
    dupb_ref[...] = jnp.sum(dact[...], axis=0, keepdims=True)
    dsecond = two.result()
    own_cot = cot_ref[block_of(p.member), :].astype(F32)
    normed = norm_scr[...]
    dresid = own_cot + norm_backward(dsecond, normed, inverse, gain)
    dres_ref[...] = dresid
    dresall_ref[block_of(p.member), :] = dresid.astype(BF)
    again = Gather(p, dresall_ref, rows, dsend, drecv)
    again.start()
    three.pass_on()
    for i, term in enumerate((dresid, dsecond * normed, dsecond, own_cot)):
        sums_ref[pl.ds(i, 1), :] = jnp.sum(term, axis=0, keepdims=True)
    chunk = 128
    width = cot_ref.shape[1]

    def grad_chunk(left, right, target):
        def body(i, carry):
            at = pl.ds(pl.multiple_of(i * chunk, chunk), chunk)
            target[at, :] = dot_over(left[:, at], right[...], 0, 0).astype(BF)
            return carry

        lax.fori_loop(0, width // chunk, body, 0)

    grad_chunk(cot_ref, hidden, dwdn_ref)
    again.wait_near()
    again.forward(0)
    again.forward(1)

    def mixed_grad(pair):
        at = pair_of(pair)
        dmixed = dot_over(wo_ref[...], dresall_ref[at, :], 1, 1).astype(BF)
        dmix_ref[:, at] = dmixed
        product = dmixed.astype(F32) * mixed_ref[:, at].astype(F32)
        stats_ref[pl.ds(0, GROUP), at] = lse_ref[:, at]
        for h in range(GROUP):
            stats_ref[pl.ds(GROUP + h, 1), at] = jnp.sum(
                product[h * HP : (h + 1) * HP], axis=0, keepdims=True
            )

    mixed_grad(p.pair)
    again.wait_rest()
    mixed_grad(other)
    grad_chunk(second, dbefore, dwup_ref)
    out_ref[...] = (res_scr[...] + three.result() + down_bias).astype(BF)
    gather.drain()
    again.drain()


def back_kernel(
    capacity, reps, rows, meta_ref, win_ref, dmix_ref, stats_ref, first_ref, w_ref, tok_ref,
    dres_ref, gain_ref,
    grad_ref, dwin_ref, dbias_ref, sums_ref,
    dwin, swin, dq, dk, dv, sbuf, dproj, part, held, stage,
    ksend, krecv, tsend, trecv, ssend, srecv, rsend, rrecv,
):
    p = Place(capacity, reps)
    barrier, count = p.wide_barrier()
    own_image = own_image_row(meta_ref, p, rows)
    own_image = jnp.where(own_image < 0, -1, own_image)
    width = GROUP * rows
    for b in range(GROUP):
        at = slice(b * rows, (b + 1) * rows)
        dwin[0, OWN + b] = dmix_ref[:, at]
        swin[0, OWN + b] = stats_ref[:, at]
    pl.semaphore_wait(barrier, count)
    only = pl.ds(0, 1)
    for_sent(p, lambda o, i: exchange_copy(p, dwin, only, o, i, ksend, krecv).start())
    for_sent(p, lambda o, i: exchange_copy(p, swin, only, o, i, tsend, trecv).start())

    def joined(ref, kind, head):
        return jnp.concatenate([ref[kind, OWN + b, head, :] for b in range(GROUP)], axis=1)

    def head_rows(h):
        return pl.ds(pl.multiple_of(h * HP, HP), HP)

    def query_grads(h, carry):
        head = head_rows(h)
        query = joined(win_ref, 0, head)
        dmixed = dmix_ref[head, :]
        lse = stats_ref[pl.ds(h, 1), :] * LOG2E
        delta = stats_ref[pl.ds(GROUP + h, 1), :]
        dq[head, :] = jnp.zeros((HP, width), F32)

        def body(slot, carry):
            @pl.when(p.shares(p.rep * GROUP + slot - OWN, p.rep))
            def _():
                key = win_ref[1, slot, head, :]
                raw = dot_over(key, query, 0, 0)
                allowed = window_image_col(meta_ref, p, slot, rows) == own_image
                probs = jnp.where(allowed, jnp.exp2(raw * (SCALE * LOG2E) - lse), 0.0)
                dprob = dot_over(win_ref[2, slot, head, :], dmixed, 0, 0)
                dscore = (probs * (dprob - delta) * SCALE).astype(BF)
                dq[head, :] += dot_over(key, dscore, 1, 0)

            return carry

        lax.fori_loop(0, WINDOW, body, 0)
        return carry

    lax.fori_loop(0, GROUP, query_grads, 0)

    def owner_of(kind):
        c = kind * GROUP + p.member
        return lax.div(c, 3), lax.rem(c, 3)

    def home(kind):
        owner, index = owner_of(kind)
        return owner, remote(
            sbuf.at[kind], dproj.at[index], ssend.at[kind], srecv.at[index], (p.rep, owner)
        )

    def send_home(kind, grads):
        sbuf[kind] = grads[...].astype(BF)
        dbias_ref[kind] = jnp.sum(grads[...], axis=1, keepdims=True)
        owner, copy = home(kind)

        @pl.when(owner != p.member)
        def _():
            copy.start()

    send_home(0, dq)
    for_received(p, lambda o, i: window_wait(p, dwin, only, o, i, ksend, krecv))
    for_received(p, lambda o, i: window_wait(p, swin, only, o, i, tsend, trecv))

    def key_grads(h, carry):
        head = head_rows(h)
        key = joined(win_ref, 1, head)
        value = joined(win_ref, 2, head)
        dk[head, :] = jnp.zeros((HP, width), F32)
        dv[head, :] = jnp.zeros((HP, width), F32)

        def body(slot, carry):
            @pl.when(p.shares(p.rep * GROUP + slot - OWN, p.rep))
            def _():
                query = win_ref[0, slot, head, :]
                dmixed = dwin[0, slot, head, :]
                stats = jnp.transpose(
                    jnp.concatenate(
                        [swin[0, slot, pl.ds(h, 1), :], swin[0, slot, pl.ds(GROUP + h, 1), :],
                         jnp.zeros((6, rows), F32)], axis=0
                    )
                )
                lse, delta = stats[:, 0:1] * LOG2E, stats[:, 1:2]
                raw = dot_over(query, key, 0, 0)
                allowed = window_image_col(meta_ref, p, slot, rows) == own_image
                probs = jnp.where(allowed, jnp.exp2(raw * (SCALE * LOG2E) - lse), 0.0)
                dprob = dot_over(dmixed, value, 0, 0)
                dscore = (probs * (dprob - delta) * SCALE).astype(BF)
                dk[head, :] += dot_over(query, dscore, 1, 0)
                dv[head, :] += dot_over(dmixed, probs.astype(BF), 1, 0)

            return carry

        lax.fori_loop(0, WINDOW, body, 0)
        return carry

    lax.fori_loop(0, GROUP, key_grads, 0)
    send_home(1, dk)
    send_home(2, dv)
    for kind in range(3):
        owner, index = owner_of(kind)

        @pl.when(owner == p.member)
        def _():
            dproj[pl.ds(index, 1)] = sbuf[kind : kind + 1]

    for index in range(3):
        source = lax.rem(3 * p.member + index, GROUP)

        @pl.when(source != p.member)
        def _():
            remote(
                sbuf.at[0], dproj.at[index], ssend.at[0], srecv.at[index], (p.rep, p.near)
            ).wait_recv()

    block_of = lambda owner: pl.ds(pl.multiple_of(owner * rows, rows), rows)

    def partial(owner):
        total = dot_over(dproj[0, :, block_of(owner)], w_ref[0], 0, 0)
        for i in (1, 2):
            total = total + dot_over(dproj[i, :, block_of(owner)], w_ref[i], 0, 0)
        part[block_of(owner), :] = total.astype(BF)

    scatter = Scatter(p, part, held, stage, rows, rsend, rrecv)
    partial(p.diagonal)
    scatter.ahead().start()
    partial(p.near)
    scatter.own().start()
    partial(p.far)
    scatter.pass_on()
    partial(p.member)
    chunk = 128
    high = w_ref.shape[1]

    def grad_chunk(i, carry):
        at = pl.ds(pl.multiple_of(i * chunk, chunk), chunk)
        for k in range(3):
            dwin_ref[k, :, at] = dot_over(dproj[k], first_ref[:, at], 1, 0).astype(BF)
        return carry

    lax.fori_loop(0, first_ref.shape[1] // chunk, grad_chunk, 0)
    normed, inverse = norm_parts(tok_ref[...].astype(F32))
    dfirst = scatter.result()
    grad_ref[...] = dres_ref[...] + norm_backward(dfirst, normed, inverse, gain_ref[...])
    for i, term in enumerate((dfirst * normed, dfirst)):
        sums_ref[pl.ds(i, 1), :] = jnp.sum(term, axis=0, keepdims=True)
    for kind in range(3):
        owner, copy = home(kind)

        @pl.when(owner != p.member)
        def _():
            copy.wait_send()

    for_sent(p, lambda o, i: exchange_copy(p, dwin, only, o, i, ksend, krecv).wait_send())
    for_sent(p, lambda o, i: exchange_copy(p, swin, only, o, i, tsend, trecv).wait_send())


def flipped(index, bit):
    return index + bit * (1 - 2 * ((index // bit) % 2))


def doublings(count):
    return [1 << i for i in range(count.bit_length() - 1)]


def total_kernel(reps, x_ref, o_ref, held, send, recv):
    rep, member = lax.axis_index("rep"), lax.axis_index("grp")
    places = [(rep, flipped(member, bit)) for bit in doublings(GROUP)]
    places += [(flipped(rep, bit), member) for bit in doublings(reps)]
    barrier = pltpu.get_barrier_semaphore()
    for place in places:
        pl.semaphore_signal(barrier, inc=1, device_id=place, device_id_type=MESH)
    pl.semaphore_wait(barrier, len(places))
    o_ref[...] = x_ref[...]
    for slot, place in enumerate(places):
        copy = remote(o_ref, held.at[slot], send.at[slot], recv.at[slot], place)
        copy.start()
        copy.wait()
        o_ref[...] += held[slot]


def dma(count):
    return [pltpu.SemaphoreType.DMA((count,))] * 2


def call(kernel, number, args, outs, scratch, smem=0, limit=56):
    vmem = pl.BlockSpec(memory_space=pltpu.VMEM)
    smem_spec = pl.BlockSpec(memory_space=pltpu.SMEM)
    linked = {} if number is None else {"collective_id": number, "has_side_effects": True}
    return pl.pallas_call(
        kernel,
        out_shape=[jax.ShapeDtypeStruct(*o) for o in outs],
        in_specs=[smem_spec] * smem + [vmem] * (len(args) - smem),
        out_specs=[vmem] * len(outs),
        scratch_shapes=scratch,
        compiler_params=pltpu.CompilerParams(vmem_limit_bytes=limit * 2**20, **linked),
    )(*args)


def per_device(
    tokens,
    cotangent,
    slice_sizes,
    gain_one,
    shift_one,
    attn_in,
    attn_bias,
    attn_out,
    out_bias,
    gain_two,
    shift_two,
    mlp_up,
    up_bias,
    mlp_down,
    down_bias,
):
    capacity, width = tokens.shape
    reps, groups = lax.axis_size("rep"), lax.axis_size("grp")
    assert groups == GROUP
    rows = -(-capacity // 128) * 128
    all_rows = GROUP * rows
    rep, member = lax.axis_index("rep"), lax.axis_index("grp")
    device = rep * groups + member
    ff_rows = mlp_up.shape[0]
    heads_high = GROUP * HP
    devices = reps * groups
    vm = pltpu.VMEM

    order = jnp.arange(devices)
    starts = jnp.sum(jnp.where(order[None, :] < order[:, None], slice_sizes[None, :], 0), axis=1)
    base = starts // IMG
    meta = jnp.stack([base, (base + 1) * IMG - starts, slice_sizes]).astype(jnp.int32)
    own_count = slice_sizes[device]
    live_col = (jnp.arange(capacity, dtype=jnp.int32) < own_count)[:, None]

    def padded(x):
        return jnp.pad(jnp.where(live_col, x, jnp.zeros_like(x)), ((0, rows - capacity), (0, 0)))

    tok, cot = padded(tokens), padded(cotangent)
    w_in = jnp.pad(
        attn_in.reshape(3, GROUP, HD, width), ((0, 0), (0, 0), (0, HP - HD), (0, 0))
    ).reshape(3, heads_high, width)
    bias_full = jnp.concatenate([attn_bias[0], jnp.zeros((width,), F32), attn_bias[1]])
    own_bias = lax.dynamic_slice_in_dim(bias_full, member * 3 * GROUP * HD, 3 * GROUP * HD, 0)
    own_bias = jnp.pad(
        own_bias.reshape(3, GROUP, HD), ((0, 0), (0, 0), (0, HP - HD))
    ).reshape(3, heads_high, 1)
    w_out = jnp.pad(
        attn_out.reshape(GROUP, HD, width), ((0, 0), (0, HP - HD), (0, 0))
    ).reshape(heads_high, width)
    own_up_bias = lax.dynamic_slice_in_dim(up_bias, member * ff_rows, ff_rows, 0)[None, :]
    vectors = jnp.stack([out_bias, gain_two, shift_two, down_bias])
    place = (capacity, reps, rows)

    first, window, cot_all = call(
        functools.partial(front_kernel, *place), 1,
        (tok, cot, gain_one[None, :], shift_one[None, :], w_in, own_bias),
        [((all_rows, width), BF), ((3, WINDOW, heads_high, rows), BF), ((all_rows, width), BF)],
        [vm((all_rows, width), BF), vm((3, GROUP, heads_high, rows), BF),
         *dma(5), *dma(5), *dma(4),
         pltpu.SemaphoreType.DMA((len(OFFSETS) * GROUP,)), pltpu.SemaphoreType.DMA((WINDOW,))],
    )
    mixed, lse = call(
        functools.partial(attend_kernel, *place), None, (meta, window),
        [((heads_high, all_rows), BF), ((GROUP, all_rows), F32)],
        [vm((WINDOW, rows, all_rows), F32), vm((8, all_rows), F32), vm((8, all_rows), F32),
         vm((HP, all_rows), F32)],
        smem=1,
    )
    out, dresid, dmixed, stats, dresid_all, dw_up, dw_down, sums_two, dup = call(
        functools.partial(middle_kernel, *place), 2,
        (tok, cot_all, mixed, lse, w_out, mlp_up, mlp_down, own_up_bias, vectors),
        [((rows, width), BF), ((rows, width), F32), ((heads_high, all_rows), BF),
         ((2 * GROUP, all_rows), F32), ((all_rows, width), BF), ((width, ff_rows), BF),
         ((width, ff_rows), BF), ((4, width), F32), ((1, ff_rows), F32)],
        [vm((all_rows, width), BF)] * 4
        + [vm((all_rows, ff_rows), BF)] * 2
        + [vm((all_rows, ff_rows), F32), vm((rows, width), F32), vm((rows, width), F32),
           vm((3, 3, rows, width), BF), vm((3, rows, width), BF)]
        + dma(3) + dma(5) + dma(3) + dma(5) + dma(3),
    )
    input_grad, dw_in, dbias, sums_one = call(
        functools.partial(back_kernel, *place), 3,
        (meta, window, dmixed, stats, first, w_in, tok, dresid, gain_one[None, :]),
        [((rows, width), F32), ((3, heads_high, width), BF), ((3, heads_high, 1), F32),
         ((2, width), F32)],
        [vm((1, WINDOW, heads_high, rows), BF), vm((1, WINDOW, 2 * GROUP, rows), F32)]
        + [vm((heads_high, all_rows), F32)] * 3
        + [vm((3, heads_high, all_rows), BF)] * 2
        + [vm((all_rows, width), BF), vm((3, rows, width), BF), vm((rows, width), BF)]
        + [pltpu.SemaphoreType.DMA((len(OFFSETS) * GROUP,)), pltpu.SemaphoreType.DMA((WINDOW,))] * 2
        + dma(3) + dma(3),
        smem=1,
    )

    def rep_summed(partial, bits):
        sizes = doublings(reps)[::-1]
        current = partial.reshape((2,) * len(sizes) + (width // reps, partial.shape[1]))
        left = list(sizes)
        for bit in bits:
            axis = left.index(bit)
            left.remove(bit)
            mine = (rep // bit) % 2
            keep = lax.dynamic_index_in_dim(current, mine, axis, keepdims=False)
            give = lax.dynamic_index_in_dim(current, 1 - mine, axis, keepdims=False)
            got = lax.ppermute(give, "rep", [(r, r ^ bit) for r in range(reps)])
            current = keep.astype(F32) + got.astype(F32)
            if left:
                current = current.astype(BF)
        return current

    bits = doublings(reps)
    dmlp_down = rep_summed(dw_down, bits).T
    dmlp_up = rep_summed(dw_up, bits[1:] + bits[:1]).T
    dw_out = dot_over(dresid_all, mixed, 0, 1).astype(BF)
    dattn_out = rep_summed(dw_out, bits).T.reshape(GROUP, HP, -1)[:, :HD].reshape(GROUP * HD, -1)
    dw_in = dw_in.reshape(3, GROUP, HP, width)[:, :, :HD].reshape(3 * GROUP * HD, width)
    dattn_in = lax.psum_scatter(dw_in, "rep", scatter_dimension=1, tiled=True).astype(F32)

    def totals(parts):
        flat = jnp.concatenate([part.reshape(-1) for part in parts])
        lines = -(-flat.shape[0] // 1024) * 8
        flat = jnp.pad(flat, (0, lines * 128 - flat.shape[0])).reshape(lines, 128)
        steps = len(doublings(reps)) + len(doublings(groups))
        [summed] = call(
            functools.partial(total_kernel, reps), 0, (flat,), [(flat.shape, F32)],
            [vm((steps, lines, 128), F32), *dma(steps)], limit=16,
        )
        summed = summed.reshape(-1)
        spot, outs = 0, []
        for part in parts:
            outs.append(summed[spot : spot + part.size].reshape(part.shape))
            spot += part.size
        return outs

    dbias = dbias.reshape(3, GROUP, HP)[:, :, :HD].reshape(3, GROUP * HD)
    dattn_bias = lax.dynamic_update_slice_in_dim(
        jnp.zeros((2, width), F32), dbias[0::2], member * GROUP * HD, 1
    )
    dup_bias = lax.dynamic_update_slice_in_dim(
        jnp.zeros(up_bias.shape, F32), dup[0], member * ff_rows, 0
    )
    dgain_one, dshift_one, dattn_bias, dout_bias, dgain_two, dshift_two, dup_bias, ddown_bias = (
        totals(
            (
                sums_one[0], sums_one[1], dattn_bias, sums_two[0], sums_two[1], sums_two[2],
                dup_bias, sums_two[3],
            )
        )
    )
    block_output = jnp.where(live_col, out[:capacity], jnp.zeros((), BF))
    input_grad = jnp.where(live_col, input_grad[:capacity], 0.0)
    return (
        block_output, input_grad, dgain_one, dshift_one, dattn_in, dattn_bias, dattn_out,
        dout_bias, dgain_two, dshift_two, dmlp_up, dup_bias, dmlp_down, ddown_bias,
    )


def solution(mesh):
    rows, rep_grp = P("grp", None), P(("rep", "grp"), None)
    in_specs = (
        rep_grp, rep_grp, P(), P(), P(), rows, P(), rows, P(), P(), P(), rows, P(), rows, P(),
    )
    grads = P("grp", "rep")
    out_specs = (
        rep_grp, rep_grp, P(), P(), grads, P(), grads, P(), P(), P(), grads, P(), grads, P(),
    )
    return jax.shard_map(
        per_device, mesh=mesh, in_specs=in_specs, out_specs=out_specs, check_vma=False
    )
```

```python
import functools

import jax
import jax.numpy as jnp
from jax import lax
from jax.experimental import pallas as pl
from jax.experimental.pallas import tpu as pltpu
from jax.sharding import PartitionSpec as P

H = 16
HD = 72
HP = 80
IMG = 729
GROUP = 4
NEAR_GROUPS = 2
WINDOW = (2 * NEAR_GROUPS + 1) * GROUP
OWN = NEAR_GROUPS * GROUP
OFFSETS = (1, -1, 2, -2)

EPSILON = 1e-06
SQRT_TWO_PI = 0.7978845608028654
CUBIC = 0.044715
FAR = -(2.0**80)
SCALE = HD ** (-0.5)
LOG2E = 1.4426950408889634
BF = jnp.bfloat16
F32 = jnp.float32
MESH = pl.DeviceIdType.MESH


def norm_parts(rows):
    centered = rows - jnp.mean(rows, axis=-1, keepdims=True)
    inverse = lax.rsqrt(jnp.mean(centered * centered, axis=-1, keepdims=True) + EPSILON)
    return centered * inverse, inverse


def norm_backward(dscaled, normed, inverse, gain_row):
    dnormed = dscaled * gain_row
    return inverse * (
        dnormed
        - jnp.mean(dnormed, axis=-1, keepdims=True)
        - normed * jnp.mean(dnormed * normed, axis=-1, keepdims=True)
    )


def gelu_parts(before):
    square = before * before
    tangent = jnp.tanh(SQRT_TWO_PI * before * (1.0 + CUBIC * square))
    half = 0.5 * (1.0 + tangent)
    derivative = half + 0.5 * before * (1.0 - tangent * tangent) * (
        SQRT_TWO_PI + SQRT_TWO_PI * 3.0 * CUBIC * square
    )
    return before * half, derivative


def dot_over(left, right, left_axis, right_axis):
    return lax.dot_general(
        left, right, (((left_axis,), (right_axis,)), ((), ())), preferred_element_type=F32
    )


def flipped(index, bit):
    return index + bit * (1 - 2 * ((index // bit) % 2))


def doublings(count):
    return [1 << i for i in range(count.bit_length() - 1)]


class Place:
    def __init__(self, capacity, reps, rows):
        self.capacity, self.reps, self.rows = capacity, reps, rows
        self.devices = reps * GROUP
        self.images = capacity * self.devices // IMG
        self.short = capacity * self.devices - self.images * IMG
        self.rep, self.member = lax.axis_index("rep"), lax.axis_index("grp")
        low = lax.rem(self.member, 2)
        self.near = self.member + 1 - 2 * low
        self.far = lax.rem(self.member + 2, GROUP)
        self.diagonal = lax.rem(self.near + 2, GROUP)
        self.pair = lax.div(self.member, 2)

    def sharing(self, low, high):
        capacity, short, image = self.capacity, self.short, jnp.int32(IMG)
        start = low * capacity - jnp.minimum(low, short)
        end = high * capacity - jnp.maximum(high - (self.devices - short), 0) - 1
        first = lax.div(start, image) * IMG
        after = (jnp.minimum(lax.div(end, image), self.images - 1) + 1) * IMG
        begin = lax.div(first, jnp.int32(capacity))
        stop = jnp.minimum(
            lax.div(after + short + capacity - 1, jnp.int32(capacity)),
            lax.div(after + capacity - 2, jnp.int32(capacity - 1)),
        )
        return begin, jnp.minimum(stop, self.devices)

    def slots(self, low, high):
        base = self.rep * GROUP
        begin, stop = self.sharing(base + low, base + high)
        return jnp.maximum(begin - base + OWN, 0), jnp.minimum(stop - base + OWN, WINDOW)

    def shares(self, block, group):
        begin, stop = self.sharing(group * GROUP, group * GROUP + GROUP)
        return (group >= 0) & (group < self.reps) & (block >= begin) & (block < stop)

    def block(self, owner):
        return pl.ds(pl.multiple_of(owner * self.rows, self.rows), self.rows)

    def pair_block(self, pair):
        return pl.ds(pl.multiple_of(pair * 2 * self.rows, 2 * self.rows), 2 * self.rows)

    def halving_barrier(self):
        barrier = pltpu.get_barrier_semaphore()
        bits = doublings(self.reps)
        for bit in bits:
            pl.semaphore_signal(
                barrier, inc=1, device_id=(flipped(self.rep, bit), self.member),
                device_id_type=MESH,
            )
        return len(bits)

    def group_barrier(self):
        barrier = pltpu.get_barrier_semaphore()
        for other in (self.near, self.far):
            pl.semaphore_signal(
                barrier, inc=1, device_id=(self.rep, other), device_id_type=MESH
            )
        return barrier, 2

    def wide_barrier(self):
        barrier, count = self.group_barrier()
        count = jnp.int32(count)
        for offset in OFFSETS:
            there = self.rep + offset
            valid = (there >= 0) & (there < self.reps)

            @pl.when(valid)
            def _():
                pl.semaphore_signal(
                    barrier, inc=1, device_id=(there, self.member), device_id_type=MESH
                )

            count = count + jnp.where(valid, 1, 0)
        return barrier, count


def remote(source, target, send, recv, place):
    return pltpu.make_async_remote_copy(
        src_ref=source,
        dst_ref=target,
        send_sem=send,
        recv_sem=recv,
        device_id=place,
        device_id_type=MESH,
    )


class Gather:
    def __init__(self, place, ref, rows, send, recv):
        self.place, self.ref, self.rows, self.send, self.recv = place, ref, rows, send, recv
        self.half = rows // 2

    def copy(self, owner, part, slot, target):
        if part is None:
            piece = self.ref.at[pl.ds(pl.multiple_of(owner * self.rows, self.rows), self.rows), :]
        else:
            start = pl.multiple_of(owner * self.rows + part * self.half, self.half)
            piece = self.ref.at[pl.ds(start, self.half), :]
        return remote(
            piece, piece, self.send.at[slot], self.recv.at[slot], (self.place.rep, target)
        )

    def start(self):
        p = self.place
        for part in range(2):
            self.copy(p.member, part, 1 + part, p.far).start()
        self.copy(p.member, None, 0, p.near).start()

    def wait_near(self):
        p = self.place
        self.copy(p.near, None, 0, p.near).wait_recv()

    def forward(self, part):
        p = self.place
        self.copy(p.far, part, 1 + part, p.far).wait_recv()
        self.copy(p.far, part, 3 + part, p.near).start()

    def wait_rest(self):
        p = self.place
        for part in range(2):
            self.copy(p.diagonal, part, 3 + part, p.near).wait_recv()

    def drain(self):
        p = self.place
        self.copy(p.member, None, 0, p.near).wait_send()
        for part in range(2):
            self.copy(p.member, part, 1 + part, p.far).wait_send()
            self.copy(p.far, part, 3 + part, p.near).wait_send()


class Scatter:
    def __init__(self, place, ref, held, rows, send, recv):
        self.place, self.ref, self.held = place, ref, held
        self.rows, self.send, self.recv = rows, send, recv

    def block(self, owner):
        return pl.ds(pl.multiple_of(owner * self.rows, self.rows), self.rows)

    def ahead(self):
        p = self.place
        return remote(
            self.ref.at[self.block(p.diagonal), :], self.held.at[0],
            self.send.at[0], self.recv.at[0], (p.rep, p.near),
        )

    def own(self):
        p = self.place
        return remote(
            self.ref.at[self.block(p.near), :], self.held.at[1],
            self.send.at[1], self.recv.at[1], (p.rep, p.near),
        )

    def across(self):
        p = self.place
        return remote(
            self.held.at[0], self.held.at[2], self.send.at[2], self.recv.at[2], (p.rep, p.far)
        )

    def pass_on(self):
        p = self.place
        self.ahead().wait_recv()
        self.held[0] = (
            self.ref[self.block(p.far), :].astype(F32) + self.held[0].astype(F32)
        ).astype(BF)
        self.across().start()

    def result(self):
        p = self.place
        self.own().wait_recv()
        total = self.ref[self.block(p.member), :].astype(F32) + self.held[1].astype(F32)
        self.across().wait_recv()
        total = total + self.held[2].astype(F32)
        self.ahead().wait_send()
        self.own().wait_send()
        self.across().wait_send()
        return total


class Exchange:
    def __init__(self, place, view, send, recv):
        self.place, self.view, self.send, self.recv = place, view, send, recv

    def outgoing(self, act):
        p = self.place
        for number, offset in enumerate(OFFSETS):
            begin, stop = p.sharing((p.rep + offset) * GROUP, (p.rep + offset + 1) * GROUP)
            valid = (p.rep + offset >= 0) & (p.rep + offset < p.reps)
            for index in range(GROUP):
                block = p.rep * GROUP + index
                slot_there = OWN - offset * GROUP + index

                @pl.when(valid & (block >= begin) & (block < stop))
                def _():
                    act(
                        remote(
                            self.view(OWN + index),
                            self.view(slot_there),
                            self.send.at[number * GROUP + index],
                            self.recv.at[slot_there],
                            (p.rep + offset, p.member),
                        )
                    )

    def start(self):
        self.outgoing(lambda copy: copy.start())

    def drain(self):
        self.outgoing(lambda copy: copy.wait_send())

    def wait(self):
        p = self.place
        begin, stop = p.slots(0, GROUP)
        for offset in OFFSETS:
            for index in range(GROUP):
                slot = OWN + offset * GROUP + index

                @pl.when((slot >= begin) & (slot < stop))
                def _():
                    remote(
                        self.view(slot), self.view(slot), self.send.at[0], self.recv.at[slot],
                        (p.rep, p.near),
                    ).wait_recv()


def dma(count):
    return [pltpu.SemaphoreType.DMA((count,))] * 2


class Halving:
    def __init__(self, place, levels, deep, send, recv):
        self.place, self.levels, self.deep = place, levels, deep
        self.send, self.recv = send, recv
        self.bits = doublings(place.reps)

    def mine(self, step):
        return lax.rem(lax.div(self.place.rep, jnp.int32(self.bits[step])), 2)

    def partner(self, step):
        p = self.place
        return (flipped(p.rep, self.bits[step]), p.member)

    def rows(self, start, count):
        return pl.ds(pl.multiple_of(start * self.deep, self.deep), count * self.deep)

    def firsts(self):
        rest = self.bits[1:]
        for j in range(self.place.reps // 2):
            yield j, sum(bit * ((j >> (len(rest) - 1 - q)) & 1) for q, bit in enumerate(rest))

    def copies(self, step):
        give = 1 - self.mine(step)
        source, target = self.levels[step], self.levels[step + 1]
        if step == 0:
            return [
                remote(
                    source.at[self.rows(give * self.bits[0] + offset, 1), :],
                    target.at[self.rows(j, 1), :],
                    self.send.at[j], self.recv.at[j], self.partner(0),
                )
                for j, offset in self.firsts()
            ]
        half = self.place.reps >> (step + 1)
        slot = self.place.reps // 2 + step - 1
        return [
            remote(
                source.at[self.rows(give * half, half), :], target.at[self.rows(0, half), :],
                self.send.at[slot], self.recv.at[slot], self.partner(step),
            )
        ]

    def start(self, step):
        for copy in self.copies(step):
            copy.start()

    def finish(self, step, out=None):
        copies = self.copies(step)
        mine = self.mine(step)
        source, target = self.levels[step], self.levels[step + 1]
        half = self.place.reps >> (step + 1)
        if step == 0:
            for j, offset in self.firsts():
                copies[j].wait_recv()
                at = self.rows(j, 1)
                kept = source[self.rows(mine * self.bits[0] + offset, 1), :]
                target[at, :] = (target[at, :].astype(F32) + kept.astype(F32)).astype(BF)
            return
        copies[0].wait_recv()
        for j in range(half):
            at = self.rows(j, 1)
            kept = source[self.rows(mine * half + j, 1), :]
            total = target[at, :].astype(F32) + kept.astype(F32)
            if out is None:
                target[at, :] = total.astype(BF)
            else:
                out[...] = total

    def drain(self, step):
        for copy in self.copies(step):
            copy.wait_send()


def halving_sems(reps):
    return dma(reps // 2 + reps.bit_length() - 2)


def halving_levels(reps, deep, wide, first):
    return [
        pltpu.VMEM(((reps >> s) * deep, wide), BF) for s in range(first, reps.bit_length())
    ]


def grad_chunks(left, right, right_axis, target, deep, narrow):
    chunk = 128
    width = left.shape[1]

    def body(i, carry):
        at = pl.ds(pl.multiple_of(i * chunk, chunk), chunk)
        if deep == narrow:
            columns = left[:, at]
        else:
            source = lax.broadcasted_iota(jnp.int32, (width, chunk), 0)
            column = lax.broadcasted_iota(jnp.int32, (width, chunk), 1) + i * chunk
            within = column % deep
            picked = (source == (column // deep) * narrow + within) & (within < narrow)
            columns = dot_over(left[...], jnp.where(picked, 1.0, 0.0).astype(BF), 1, 0).astype(BF)
        target[at, :] = dot_over(columns, right[...], 0, right_axis).astype(BF)
        return carry

    lax.fori_loop(0, target.shape[0] // chunk, body, 0)


def image_codes(place, sizes_ref, kind):
    start = lax.fori_loop(0, place.rep * GROUP, lambda i, n: n + sizes_ref[i], jnp.int32(0))
    index = lax.broadcasted_iota(jnp.int32, (8, place.rows), 1)
    row = lax.broadcasted_iota(jnp.int32, (8, place.rows), 0)
    codes = []
    for b in range(GROUP):
        size = sizes_ref[place.rep * GROUP + b]
        base = lax.div(start, jnp.int32(IMG))
        turn = (base + 1) * IMG - start
        kind_of_image = lax.rem(base + jnp.where(index >= turn, 1, 0), 4)
        live = index < size
        same = kind_of_image == row
        query = jnp.where(same | ~live, 1.0, 0.0)
        key = jnp.where(same & live, 0.0, FAR)
        code = jnp.where(kind == 0, query, key)
        code = jnp.where(row < 4, code, 0.0)
        codes.append(jnp.where(kind == 2, jnp.where(row == 0, 1.0, 0.0), code))
        start = start + size
    return codes


def front_kernel(
    capacity, reps, rows, sizes_ref, tok_ref, cot_ref, vec_ref, w_ref, bias_ref,
    first_ref, own_ref, query_ref, win_ref, cotall_ref,
    xall, sbuf, code, gsend, grecv, csend, crecv, ssend, srecv, ksend, krecv, vsend, vrecv,
):
    p = Place(capacity, reps, rows)
    barrier, count = p.wide_barrier()
    size = sizes_ref[p.rep * GROUP + p.member]
    live = lax.broadcasted_iota(jnp.int32, (capacity, 1), 0) < size
    clean = lambda ref: jnp.where(live, ref[...].astype(F32), 0.0).astype(BF)
    own_ref[...] = jnp.zeros_like(own_ref)
    own_ref[pl.ds(0, capacity), :] = clean(tok_ref)
    xall[p.block(p.member), :] = own_ref[...]
    pl.semaphore_wait(barrier, count)
    tokens = Gather(p, xall, rows, gsend, grecv)
    tokens.start()
    cotall_ref[p.block(p.member), :] = jnp.zeros((rows, tok_ref.shape[1]), BF)
    cotall_ref[pl.ds(pl.multiple_of(p.member * rows, rows), capacity), :] = clean(cot_ref)
    gain, shift = vec_ref[pl.ds(0, 1), :], vec_ref[pl.ds(1, 1), :]

    def normalize(owner):
        block = p.block(owner)
        normed, _ = norm_parts(xall[block, :].astype(F32))
        first_ref[block, :] = (normed * gain + shift).astype(BF)

    odd = lax.rem(p.member, 2)
    cross = 2 - 2 * odd
    kept = 2 * odd
    kind_of = lambda i: lax.div(3 * p.member + i, GROUP)
    def spot_of(i):
        kind = kind_of(i)
        return jnp.where(kind == 0, 2 * WINDOW, (kind - 1) * WINDOW + OWN)

    gap = jnp.zeros((HD, rows), F32)
    for i in range(3):
        for b, rest in enumerate(image_codes(p, sizes_ref, kind_of(i))):
            at = slice(b * rows, (b + 1) * rows)
            for h in range(GROUP):
                code[i, h * HP : (h + 1) * HP, at] = jnp.concatenate([gap, rest], axis=0)

    def project(i, pair):
        block = first_ref[p.pair_block(pair), :]
        bias = bias_ref[pl.ds(3 * p.member + i, 1), :]
        bias = jnp.transpose(jnp.broadcast_to(bias, (8, bias.shape[1])))[:, 0:1]
        total = dot_over(w_ref[i], block, 1, 1) + bias + code[i, :, p.pair_block(pair)]
        for b in range(2):
            sbuf[i, pair * 2 + b] = total[:, b * rows : (b + 1) * rows].astype(BF)

    def shuffle(i, pair, way, target):
        slot = way * 2 + pair
        return remote(
            sbuf.at[i, pl.ds(pair * 2, 2)],
            win_ref.at[pl.ds(spot_of(i) + pair * 2, 2)],
            ssend.at[slot], srecv.at[slot], (p.rep, target),
        )

    normalize(p.member)
    tokens.wait_near()
    normalize(p.near)
    tokens.forward(0)
    project(cross, p.pair)
    shuffle(cross, p.pair, 0, p.far).start()
    tokens.forward(1)
    project(1, p.pair)
    shuffle(1, p.pair, 1, p.near).start()
    project(kept, p.pair)
    other = 1 - p.pair
    normalize(p.far)
    tokens.wait_rest()
    normalize(p.diagonal)
    project(cross, other)
    shuffle(cross, other, 0, p.far).start()
    project(1, other)
    shuffle(1, other, 1, p.near).start()
    project(kept, other)
    win_ref[pl.ds(spot_of(kept), GROUP)] = sbuf[kept]
    for pair in (p.pair, other):
        shuffle(cross, pair, 0, p.far).wait_recv()
        shuffle(1, pair, 1, p.near).wait_recv()
    keys = Exchange(p, lambda slot: win_ref.at[slot], ksend, krecv)
    values = Exchange(p, lambda slot: win_ref.at[WINDOW + slot], vsend, vrecv)
    keys.start()
    values.start()
    cotangents = Gather(p, cotall_ref, rows, csend, crecv)
    cotangents.start()
    query_ref[...] = win_ref[pl.ds(2 * WINDOW, GROUP)]
    cotangents.wait_near()
    cotangents.forward(0)
    cotangents.forward(1)
    cotangents.wait_rest()
    keys.wait()
    values.wait()
    keys.drain()
    values.drain()
    for pair in (p.pair, other):
        shuffle(cross, pair, 0, p.far).wait_send()
        shuffle(1, pair, 1, p.near).wait_send()
    tokens.drain()
    cotangents.drain()


def joined(view, head, pair):
    return jnp.concatenate([view(2 * pair + b)[head, :] for b in range(2)], axis=1)


def attend_kernel(
    capacity, reps, rows, sizes_ref, query_ref, win_ref, mixed_ref, lse_ref, best, acc
):
    p = Place(capacity, reps, rows)
    width = 2 * rows
    heads = [slice(h * HP, (h + 1) * HP) for h in range(GROUP)]
    for pair in range(2):
        begin, stop = p.slots(2 * pair, 2 * pair + 2)
        at = slice(pair * width, (pair + 1) * width)
        best[...] = jnp.full_like(best, 4.0 * FAR)
        acc[...] = jnp.zeros_like(acc)
        queries = [
            jnp.concatenate([query_ref[2 * pair + b, head, :] for b in range(2)], axis=1)
            for head in heads
        ]

        def scores(slot, carry):
            for h, head in enumerate(heads):
                raw = dot_over(win_ref[slot, head, :], queries[h], 0, 0)
                best[h] = jnp.maximum(best[h], jnp.max(raw.reshape(rows // 8, 8, width), axis=0))
            return carry

        lax.fori_loop(begin, stop, scores, 0)
        tops = [
            jnp.max(best[h], axis=0, keepdims=True) * (SCALE * LOG2E) for h in range(GROUP)
        ]

        def weigh(slot, carry):
            for h, head in enumerate(heads):
                raw = dot_over(win_ref[slot, head, :], queries[h], 0, 0)
                powers = jnp.exp2(raw * (SCALE * LOG2E) - tops[h]).astype(BF)
                acc[head, :] += dot_over(win_ref[WINDOW + slot, head, :], powers, 1, 0)
            return carry

        lax.fori_loop(begin, stop, weigh, 0)
        index = lax.broadcasted_iota(jnp.int32, (1, rows), 1)
        live = jnp.concatenate(
            [
                jnp.where(index < sizes_ref[p.rep * GROUP + 2 * pair + b], 1.0, 0.0)
                for b in range(2)
            ],
            axis=1,
        )
        for h, head in enumerate(heads):
            whole = acc[h * HP + HD : h * HP + HD + 1, :]
            mixed_ref[head, at] = (acc[head, :] / whole).astype(BF)
            lse_ref[h : h + 1, at] = jnp.where(
                live > 0.0, tops[h] + jnp.log(whole) * LOG2E, 0.0
            )


def middle_kernel(
    capacity, reps, rows, deep, tok_ref, cot_ref, query_ref, mixed_ref, lse_ref, wo_ref, wup_ref,
    wdn_ref, upb_ref, vec_ref,
    out_ref, dres_ref, dmix_ref, stats_ref, qwin_ref, dwup_ref, down_ref, dwo_ref, sums_ref,
    dupb_ref,
    part, part2, second, hidden, dbefore, dresall, dact, dwdn, res_scr, norm_scr, held,
    asend, arecv, bsend, brecv, csend, crecv, dsend, drecv, esend, erecv, qsend, qrecv,
    hsend, hrecv,
):
    p = Place(capacity, reps, rows)
    barrier, count = p.wide_barrier()
    count = count + p.halving_barrier()
    out_bias, gain, shift, down_bias = (vec_ref[pl.ds(i, 1), :] for i in range(2, 6))
    other = 1 - p.pair
    narrow = cot_ref.shape[1] // reps

    def attn_partial(owner):
        part[p.block(owner), :] = dot_over(
            mixed_ref[:, p.block(owner)], wo_ref[...], 0, 0
        ).astype(BF)

    attn_partial(p.diagonal)
    pl.semaphore_wait(barrier, count)
    one = Scatter(p, part, held.at[0], rows, asend, arecv)
    one.ahead().start()
    attn_partial(p.near)
    one.own().start()
    qwin_ref[pl.ds(OWN, GROUP)] = query_ref[...]
    queries = Exchange(p, lambda slot: qwin_ref.at[slot], qsend, qrecv)
    queries.start()
    attn_partial(p.far)
    one.pass_on()
    attn_partial(p.member)
    for pair in (0, 1):
        at = pl.ds(pair * 2 * rows, 2 * rows)
        dact[at, :] = dot_over(cot_ref[at, :], wdn_ref[...], 1, 1)
    resid = tok_ref[...].astype(F32) + one.result() + out_bias
    res_scr[...] = resid
    normed, inverse = norm_parts(resid)
    norm_scr[...] = normed
    second[p.block(p.member), :] = (normed * gain + shift).astype(BF)
    gather = Gather(p, second, rows, bsend, brecv)
    gather.start()

    def mlp(pair):
        at = p.pair_block(pair)
        before = dot_over(second[at, :], wup_ref[...], 1, 1) + upb_ref[pl.ds(p.member, 1), :]
        activated, derivative = gelu_parts(before)
        hidden[at, :] = activated.astype(BF)
        grad = dact[at, :] * derivative
        dact[at, :] = grad
        dbefore[at, :] = grad.astype(BF)
        part2[at, :] = dot_over(dbefore[at, :], wup_ref[...], 1, 0).astype(BF)

    gather.wait_near()
    gather.forward(0)
    mlp(p.pair)
    gather.forward(1)
    two = Scatter(p, part2, held.at[1], rows, csend, crecv)
    two.own().start()
    gather.wait_rest()
    mlp(other)
    two.ahead().start()
    grad_chunks(cot_ref, hidden, 0, dwdn, deep, narrow)
    halving = Halving(p, [dwdn, down_ref], deep, hsend, hrecv)
    halving.start(0)
    two.pass_on()

    def down(pair):
        at = p.pair_block(pair)
        part[at, :] = dot_over(hidden[at, :], wdn_ref[...], 1, 0).astype(BF)

    down(other)
    down(p.pair)
    three = Scatter(p, part, held.at[2], rows, esend, erecv)
    three.ahead().start()
    three.own().start()
    dsecond = two.result()
    own_cot = cot_ref[p.block(p.member), :].astype(F32)
    normed = norm_scr[...]
    dresid = own_cot + norm_backward(dsecond, normed, inverse, gain)
    dres_ref[...] = dresid
    dresall[p.block(p.member), :] = dresid.astype(BF)
    again = Gather(p, dresall, rows, dsend, drecv)
    again.start()
    three.pass_on()
    dupb_ref[...] = jnp.sum(dact[...], axis=0, keepdims=True)
    for i, term in enumerate((dresid, dsecond * normed, dsecond, own_cot)):
        sums_ref[pl.ds(i, 1), :] = jnp.sum(term, axis=0, keepdims=True)
    again.wait_near()
    again.forward(0)

    def mixed_grad(pair):
        at = p.pair_block(pair)
        dmixed = dot_over(wo_ref[...], dresall[at, :], 1, 1).astype(BF)
        dmix_ref[:, at] = dmixed
        product = dmixed.astype(F32) * mixed_ref[:, at].astype(F32)
        stats_ref[pl.ds(0, GROUP), at] = lse_ref[:, at]
        for h in range(GROUP):
            stats_ref[pl.ds(GROUP + h, 1), at] = jnp.sum(
                product[h * HP : (h + 1) * HP], axis=0, keepdims=True
            )

    grad_chunks(second, dbefore, 0, dwup_ref, deep, narrow)
    mixed_grad(p.pair)
    again.forward(1)
    again.wait_rest()
    mixed_grad(other)
    grad_chunks(dresall, mixed_ref, 1, dwo_ref, deep, narrow)
    out_ref[...] = (res_scr[...] + three.result() + down_bias).astype(BF)
    queries.wait()
    queries.drain()
    halving.finish(0)
    halving.drain(0)
    gather.drain()
    again.drain()


def back_kernel(
    capacity, reps, rows, deep, win_ref, qwin_ref, dmix_ref, stats_ref, first_ref, w_ref, tok_ref,
    dres_ref, vec_ref, dwup_ref, down_ref, dwo_ref,
    grad_ref, dbias_ref, sums_ref, dup_out, ddn_out, dwo_out, dwi_out,
    dwin, swin, dq, dv, sbuf, dproj, part, held, *rest,
):
    steps = reps.bit_length() - 1
    scratch = list(rest)
    take = lambda n: [scratch.pop(0) for _ in range(n)]
    up_levels, dn_levels = [dwup_ref] + take(steps), [None, down_ref] + take(steps - 1)
    wo_levels, wi_levels = [dwo_ref] + take(steps), take(steps + 1)
    (ksend, krecv, tsend, trecv, ssend, srecv, rsend, rrecv) = take(8)
    p = Place(capacity, reps, rows)
    barrier, count = p.wide_barrier()
    count = count + p.halving_barrier()
    width = 2 * rows
    for b in range(GROUP):
        at = slice(b * rows, (b + 1) * rows)
        dwin[OWN + b] = dmix_ref[:, at]
        swin[OWN + b] = stats_ref[:, at]
    pl.semaphore_wait(barrier, count)
    grads_in = Exchange(p, lambda slot: dwin.at[slot], ksend, krecv)
    stats_in = Exchange(p, lambda slot: swin.at[slot], tsend, trecv)
    grads_in.start()
    stats_in.start()
    down = Halving(p, dn_levels, deep, *take(2))
    up = Halving(p, up_levels, deep, *take(2))
    inner = Halving(p, wi_levels, deep, *take(2))
    outer = Halving(p, wo_levels, deep, *take(2))
    down.start(1)
    up.start(0)
    heads = [slice(h * HP, (h + 1) * HP) for h in range(GROUP)]
    for pair in range(2):
        begin, stop = p.slots(2 * pair, 2 * pair + 2)
        at = slice(pair * width, (pair + 1) * width)
        queries = [joined(lambda b: qwin_ref.at[OWN + b], head, pair) for head in heads]
        dq[:, at] = jnp.zeros((GROUP * HP, width), F32)

        def query_grads(slot, carry):
            for h, head in enumerate(heads):
                key = win_ref[slot, head, :]
                raw = dot_over(key, queries[h], 0, 0)
                probs = jnp.exp2(raw * (SCALE * LOG2E) - stats_ref[h : h + 1, at])
                dprob = dot_over(win_ref[WINDOW + slot, head, :], dmix_ref[head, at], 0, 0)
                dscore = (probs * (dprob - stats_ref[GROUP + h : GROUP + h + 1, at])).astype(BF)
                dq[head, at] += dot_over(key, dscore, 1, 0)
            return carry

        lax.fori_loop(begin, stop, query_grads, 0)

    def owner_of(kind):
        c = kind * GROUP + p.member
        return lax.div(c, 3), lax.rem(c, 3)

    high = GROUP * HP

    def part_of(index):
        return pl.ds(pl.multiple_of(index * high, high), high)

    def home(kind):
        owner, index = owner_of(kind)
        return owner, remote(
            sbuf.at[kind], dproj.at[part_of(index), :], ssend.at[kind], srecv.at[index],
            (p.rep, owner),
        )

    def send_home(kind, grads, scale):
        value = grads[...] * scale
        sbuf[kind] = value.astype(BF)
        dbias_ref[:, kind : kind + 1] = jnp.sum(value, axis=1, keepdims=True)
        owner, copy = home(kind)

        @pl.when(owner != p.member)
        def _():
            copy.start()

    send_home(0, dq, SCALE)
    dk = dq
    grads_in.wait()
    stats_in.wait()
    for pair in range(2):
        begin, stop = p.slots(2 * pair, 2 * pair + 2)
        at = slice(pair * width, (pair + 1) * width)
        keys = [joined(lambda b: win_ref.at[OWN + b], head, pair) for head in heads]
        values = [joined(lambda b: win_ref.at[WINDOW + OWN + b], head, pair) for head in heads]
        dk[:, at] = jnp.zeros((high, width), F32)
        dv[:, at] = jnp.zeros((high, width), F32)

        def key_grads(slot, carry):
            stats = jnp.transpose(swin[slot])
            for h, head in enumerate(heads):
                query = qwin_ref[slot, head, :]
                dmixed = dwin[slot, head, :]
                raw = dot_over(query, keys[h], 0, 0)
                probs = jnp.exp2(raw * (SCALE * LOG2E) - stats[:, h : h + 1])
                dprob = dot_over(dmixed, values[h], 0, 0)
                dscore = (probs * (dprob - stats[:, GROUP + h : GROUP + h + 1])).astype(BF)
                dk[head, at] += dot_over(query, dscore, 1, 0)
                dv[head, at] += dot_over(dmixed, probs.astype(BF), 1, 0)
            return carry

        lax.fori_loop(begin, stop, key_grads, 0)
    send_home(1, dk, SCALE)
    send_home(2, dv, 1.0)
    for kind in range(3):
        owner, index = owner_of(kind)

        @pl.when(owner == p.member)
        def _():
            dproj[part_of(index), :] = sbuf[kind]

    down.finish(1)
    down.start(2)
    up.finish(0)
    up.start(1)
    for index in range(3):
        source = lax.rem(3 * p.member + index, GROUP)

        @pl.when(source != p.member)
        def _():
            remote(
                sbuf.at[0], dproj.at[part_of(index), :], ssend.at[0], srecv.at[index],
                (p.rep, p.near),
            ).wait_recv()

    narrow = first_ref.shape[1] // reps
    grad_chunks(first_ref, dproj, 1, wi_levels[0], deep, narrow)
    inner.start(0)
    outer.start(0)

    def partial(owner):
        part[p.block(owner), :] = dot_over(dproj[:, p.block(owner)], w_ref[...], 0, 0).astype(BF)

    scatter = Scatter(p, part, held, rows, rsend, rrecv)
    partial(p.diagonal)
    scatter.ahead().start()
    partial(p.near)
    scatter.own().start()
    partial(p.far)
    scatter.pass_on()
    partial(p.member)
    normed, inverse = norm_parts(tok_ref[...].astype(F32))
    dfirst = scatter.result()
    for i, term in enumerate((dfirst * normed, dfirst)):
        sums_ref[pl.ds(i, 1), :] = jnp.sum(term, axis=0, keepdims=True)
    grad_ref[...] = dres_ref[...] + norm_backward(dfirst, normed, inverse, vec_ref[pl.ds(0, 1), :])
    work = [(down, 1, ddn_out), (up, 0, dup_out), (inner, -1, dwi_out), (outer, -1, dwo_out)]
    for _ in range(steps + 1):
        for number, (one, done, out) in enumerate(work):
            step = done + 1
            if step < steps:
                one.finish(step, out if step == steps - 1 else None)
                if step + 1 < steps:
                    one.start(step + 1)
                work[number] = (one, step, out)
    for kind in range(3):
        owner, copy = home(kind)

        @pl.when(owner != p.member)
        def _():
            copy.wait_send()

    grads_in.drain()
    stats_in.drain()
    for one, begin in ((down, 1), (up, 0), (inner, 0), (outer, 0)):
        for step in range(begin, steps):
            one.drain(step)


def total_kernel(reps, x_ref, o_ref, held, send, recv):
    rep, member = lax.axis_index("rep"), lax.axis_index("grp")
    places = [(rep, flipped(member, bit)) for bit in doublings(GROUP)]
    places += [(flipped(rep, bit), member) for bit in doublings(reps)]
    barrier = pltpu.get_barrier_semaphore()
    for place in places:
        pl.semaphore_signal(barrier, inc=1, device_id=place, device_id_type=MESH)
    pl.semaphore_wait(barrier, len(places))
    o_ref[...] = x_ref[...]
    for slot, place in enumerate(places):
        copy = remote(o_ref, held.at[slot], send.at[slot], recv.at[slot], place)
        copy.start()
        copy.wait()
        o_ref[...] += held[slot]


def call(kernel, number, args, outs, scratch, smem=0, limit=63):
    vmem = pl.BlockSpec(memory_space=pltpu.VMEM)
    smem_spec = pl.BlockSpec(memory_space=pltpu.SMEM)
    linked = {} if number is None else {"collective_id": number, "has_side_effects": True}
    return pl.pallas_call(
        kernel,
        out_shape=[jax.ShapeDtypeStruct(*o) for o in outs],
        in_specs=[smem_spec] * smem + [vmem] * (len(args) - smem),
        out_specs=[vmem] * len(outs),
        scratch_shapes=scratch,
        compiler_params=pltpu.CompilerParams(vmem_limit_bytes=limit * 2**20, **linked),
    )(*args)


def per_device(
    tokens,
    cotangent,
    slice_sizes,
    gain_one,
    shift_one,
    attn_in,
    attn_bias,
    attn_out,
    out_bias,
    gain_two,
    shift_two,
    mlp_up,
    up_bias,
    mlp_down,
    down_bias,
):
    capacity, width = tokens.shape
    reps, groups = lax.axis_size("rep"), lax.axis_size("grp")
    assert groups == GROUP
    rows = -(-capacity // 128) * 128
    all_rows = GROUP * rows
    rep, member = lax.axis_index("rep"), lax.axis_index("grp")
    device = rep * groups + member
    ff_rows = mlp_up.shape[0]
    heads_high = GROUP * HP
    devices = reps * groups
    vm = pltpu.VMEM

    deep = -(-(width // reps) // 16) * 16
    own_count = slice_sizes[device]
    live_col = (jnp.arange(capacity, dtype=jnp.int32) < own_count)[:, None]
    w_in = jnp.pad(
        attn_in.reshape(3, GROUP, HD, width), ((0, 0), (0, 0), (0, HP - HD), (0, 0))
    ).reshape(3, heads_high, width)
    bias = jnp.stack([attn_bias[0], jnp.zeros((width,), F32), attn_bias[1]])
    bias = jnp.pad(
        bias.reshape(3 * GROUP, GROUP, HD), ((0, 0), (0, 0), (0, HP - HD))
    ).reshape(3 * GROUP, heads_high)
    w_out = jnp.pad(
        attn_out.reshape(GROUP, HD, width), ((0, 0), (0, HP - HD), (0, 0))
    ).reshape(heads_high, width)
    vectors = jnp.stack([gain_one, shift_one, out_bias, gain_two, shift_two, down_bias])
    place = (capacity, reps, rows)
    window_sems = [
        pltpu.SemaphoreType.DMA((len(OFFSETS) * GROUP,)), pltpu.SemaphoreType.DMA((WINDOW,))
    ]

    first, tok, query, window, cot_all = call(
        functools.partial(front_kernel, *place), 1,
        (slice_sizes, tokens, cotangent, vectors, w_in, bias),
        [((all_rows, width), BF), ((rows, width), BF), ((GROUP, heads_high, rows), BF),
         ((2 * WINDOW + GROUP, heads_high, rows), BF), ((all_rows, width), BF)],
        [vm((all_rows, width), BF), vm((3, GROUP, heads_high, rows), BF),
         vm((3, heads_high, all_rows), F32), *dma(5), *dma(5), *dma(4), *window_sems * 2],
        smem=1,
    )
    mixed, lse = call(
        functools.partial(attend_kernel, *place), None, (slice_sizes, query, window),
        [((heads_high, all_rows), BF), ((GROUP, all_rows), F32)],
        [vm((GROUP, 8, 2 * rows), F32), vm((heads_high, 2 * rows), F32)],
        smem=1,
    )
    gapped = reps * deep
    out, dresid, dmixed, stats, qwindow, dw_up, down_half, dw_out, sums_two, dup = call(
        functools.partial(middle_kernel, *place, deep), 2,
        (tok, cot_all, query, mixed, lse, w_out, mlp_up, mlp_down,
         up_bias.reshape(GROUP, ff_rows), vectors),
        [((rows, width), BF), ((rows, width), F32), ((heads_high, all_rows), BF),
         ((2 * GROUP, all_rows), F32), ((WINDOW, heads_high, rows), BF), ((gapped, ff_rows), BF),
         ((gapped // 2, ff_rows), BF), ((gapped, heads_high), BF), ((4, width), F32),
         ((1, ff_rows), F32)],
        [vm((all_rows, width), BF)] * 3
        + [vm((all_rows, ff_rows), BF)] * 2
        + [vm((all_rows, width), BF), vm((all_rows, ff_rows), F32), vm((gapped, ff_rows), BF),
           vm((rows, width), F32), vm((rows, width), F32), vm((3, 3, rows, width), BF)]
        + dma(3) + dma(5) + dma(3) + dma(5) + dma(3) + window_sems + halving_sems(reps),
    )
    input_grad, dbias, sums_one, dmlp_up, dmlp_down, dattn_out, dattn_in = call(
        functools.partial(back_kernel, *place, deep), 3,
        (window, qwindow, dmixed, stats, first, w_in.reshape(3 * heads_high, width), tok, dresid,
         vectors, dw_up, down_half, dw_out),
        [((rows, width), F32), ((heads_high, 3), F32), ((2, width), F32),
         ((deep, ff_rows), F32), ((deep, ff_rows), F32), ((deep, heads_high), F32),
         ((deep, 3 * heads_high), F32)],
        [vm((WINDOW, heads_high, rows), BF), vm((WINDOW, 2 * GROUP, rows), F32)]
        + [vm((heads_high, all_rows), F32)] * 2
        + [vm((3, heads_high, all_rows), BF), vm((3 * heads_high, all_rows), BF)]
        + [vm((all_rows, width), BF), vm((3, rows, width), BF)]
        + halving_levels(reps, deep, ff_rows, 1) + halving_levels(reps, deep, ff_rows, 2)
        + halving_levels(reps, deep, heads_high, 1)
        + halving_levels(reps, deep, 3 * heads_high, 0)
        + window_sems * 2 + dma(3) + dma(3) + halving_sems(reps) * 4,
    )
    narrow = width // reps
    dmlp_up, dmlp_down = dmlp_up[:narrow].T, dmlp_down[:narrow].T

    def without_gaps(grads):
        kinds = grads.shape[1] // heads_high
        return (
            grads[:narrow].T.reshape(kinds, GROUP, HP, narrow)[:, :, :HD]
            .reshape(kinds * GROUP * HD, narrow)
        )

    dattn_out, dattn_in = without_gaps(dattn_out), without_gaps(dattn_in)

    def totals(parts):
        flat = jnp.concatenate([part.reshape(-1) for part in parts])
        lines = -(-flat.shape[0] // 1024) * 8
        flat = jnp.pad(flat, (0, lines * 128 - flat.shape[0])).reshape(lines, 128)
        steps = len(doublings(reps)) + len(doublings(groups))
        [summed] = call(
            functools.partial(total_kernel, reps), 0, (flat,), [(flat.shape, F32)],
            [vm((steps, lines, 128), F32), *dma(steps)], limit=16,
        )
        summed = summed.reshape(-1)
        spot, outs = 0, []
        for part in parts:
            outs.append(summed[spot : spot + part.size].reshape(part.shape))
            spot += part.size
        return outs

    dbias = dbias.T.reshape(3, GROUP, HP)[:, :, :HD].reshape(3, GROUP * HD)
    dattn_bias = lax.dynamic_update_slice_in_dim(
        jnp.zeros((2, width), F32), dbias[0::2], member * GROUP * HD, 1
    )
    dup_bias = lax.dynamic_update_slice_in_dim(
        jnp.zeros(up_bias.shape, F32), dup[0], member * ff_rows, 0
    )
    dgain_one, dshift_one, dattn_bias, dout_bias, dgain_two, dshift_two, dup_bias, ddown_bias = (
        totals(
            (
                sums_one[0], sums_one[1], dattn_bias, sums_two[0], sums_two[1], sums_two[2],
                dup_bias, sums_two[3],
            )
        )
    )
    block_output = jnp.where(live_col, out[:capacity], jnp.zeros((), BF))
    input_grad = jnp.where(live_col, input_grad[:capacity], 0.0)
    return (
        block_output, input_grad, dgain_one, dshift_one, dattn_in, dattn_bias, dattn_out,
        dout_bias, dgain_two, dshift_two, dmlp_up, dup_bias, dmlp_down, ddown_bias,
    )


def solution(mesh):
    rows, rep_grp = P("grp", None), P(("rep", "grp"), None)
    in_specs = (
        rep_grp, rep_grp, P(), P(), P(), rows, P(), rows, P(), P(), P(), rows, P(), rows, P(),
    )
    grads = P("grp", "rep")
    out_specs = (
        rep_grp, rep_grp, P(), P(), grads, P(), grads, P(), P(), P(), grads, P(), grads, P(),
    )
    return jax.shard_map(
        per_device, mesh=mesh, in_specs=in_specs, out_specs=out_specs, check_vma=False
    )
```

```python
import functools

import jax
import jax.numpy as jnp
from jax import lax
from jax.experimental import pallas as pl
from jax.experimental.pallas import tpu as pltpu
from jax.sharding import PartitionSpec as P

H = 16
HD = 72
HP = 80
IMG = 729
GROUP = 4
NEAR_GROUPS = 2
WINDOW = (2 * NEAR_GROUPS + 1) * GROUP
OWN = NEAR_GROUPS * GROUP
OFFSETS = (1, -1, 2, -2)

EPSILON = 1e-06
SQRT_TWO_PI = 0.7978845608028654
CUBIC = 0.044715
FAR = -(2.0**80)
SCALE = HD ** (-0.5)
LOG2E = 1.4426950408889634
BF = jnp.bfloat16
F32 = jnp.float32
MESH = pl.DeviceIdType.MESH


def norm_parts(rows):
    centered = rows - jnp.mean(rows, axis=-1, keepdims=True)
    inverse = lax.rsqrt(jnp.mean(centered * centered, axis=-1, keepdims=True) + EPSILON)
    return centered * inverse, inverse


def norm_backward(dscaled, normed, inverse, gain_row):
    dnormed = dscaled * gain_row
    return inverse * (
        dnormed
        - jnp.mean(dnormed, axis=-1, keepdims=True)
        - normed * jnp.mean(dnormed * normed, axis=-1, keepdims=True)
    )


def gelu_parts(before):
    square = before * before
    tangent = jnp.tanh(SQRT_TWO_PI * before * (1.0 + CUBIC * square))
    half = 0.5 * (1.0 + tangent)
    derivative = half + 0.5 * before * (1.0 - tangent * tangent) * (
        SQRT_TWO_PI + SQRT_TWO_PI * 3.0 * CUBIC * square
    )
    return before * half, derivative


def dot_over(left, right, left_axis, right_axis):
    return lax.dot_general(
        left, right, (((left_axis,), (right_axis,)), ((), ())), preferred_element_type=F32
    )


def flipped(index, bit):
    return index + bit * (1 - 2 * ((index // bit) % 2))


def doublings(count):
    return [1 << i for i in range(count.bit_length() - 1)]


class Place:
    def __init__(self, capacity, reps, rows):
        self.capacity, self.reps, self.rows = capacity, reps, rows
        self.devices = reps * GROUP
        self.images = capacity * self.devices // IMG
        self.short = capacity * self.devices - self.images * IMG
        self.rep, self.member = lax.axis_index("rep"), lax.axis_index("grp")
        low = lax.rem(self.member, 2)
        self.near = self.member + 1 - 2 * low
        self.far = lax.rem(self.member + 2, GROUP)
        self.diagonal = lax.rem(self.near + 2, GROUP)
        self.pair = lax.div(self.member, 2)

    def sharing(self, low, high):
        capacity, short, image = self.capacity, self.short, jnp.int32(IMG)
        start = low * capacity - jnp.minimum(low, short)
        end = high * capacity - jnp.maximum(high - (self.devices - short), 0) - 1
        first = lax.div(start, image) * IMG
        after = (jnp.minimum(lax.div(end, image), self.images - 1) + 1) * IMG
        begin = lax.div(first, jnp.int32(capacity))
        stop = jnp.minimum(
            lax.div(after + short + capacity - 1, jnp.int32(capacity)),
            lax.div(after + capacity - 2, jnp.int32(capacity - 1)),
        )
        return begin, jnp.minimum(stop, self.devices)

    def slots(self, low, high):
        base = self.rep * GROUP
        begin, stop = self.sharing(base + low, base + high)
        return jnp.maximum(begin - base + OWN, 0), jnp.minimum(stop - base + OWN, WINDOW)

    def shares(self, block, group):
        begin, stop = self.sharing(group * GROUP, group * GROUP + GROUP)
        return (group >= 0) & (group < self.reps) & (block >= begin) & (block < stop)

    def block(self, owner):
        return pl.ds(pl.multiple_of(owner * self.rows, self.rows), self.rows)

    def pair_block(self, pair):
        return pl.ds(pl.multiple_of(pair * 2 * self.rows, 2 * self.rows), 2 * self.rows)

    def halving_barrier(self):
        barrier = pltpu.get_barrier_semaphore()
        bits = doublings(self.reps)
        for bit in bits:
            pl.semaphore_signal(
                barrier, inc=1, device_id=(flipped(self.rep, bit), self.member),
                device_id_type=MESH,
            )
        return len(bits)

    def group_barrier(self):
        barrier = pltpu.get_barrier_semaphore()
        for other in (self.near, self.far):
            pl.semaphore_signal(
                barrier, inc=1, device_id=(self.rep, other), device_id_type=MESH
            )
        return barrier, 2

    def wide_barrier(self):
        barrier, count = self.group_barrier()
        count = jnp.int32(count)
        for offset in OFFSETS:
            there = self.rep + offset
            valid = (there >= 0) & (there < self.reps)

            @pl.when(valid)
            def _():
                pl.semaphore_signal(
                    barrier, inc=1, device_id=(there, self.member), device_id_type=MESH
                )

            count = count + jnp.where(valid, 1, 0)
        return barrier, count


def remote(source, target, send, recv, place):
    return pltpu.make_async_remote_copy(
        src_ref=source,
        dst_ref=target,
        send_sem=send,
        recv_sem=recv,
        device_id=place,
        device_id_type=MESH,
    )


class Gather:
    def __init__(self, place, ref, rows, send, recv):
        self.place, self.ref, self.rows, self.send, self.recv = place, ref, rows, send, recv
        self.half = rows // 2

    def copy(self, owner, part, slot, target):
        if part is None:
            piece = self.ref.at[pl.ds(pl.multiple_of(owner * self.rows, self.rows), self.rows), :]
        else:
            start = pl.multiple_of(owner * self.rows + part * self.half, self.half)
            piece = self.ref.at[pl.ds(start, self.half), :]
        return remote(
            piece, piece, self.send.at[slot], self.recv.at[slot], (self.place.rep, target)
        )

    def start(self):
        p = self.place
        for part in range(2):
            self.copy(p.member, part, 1 + part, p.far).start()
        self.copy(p.member, None, 0, p.near).start()

    def wait_near(self):
        p = self.place
        self.copy(p.near, None, 0, p.near).wait_recv()

    def forward(self, part):
        p = self.place
        self.copy(p.far, part, 1 + part, p.far).wait_recv()
        self.copy(p.far, part, 3 + part, p.near).start()

    def wait_rest(self):
        p = self.place
        for part in range(2):
            self.copy(p.diagonal, part, 3 + part, p.near).wait_recv()

    def drain(self):
        p = self.place
        self.copy(p.member, None, 0, p.near).wait_send()
        for part in range(2):
            self.copy(p.member, part, 1 + part, p.far).wait_send()
            self.copy(p.far, part, 3 + part, p.near).wait_send()


class Scatter:
    def __init__(self, place, ref, held, rows, send, recv):
        self.place, self.ref, self.held = place, ref, held
        self.rows, self.send, self.recv = rows, send, recv

    def block(self, owner):
        return pl.ds(pl.multiple_of(owner * self.rows, self.rows), self.rows)

    def ahead(self):
        p = self.place
        return remote(
            self.ref.at[self.block(p.diagonal), :], self.held.at[0],
            self.send.at[0], self.recv.at[0], (p.rep, p.near),
        )

    def own(self):
        p = self.place
        return remote(
            self.ref.at[self.block(p.near), :], self.held.at[1],
            self.send.at[1], self.recv.at[1], (p.rep, p.near),
        )

    def across(self):
        p = self.place
        return remote(
            self.held.at[0], self.held.at[2], self.send.at[2], self.recv.at[2], (p.rep, p.far)
        )

    def pass_on(self):
        p = self.place
        self.ahead().wait_recv()
        self.held[0] = (
            self.ref[self.block(p.far), :].astype(F32) + self.held[0].astype(F32)
        ).astype(BF)
        self.across().start()

    def result(self):
        p = self.place
        self.own().wait_recv()
        total = self.ref[self.block(p.member), :].astype(F32) + self.held[1].astype(F32)
        self.across().wait_recv()
        total = total + self.held[2].astype(F32)
        self.ahead().wait_send()
        self.own().wait_send()
        self.across().wait_send()
        return total


class Exchange:
    def __init__(self, place, view, send, recv):
        self.place, self.view, self.send, self.recv = place, view, send, recv

    def outgoing(self, act):
        p = self.place
        for number, offset in enumerate(OFFSETS):
            begin, stop = p.sharing((p.rep + offset) * GROUP, (p.rep + offset + 1) * GROUP)
            valid = (p.rep + offset >= 0) & (p.rep + offset < p.reps)
            for index in range(GROUP):
                block = p.rep * GROUP + index
                slot_there = OWN - offset * GROUP + index

                @pl.when(valid & (block >= begin) & (block < stop))
                def _():
                    act(
                        remote(
                            self.view(OWN + index),
                            self.view(slot_there),
                            self.send.at[number * GROUP + index],
                            self.recv.at[slot_there],
                            (p.rep + offset, p.member),
                        )
                    )

    def start(self):
        self.outgoing(lambda copy: copy.start())

    def drain(self):
        self.outgoing(lambda copy: copy.wait_send())

    def wait(self):
        p = self.place
        begin, stop = p.slots(0, GROUP)
        for offset in OFFSETS:
            for index in range(GROUP):
                slot = OWN + offset * GROUP + index

                @pl.when((slot >= begin) & (slot < stop))
                def _():
                    remote(
                        self.view(slot), self.view(slot), self.send.at[0], self.recv.at[slot],
                        (p.rep, p.near),
                    ).wait_recv()


def dma(count):
    return [pltpu.SemaphoreType.DMA((count,))] * 2


class Halving:
    def __init__(self, place, levels, deep, send, recv):
        self.place, self.levels, self.deep = place, levels, deep
        self.send, self.recv = send, recv
        self.bits = doublings(place.reps)

    def mine(self, step):
        return lax.rem(lax.div(self.place.rep, jnp.int32(self.bits[step])), 2)

    def partner(self, step):
        p = self.place
        return (flipped(p.rep, self.bits[step]), p.member)

    def rows(self, start, count):
        return pl.ds(pl.multiple_of(start * self.deep, self.deep), count * self.deep)

    def firsts(self):
        rest = self.bits[1:]
        for j in range(self.place.reps // 2):
            yield j, sum(bit * ((j >> (len(rest) - 1 - q)) & 1) for q, bit in enumerate(rest))

    def copies(self, step):
        give = 1 - self.mine(step)
        source, target = self.levels[step], self.levels[step + 1]
        if step == 0:
            return [
                remote(
                    source.at[self.rows(give * self.bits[0] + offset, 1), :],
                    target.at[self.rows(j, 1), :],
                    self.send.at[j], self.recv.at[j], self.partner(0),
                )
                for j, offset in self.firsts()
            ]
        half = self.place.reps >> (step + 1)
        slot = self.place.reps // 2 + step - 1
        return [
            remote(
                source.at[self.rows(give * half, half), :], target.at[self.rows(0, half), :],
                self.send.at[slot], self.recv.at[slot], self.partner(step),
            )
        ]

    def start(self, step):
        for copy in self.copies(step):
            copy.start()

    def finish(self, step, out=None):
        copies = self.copies(step)
        mine = self.mine(step)
        source, target = self.levels[step], self.levels[step + 1]
        half = self.place.reps >> (step + 1)
        if step == 0:
            for j, offset in self.firsts():
                copies[j].wait_recv()
                at = self.rows(j, 1)
                kept = source[self.rows(mine * self.bits[0] + offset, 1), :]
                target[at, :] = (target[at, :].astype(F32) + kept.astype(F32)).astype(BF)
            return
        copies[0].wait_recv()
        for j in range(half):
            at = self.rows(j, 1)
            kept = source[self.rows(mine * half + j, 1), :]
            total = target[at, :].astype(F32) + kept.astype(F32)
            if out is None:
                target[at, :] = total.astype(BF)
            else:
                out[...] = total

    def drain(self, step):
        for copy in self.copies(step):
            copy.wait_send()


def halving_sems(reps):
    return dma(reps // 2 + reps.bit_length() - 2)


def halving_levels(reps, deep, wide, first):
    return [
        pltpu.VMEM(((reps >> s) * deep, wide), BF) for s in range(first, reps.bit_length())
    ]


def grad_chunks(left, right, right_axis, target, deep, narrow):
    chunk = 128
    width = left.shape[1]

    def body(i, carry):
        at = pl.ds(pl.multiple_of(i * chunk, chunk), chunk)
        if deep == narrow:
            columns = left[:, at]
        else:
            source = lax.broadcasted_iota(jnp.int32, (width, chunk), 0)
            column = lax.broadcasted_iota(jnp.int32, (width, chunk), 1) + i * chunk
            within = column % deep
            picked = (source == (column // deep) * narrow + within) & (within < narrow)
            columns = dot_over(left[...], jnp.where(picked, 1.0, 0.0).astype(BF), 1, 0).astype(BF)
        target[at, :] = dot_over(columns, right[...], 0, right_axis).astype(BF)
        return carry

    lax.fori_loop(0, target.shape[0] // chunk, body, 0)


def image_codes(place, sizes_ref, kind):
    start = lax.fori_loop(0, place.rep * GROUP, lambda i, n: n + sizes_ref[i], jnp.int32(0))
    index = lax.broadcasted_iota(jnp.int32, (8, place.rows), 1)
    row = lax.broadcasted_iota(jnp.int32, (8, place.rows), 0)
    codes = []
    for b in range(GROUP):
        size = sizes_ref[place.rep * GROUP + b]
        base = lax.div(start, jnp.int32(IMG))
        turn = (base + 1) * IMG - start
        kind_of_image = lax.rem(base + jnp.where(index >= turn, 1, 0), 4)
        live = index < size
        same = kind_of_image == row
        query = jnp.where(same | ~live, 1.0, 0.0)
        key = jnp.where(same & live, 0.0, FAR)
        code = jnp.where(kind == 0, query, key)
        code = jnp.where(row < 4, code, 0.0)
        codes.append(jnp.where(kind == 2, jnp.where(row == 0, 1.0, 0.0), code))
        start = start + size
    return codes


def front_kernel(
    capacity, reps, rows, sizes_ref, tok_ref, cot_ref, gain_ref, shift_ref, w_ref, bias_ref,
    first_ref, own_ref, query_ref, win_ref, cotall_ref,
    xall, sbuf, code, gsend, grecv, csend, crecv, ssend, srecv, ksend, krecv, vsend, vrecv,
):
    p = Place(capacity, reps, rows)
    barrier, count = p.wide_barrier()
    size = sizes_ref[p.rep * GROUP + p.member]
    live = lax.broadcasted_iota(jnp.int32, (capacity, 1), 0) < size
    clean = lambda ref: jnp.where(live, ref[...].astype(F32), 0.0).astype(BF)
    own_ref[...] = jnp.zeros_like(own_ref)
    own_ref[pl.ds(0, capacity), :] = clean(tok_ref)
    xall[p.block(p.member), :] = own_ref[...]
    pl.semaphore_wait(barrier, count)
    tokens = Gather(p, xall, rows, gsend, grecv)
    tokens.start()
    cotall_ref[p.block(p.member), :] = jnp.zeros((rows, tok_ref.shape[1]), BF)
    cotall_ref[pl.ds(pl.multiple_of(p.member * rows, rows), capacity), :] = clean(cot_ref)
    gain, shift = gain_ref[...][None, :], shift_ref[...][None, :]

    def normalize(owner):
        block = p.block(owner)
        normed, _ = norm_parts(xall[block, :].astype(F32))
        first_ref[block, :] = (normed * gain + shift).astype(BF)

    odd = lax.rem(p.member, 2)
    cross = 2 - 2 * odd
    kept = 2 * odd
    kind_of = lambda i: lax.div(3 * p.member + i, GROUP)
    def spot_of(i):
        kind = kind_of(i)
        return jnp.where(kind == 0, 2 * WINDOW, (kind - 1) * WINDOW + OWN)

    gap = jnp.zeros((HD, rows), F32)
    for i in range(3):
        for b, rest in enumerate(image_codes(p, sizes_ref, kind_of(i))):
            at = slice(b * rows, (b + 1) * rows)
            for h in range(GROUP):
                code[i, h * HP : (h + 1) * HP, at] = jnp.concatenate([gap, rest], axis=0)

    def project(i, pair):
        block = first_ref[p.pair_block(pair), :]
        bias = bias_ref[pl.ds(3 * p.member + i, 1), :]
        bias = jnp.transpose(jnp.broadcast_to(bias, (8, bias.shape[1])))[:, 0:1]
        total = dot_over(w_ref[i], block, 1, 1) + bias + code[i, :, p.pair_block(pair)]
        for b in range(2):
            sbuf[i, pair * 2 + b] = total[:, b * rows : (b + 1) * rows].astype(BF)

    def shuffle(i, pair, way, target):
        slot = way * 2 + pair
        return remote(
            sbuf.at[i, pl.ds(pair * 2, 2)],
            win_ref.at[pl.ds(spot_of(i) + pair * 2, 2)],
            ssend.at[slot], srecv.at[slot], (p.rep, target),
        )

    normalize(p.member)
    tokens.wait_near()
    normalize(p.near)
    tokens.forward(0)
    project(cross, p.pair)
    shuffle(cross, p.pair, 0, p.far).start()
    tokens.forward(1)
    project(1, p.pair)
    shuffle(1, p.pair, 1, p.near).start()
    project(kept, p.pair)
    other = 1 - p.pair
    normalize(p.far)
    tokens.wait_rest()
    normalize(p.diagonal)
    project(cross, other)
    shuffle(cross, other, 0, p.far).start()
    project(1, other)
    shuffle(1, other, 1, p.near).start()
    project(kept, other)
    win_ref[pl.ds(spot_of(kept), GROUP)] = sbuf[kept]
    for pair in (p.pair, other):
        shuffle(cross, pair, 0, p.far).wait_recv()
        shuffle(1, pair, 1, p.near).wait_recv()
    keys = Exchange(p, lambda slot: win_ref.at[slot], ksend, krecv)
    values = Exchange(p, lambda slot: win_ref.at[WINDOW + slot], vsend, vrecv)
    keys.start()
    values.start()
    cotangents = Gather(p, cotall_ref, rows, csend, crecv)
    cotangents.start()
    query_ref[...] = win_ref[pl.ds(2 * WINDOW, GROUP)]
    cotangents.wait_near()
    cotangents.forward(0)
    cotangents.forward(1)
    cotangents.wait_rest()
    keys.wait()
    values.wait()
    keys.drain()
    values.drain()
    for pair in (p.pair, other):
        shuffle(cross, pair, 0, p.far).wait_send()
        shuffle(1, pair, 1, p.near).wait_send()
    tokens.drain()
    cotangents.drain()


def joined(view, head, blocks):
    return jnp.concatenate([view(b)[head, :] for b in blocks], axis=1)


def pieces(rows):
    count = max(512 // rows, 1)
    for low in range(0, GROUP, count):
        yield range(low, low + count), slice(low * rows, (low + count) * rows)


def attend_kernel(capacity, reps, rows, sizes_ref, query_ref, win_ref, mixed_ref, lse_ref, acc):
    p = Place(capacity, reps, rows)
    heads = [slice(h * HP, (h + 1) * HP) for h in range(GROUP)]
    for blocks, at in pieces(rows):
        begin, stop = p.slots(blocks[0], blocks[-1] + 1)
        acc[:, at] = jnp.zeros((acc.shape[0], at.stop - at.start), F32)
        queries = [joined(lambda b: query_ref.at[b], head, blocks) for head in heads]

        def attend(slot, tops):
            raws = [dot_over(win_ref[slot, head, :], query, 0, 0) for head, query in zip(heads, queries)]
            news = [
                jnp.maximum(top, jnp.max(raw, axis=0, keepdims=True) * (SCALE * LOG2E))
                for top, raw in zip(tops, raws)
            ]
            powers = [
                jnp.exp2(raw * (SCALE * LOG2E) - new).astype(BF) for raw, new in zip(raws, news)
            ]
            for head, top, new, power in zip(heads, tops, news, powers):
                value = win_ref[WINDOW + slot, head, :]
                acc[head, at] = acc[head, at] * jnp.exp2(top - new) + dot_over(value, power, 1, 0)
            return tuple(news)

        tops = lax.fori_loop(
            begin, stop, attend, tuple(jnp.full((1, at.stop - at.start), 4.0 * FAR, F32) for _ in heads)
        )
        index = lax.broadcasted_iota(jnp.int32, (1, rows), 1)
        live = jnp.concatenate(
            [
                jnp.where(index < sizes_ref[p.rep * GROUP + b], 1.0, 0.0) for b in blocks
            ],
            axis=1,
        )
        for h, head in enumerate(heads):
            whole = acc[h * HP + HD : h * HP + HD + 1, at]
            mixed_ref[head, at] = (acc[head, at] / whole).astype(BF)
            lse_ref[h : h + 1, at] = jnp.where(live > 0.0, tops[h] + jnp.log(whole) * LOG2E, 0.0)


def middle_kernel(
    capacity, reps, rows, deep, tok_ref, cot_ref, query_ref, mixed_ref, lse_ref, wo_ref, wup_ref,
    wdn_ref, upb_ref, outb_ref, gain_ref, shift_ref, downb_ref,
    out_ref, dres_ref, dmix_ref, stats_ref, qwin_ref, dwup_ref, down_ref, dwo_ref, sums_ref,
    dupb_ref,
    part, part2, second, hidden, dbefore, dresall, dact, dwdn, res_scr, norm_scr, held,
    asend, arecv, bsend, brecv, csend, crecv, dsend, drecv, esend, erecv, qsend, qrecv,
    hsend, hrecv,
):
    p = Place(capacity, reps, rows)
    barrier, count = p.wide_barrier()
    count = count + p.halving_barrier()
    out_bias, gain, shift, down_bias = (
        ref[...][None, :] for ref in (outb_ref, gain_ref, shift_ref, downb_ref)
    )
    other = 1 - p.pair
    narrow = cot_ref.shape[1] // reps

    def attn_partial(owner):
        part[p.block(owner), :] = dot_over(
            mixed_ref[:, p.block(owner)], wo_ref[...], 0, 0
        ).astype(BF)

    attn_partial(p.diagonal)
    pl.semaphore_wait(barrier, count)
    one = Scatter(p, part, held.at[0], rows, asend, arecv)
    one.ahead().start()
    attn_partial(p.near)
    one.own().start()
    qwin_ref[pl.ds(OWN, GROUP)] = query_ref[...]
    queries = Exchange(p, lambda slot: qwin_ref.at[slot], qsend, qrecv)
    queries.start()
    attn_partial(p.far)
    one.pass_on()
    attn_partial(p.member)
    for pair in (0, 1):
        at = pl.ds(pair * 2 * rows, 2 * rows)
        dact[at, :] = dot_over(cot_ref[at, :], wdn_ref[...], 1, 1)
    resid = tok_ref[...].astype(F32) + one.result() + out_bias
    res_scr[...] = resid
    normed, inverse = norm_parts(resid)
    norm_scr[...] = normed
    second[p.block(p.member), :] = (normed * gain + shift).astype(BF)
    gather = Gather(p, second, rows, bsend, brecv)
    gather.start()

    def mlp(pair):
        at = p.pair_block(pair)
        before = dot_over(second[at, :], wup_ref[...], 1, 1) + upb_ref[pl.ds(p.member, 1), :]
        activated, derivative = gelu_parts(before)
        hidden[at, :] = activated.astype(BF)
        grad = dact[at, :] * derivative
        dact[at, :] = grad
        dbefore[at, :] = grad.astype(BF)
        part2[at, :] = dot_over(dbefore[at, :], wup_ref[...], 1, 0).astype(BF)

    gather.wait_near()
    gather.forward(0)
    mlp(p.pair)
    gather.forward(1)
    two = Scatter(p, part2, held.at[1], rows, csend, crecv)
    two.own().start()
    gather.wait_rest()
    mlp(other)
    two.ahead().start()
    grad_chunks(cot_ref, hidden, 0, dwdn, deep, narrow)
    halving = Halving(p, [dwdn, down_ref], deep, hsend, hrecv)
    halving.start(0)
    two.pass_on()

    def down(pair):
        at = p.pair_block(pair)
        part[at, :] = dot_over(hidden[at, :], wdn_ref[...], 1, 0).astype(BF)

    down(other)
    down(p.pair)
    three = Scatter(p, part, held.at[2], rows, esend, erecv)
    three.ahead().start()
    three.own().start()
    dsecond = two.result()
    own_cot = cot_ref[p.block(p.member), :].astype(F32)
    normed = norm_scr[...]
    dresid = own_cot + norm_backward(dsecond, normed, inverse, gain)
    dres_ref[...] = dresid
    dresall[p.block(p.member), :] = dresid.astype(BF)
    again = Gather(p, dresall, rows, dsend, drecv)
    again.start()
    three.pass_on()
    dupb_ref[...] = jnp.sum(dact[...], axis=0, keepdims=True)
    for i, term in enumerate((dresid, dsecond * normed, dsecond, own_cot)):
        sums_ref[pl.ds(i, 1), :] = jnp.sum(term, axis=0, keepdims=True)
    again.wait_near()
    again.forward(0)

    def mixed_grad(pair):
        at = p.pair_block(pair)
        dmixed = dot_over(wo_ref[...], dresall[at, :], 1, 1).astype(BF)
        dmix_ref[:, at] = dmixed
        product = dmixed.astype(F32) * mixed_ref[:, at].astype(F32)
        stats_ref[pl.ds(0, GROUP), at] = lse_ref[:, at]
        for h in range(GROUP):
            stats_ref[pl.ds(GROUP + h, 1), at] = jnp.sum(
                product[h * HP : (h + 1) * HP], axis=0, keepdims=True
            )

    grad_chunks(second, dbefore, 0, dwup_ref, deep, narrow)
    mixed_grad(p.pair)
    again.forward(1)
    again.wait_rest()
    mixed_grad(other)
    grad_chunks(dresall, mixed_ref, 1, dwo_ref, deep, narrow)
    out_ref[...] = (res_scr[...] + three.result() + down_bias).astype(BF)
    queries.wait()
    queries.drain()
    halving.finish(0)
    halving.drain(0)
    gather.drain()
    again.drain()


def back_kernel(
    capacity, reps, rows, deep, win_ref, qwin_ref, dmix_ref, stats_ref, first_ref, w_ref, tok_ref,
    dres_ref, gain_ref, dwup_ref, down_ref, dwo_ref,
    grad_ref, dbias_ref, sums_ref, dup_out, ddn_out, dwo_out, dwi_out,
    dwin, swin, dq, dv, sbuf, dproj, part, held, *rest,
):
    steps = reps.bit_length() - 1
    scratch = list(rest)
    take = lambda n: [scratch.pop(0) for _ in range(n)]
    up_levels, dn_levels = [dwup_ref] + take(steps), [None, down_ref] + take(steps - 1)
    wo_levels, wi_levels = [dwo_ref] + take(steps), take(steps + 1)
    (ksend, krecv, tsend, trecv, ssend, srecv, rsend, rrecv) = take(8)
    p = Place(capacity, reps, rows)
    barrier, count = p.wide_barrier()
    count = count + p.halving_barrier()
    for b in range(GROUP):
        at = slice(b * rows, (b + 1) * rows)
        dwin[OWN + b] = dmix_ref[:, at]
        swin[OWN + b] = stats_ref[:, at]
    pl.semaphore_wait(barrier, count)
    grads_in = Exchange(p, lambda slot: dwin.at[slot], ksend, krecv)
    stats_in = Exchange(p, lambda slot: swin.at[slot], tsend, trecv)
    grads_in.start()
    stats_in.start()
    down = Halving(p, dn_levels, deep, *take(2))
    up = Halving(p, up_levels, deep, *take(2))
    inner = Halving(p, wi_levels, deep, *take(2))
    outer = Halving(p, wo_levels, deep, *take(2))
    down.start(1)
    up.start(0)
    heads = [slice(h * HP, (h + 1) * HP) for h in range(GROUP)]
    every = range(GROUP)
    for blocks, at in pieces(rows):
        begin, stop = p.slots(blocks[0], blocks[-1] + 1)
        queries = [joined(lambda b: qwin_ref.at[OWN + b], head, blocks) for head in heads]
        dq[:, at] = jnp.zeros((dq.shape[0], at.stop - at.start), F32)

        def query_grads(slot, carry):
            keys = [win_ref[slot, head, :] for head in heads]
            raws = [dot_over(keys[h], queries[h], 0, 0) for h in every]
            dprobs = [
                dot_over(win_ref[WINDOW + slot, head, :], dmix_ref[head, at], 0, 0) for head in heads
            ]
            dscores = [
                (
                    jnp.exp2(raws[h] * (SCALE * LOG2E) - stats_ref[h : h + 1, at])
                    * (dprobs[h] - stats_ref[GROUP + h : GROUP + h + 1, at])
                ).astype(BF)
                for h in every
            ]
            for h, head in enumerate(heads):
                dq[head, at] += dot_over(keys[h], dscores[h], 1, 0)
            return carry

        lax.fori_loop(begin, stop, query_grads, 0)

    def owner_of(kind):
        c = kind * GROUP + p.member
        return lax.div(c, 3), lax.rem(c, 3)

    high = GROUP * HP

    def part_of(index):
        return pl.ds(pl.multiple_of(index * high, high), high)

    def home(kind):
        owner, index = owner_of(kind)
        return owner, remote(
            sbuf.at[kind], dproj.at[part_of(index), :], ssend.at[kind], srecv.at[index],
            (p.rep, owner),
        )

    def send_home(kind, grads, scale):
        value = grads[...] * scale
        sbuf[kind] = value.astype(BF)
        dbias_ref[:, kind : kind + 1] = jnp.sum(value, axis=1, keepdims=True)
        owner, copy = home(kind)

        @pl.when(owner != p.member)
        def _():
            copy.start()

    send_home(0, dq, SCALE)
    dk = dq
    grads_in.wait()
    stats_in.wait()
    for blocks, at in pieces(rows):
        begin, stop = p.slots(blocks[0], blocks[-1] + 1)
        keys = [joined(lambda b: win_ref.at[OWN + b], head, blocks) for head in heads]
        values = [joined(lambda b: win_ref.at[WINDOW + OWN + b], head, blocks) for head in heads]
        dk[:, at] = jnp.zeros((dk.shape[0], at.stop - at.start), F32)
        dv[:, at] = jnp.zeros((dv.shape[0], at.stop - at.start), F32)

        def key_grads(slot, carry):
            stats = jnp.transpose(swin[slot])
            picked = [qwin_ref[slot, head, :] for head in heads]
            dmixed = [dwin[slot, head, :] for head in heads]
            raws = [dot_over(picked[h], keys[h], 0, 0) for h in every]
            dprobs = [dot_over(dmixed[h], values[h], 0, 0) for h in every]
            probs = [jnp.exp2(raws[h] * (SCALE * LOG2E) - stats[:, h : h + 1]) for h in every]
            dscores = [
                (probs[h] * (dprobs[h] - stats[:, GROUP + h : GROUP + h + 1])).astype(BF)
                for h in every
            ]
            for h, head in enumerate(heads):
                dk[head, at] += dot_over(picked[h], dscores[h], 1, 0)
            for h, head in enumerate(heads):
                dv[head, at] += dot_over(dmixed[h], probs[h].astype(BF), 1, 0)
            return carry

        lax.fori_loop(begin, stop, key_grads, 0)

    send_home(1, dk, SCALE)
    send_home(2, dv, 1.0)
    for kind in range(3):
        owner, index = owner_of(kind)

        @pl.when(owner == p.member)
        def _():
            dproj[part_of(index), :] = sbuf[kind]

    down.finish(1)
    down.start(2)
    up.finish(0)
    up.start(1)
    for index in range(3):
        source = lax.rem(3 * p.member + index, GROUP)

        @pl.when(source != p.member)
        def _():
            remote(
                sbuf.at[0], dproj.at[part_of(index), :], ssend.at[0], srecv.at[index],
                (p.rep, p.near),
            ).wait_recv()

    narrow = first_ref.shape[1] // reps
    grad_chunks(first_ref, dproj, 1, wi_levels[0], deep, narrow)
    inner.start(0)
    outer.start(0)

    def partial(owner):
        part[p.block(owner), :] = dot_over(dproj[:, p.block(owner)], w_ref[...], 0, 0).astype(BF)

    scatter = Scatter(p, part, held, rows, rsend, rrecv)
    partial(p.diagonal)
    scatter.ahead().start()
    partial(p.near)
    scatter.own().start()
    partial(p.far)
    scatter.pass_on()
    partial(p.member)
    normed, inverse = norm_parts(tok_ref[...].astype(F32))
    dfirst = scatter.result()
    for i, term in enumerate((dfirst * normed, dfirst)):
        sums_ref[pl.ds(i, 1), :] = jnp.sum(term, axis=0, keepdims=True)
    grad_ref[...] = dres_ref[...] + norm_backward(dfirst, normed, inverse, gain_ref[...][None, :])
    work = [(down, 1, ddn_out), (up, 0, dup_out), (inner, -1, dwi_out), (outer, -1, dwo_out)]
    for _ in range(steps + 1):
        for number, (one, done, out) in enumerate(work):
            step = done + 1
            if step < steps:
                one.finish(step, out if step == steps - 1 else None)
                if step + 1 < steps:
                    one.start(step + 1)
                work[number] = (one, step, out)
    for kind in range(3):
        owner, copy = home(kind)

        @pl.when(owner != p.member)
        def _():
            copy.wait_send()

    grads_in.drain()
    stats_in.drain()
    for one, begin in ((down, 1), (up, 0), (inner, 0), (outer, 0)):
        for step in range(begin, steps):
            one.drain(step)


def total_kernel(reps, x_ref, o_ref, held, send, recv):
    rep, member = lax.axis_index("rep"), lax.axis_index("grp")
    places = [(rep, flipped(member, bit)) for bit in doublings(GROUP)]
    places += [(flipped(rep, bit), member) for bit in doublings(reps)]
    barrier = pltpu.get_barrier_semaphore()
    for place in places:
        pl.semaphore_signal(barrier, inc=1, device_id=place, device_id_type=MESH)
    pl.semaphore_wait(barrier, len(places))
    o_ref[...] = x_ref[...]
    for slot, place in enumerate(places):
        copy = remote(o_ref, held.at[slot], send.at[slot], recv.at[slot], place)
        copy.start()
        copy.wait()
        o_ref[...] += held[slot]


def call(kernel, number, args, outs, scratch, smem=0, limit=63):
    vmem = pl.BlockSpec(memory_space=pltpu.VMEM)
    smem_spec = pl.BlockSpec(memory_space=pltpu.SMEM)
    linked = {} if number is None else {"collective_id": number, "has_side_effects": True}
    return pl.pallas_call(
        kernel,
        out_shape=[jax.ShapeDtypeStruct(*o) for o in outs],
        in_specs=[smem_spec] * smem + [vmem] * (len(args) - smem),
        out_specs=[vmem] * len(outs),
        scratch_shapes=scratch,
        compiler_params=pltpu.CompilerParams(vmem_limit_bytes=limit * 2**20, **linked),
    )(*args)


def per_device(
    tokens,
    cotangent,
    slice_sizes,
    gain_one,
    shift_one,
    attn_in,
    attn_bias,
    attn_out,
    out_bias,
    gain_two,
    shift_two,
    mlp_up,
    up_bias,
    mlp_down,
    down_bias,
):
    capacity, width = tokens.shape
    reps, groups = lax.axis_size("rep"), lax.axis_size("grp")
    assert groups == GROUP
    rows = -(-capacity // 128) * 128
    all_rows = GROUP * rows
    rep, member = lax.axis_index("rep"), lax.axis_index("grp")
    device = rep * groups + member
    ff_rows = mlp_up.shape[0]
    heads_high = GROUP * HP
    devices = reps * groups
    vm = pltpu.VMEM

    deep = -(-(width // reps) // 16) * 16
    own_count = slice_sizes[device]
    live_col = (jnp.arange(capacity, dtype=jnp.int32) < own_count)[:, None]
    w_in = jnp.pad(
        attn_in.reshape(3, GROUP, HD, width), ((0, 0), (0, 0), (0, HP - HD), (0, 0))
    ).reshape(3, heads_high, width)
    bias = jnp.stack([attn_bias[0], jnp.zeros((width,), F32), attn_bias[1]])
    bias = jnp.pad(
        bias.reshape(3 * GROUP, GROUP, HD), ((0, 0), (0, 0), (0, HP - HD))
    ).reshape(3 * GROUP, heads_high)
    w_out = jnp.pad(
        attn_out.reshape(GROUP, HD, width), ((0, 0), (0, HP - HD), (0, 0))
    ).reshape(heads_high, width)
    place = (capacity, reps, rows)
    window_sems = [
        pltpu.SemaphoreType.DMA((len(OFFSETS) * GROUP,)), pltpu.SemaphoreType.DMA((WINDOW,))
    ]

    first, tok, query, window, cot_all = call(
        functools.partial(front_kernel, *place), 1,
        (slice_sizes, tokens, cotangent, gain_one, shift_one, w_in, bias),
        [((all_rows, width), BF), ((rows, width), BF), ((GROUP, heads_high, rows), BF),
         ((2 * WINDOW + GROUP, heads_high, rows), BF), ((all_rows, width), BF)],
        [vm((all_rows, width), BF), vm((3, GROUP, heads_high, rows), BF),
         vm((3, heads_high, all_rows), F32), *dma(5), *dma(5), *dma(4), *window_sems * 2],
        smem=1,
    )
    mixed, lse = call(
        functools.partial(attend_kernel, *place), None, (slice_sizes, query, window),
        [((heads_high, all_rows), BF), ((GROUP, all_rows), F32)],
        [vm((heads_high, all_rows), F32)],
        smem=1,
    )
    gapped = reps * deep
    out, dresid, dmixed, stats, qwindow, dw_up, down_half, dw_out, sums_two, dup = call(
        functools.partial(middle_kernel, *place, deep), 2,
        (tok, cot_all, query, mixed, lse, w_out, mlp_up, mlp_down,
         up_bias.reshape(GROUP, ff_rows), out_bias, gain_two, shift_two, down_bias),
        [((rows, width), BF), ((rows, width), F32), ((heads_high, all_rows), BF),
         ((2 * GROUP, all_rows), F32), ((WINDOW, heads_high, rows), BF), ((gapped, ff_rows), BF),
         ((gapped // 2, ff_rows), BF), ((gapped, heads_high), BF), ((4, width), F32),
         ((1, ff_rows), F32)],
        [vm((all_rows, width), BF)] * 3
        + [vm((all_rows, ff_rows), BF)] * 2
        + [vm((all_rows, width), BF), vm((all_rows, ff_rows), F32), vm((gapped, ff_rows), BF),
           vm((rows, width), F32), vm((rows, width), F32), vm((3, 3, rows, width), BF)]
        + dma(3) + dma(5) + dma(3) + dma(5) + dma(3) + window_sems + halving_sems(reps),
    )
    input_grad, dbias, sums_one, dmlp_up, dmlp_down, dattn_out, dattn_in = call(
        functools.partial(back_kernel, *place, deep), 3,
        (window, qwindow, dmixed, stats, first, w_in.reshape(3 * heads_high, width), tok, dresid,
         gain_one, dw_up, down_half, dw_out),
        [((rows, width), F32), ((heads_high, 3), F32), ((2, width), F32),
         ((deep, ff_rows), F32), ((deep, ff_rows), F32), ((deep, heads_high), F32),
         ((deep, 3 * heads_high), F32)],
        [vm((WINDOW, heads_high, rows), BF), vm((WINDOW, 2 * GROUP, rows), F32)]
        + [vm((heads_high, all_rows), F32)] * 2
        + [vm((3, heads_high, all_rows), BF), vm((3 * heads_high, all_rows), BF)]
        + [vm((all_rows, width), BF), vm((3, rows, width), BF)]
        + halving_levels(reps, deep, ff_rows, 1) + halving_levels(reps, deep, ff_rows, 2)
        + halving_levels(reps, deep, heads_high, 1)
        + halving_levels(reps, deep, 3 * heads_high, 0)
        + window_sems * 2 + dma(3) + dma(3) + halving_sems(reps) * 4,
    )
    narrow = width // reps
    dmlp_up, dmlp_down = dmlp_up[:narrow].T, dmlp_down[:narrow].T

    def without_gaps(grads):
        kinds = grads.shape[1] // heads_high
        return (
            grads[:narrow].T.reshape(kinds, GROUP, HP, narrow)[:, :, :HD]
            .reshape(kinds * GROUP * HD, narrow)
        )

    dattn_out, dattn_in = without_gaps(dattn_out), without_gaps(dattn_in)

    def totals(parts):
        flat = jnp.concatenate([part.reshape(-1) for part in parts])
        lines = -(-flat.shape[0] // 1024) * 8
        flat = jnp.pad(flat, (0, lines * 128 - flat.shape[0])).reshape(lines, 128)
        steps = len(doublings(reps)) + len(doublings(groups))
        [summed] = call(
            functools.partial(total_kernel, reps), 0, (flat,), [(flat.shape, F32)],
            [vm((steps, lines, 128), F32), *dma(steps)], limit=16,
        )
        summed = summed.reshape(-1)
        spot, outs = 0, []
        for part in parts:
            outs.append(summed[spot : spot + part.size].reshape(part.shape))
            spot += part.size
        return outs

    dbias = dbias.T.reshape(3, GROUP, HP)[:, :, :HD].reshape(3, GROUP * HD)
    dattn_bias = lax.dynamic_update_slice_in_dim(
        jnp.zeros((2, width), F32), dbias[0::2], member * GROUP * HD, 1
    )
    dup_bias = lax.dynamic_update_slice_in_dim(
        jnp.zeros(up_bias.shape, F32), dup[0], member * ff_rows, 0
    )
    dgain_one, dshift_one, dattn_bias, dout_bias, dgain_two, dshift_two, dup_bias, ddown_bias = (
        totals(
            (
                sums_one[0], sums_one[1], dattn_bias, sums_two[0], sums_two[1], sums_two[2],
                dup_bias, sums_two[3],
            )
        )
    )
    block_output = jnp.where(live_col, out[:capacity], jnp.zeros((), BF))
    input_grad = jnp.where(live_col, input_grad[:capacity], 0.0)
    return (
        block_output, input_grad, dgain_one, dshift_one, dattn_in, dattn_bias, dattn_out,
        dout_bias, dgain_two, dshift_two, dmlp_up, dup_bias, dmlp_down, ddown_bias,
    )


def solution(mesh):
    rows, rep_grp = P("grp", None), P(("rep", "grp"), None)
    in_specs = (
        rep_grp, rep_grp, P(), P(), P(), rows, P(), rows, P(), P(), P(), rows, P(), rows, P(),
    )
    grads = P("grp", "rep")
    out_specs = (
        rep_grp, rep_grp, P(), P(), grads, P(), grads, P(), P(), P(), grads, P(), grads, P(),
    )
    return jax.shard_map(
        per_device, mesh=mesh, in_specs=in_specs, out_specs=out_specs, check_vma=False
    )
```

```python
import functools

import jax
import jax.numpy as jnp
from jax import lax
from jax.experimental import pallas as pl
from jax.experimental.pallas import tpu as pltpu
from jax.sharding import PartitionSpec as P

H = 16
HD = 72
HP = 80
IMG = 729
GROUP = 4
NEAR_GROUPS = 2
WINDOW = (2 * NEAR_GROUPS + 1) * GROUP
OWN = NEAR_GROUPS * GROUP
OFFSETS = (1, -1, 2, -2)

EPSILON = 1e-06
SQRT_TWO_PI = 0.7978845608028654
CUBIC = 0.044715
FAR = -(2.0**80)
SCALE = HD ** (-0.5)
LOG2E = 1.4426950408889634
BF = jnp.bfloat16
F32 = jnp.float32
MESH = pl.DeviceIdType.MESH


def norm_parts(rows):
    centered = rows - jnp.mean(rows, axis=-1, keepdims=True)
    inverse = lax.rsqrt(jnp.mean(centered * centered, axis=-1, keepdims=True) + EPSILON)
    return centered * inverse, inverse


def norm_backward(dscaled, normed, inverse, gain_row):
    dnormed = dscaled * gain_row
    return inverse * (
        dnormed
        - jnp.mean(dnormed, axis=-1, keepdims=True)
        - normed * jnp.mean(dnormed * normed, axis=-1, keepdims=True)
    )


def gelu_parts(before):
    square = before * before
    tangent = jnp.tanh(SQRT_TWO_PI * before * (1.0 + CUBIC * square))
    half = 0.5 * (1.0 + tangent)
    derivative = half + 0.5 * before * (1.0 - tangent * tangent) * (
        SQRT_TWO_PI + SQRT_TWO_PI * 3.0 * CUBIC * square
    )
    return before * half, derivative


def dot_over(left, right, left_axis, right_axis):
    return lax.dot_general(
        left, right, (((left_axis,), (right_axis,)), ((), ())), preferred_element_type=F32
    )


def flipped(index, bit):
    return index + bit * (1 - 2 * ((index // bit) % 2))


def doublings(count):
    return [1 << i for i in range(count.bit_length() - 1)]


class Place:
    def __init__(self, capacity, reps, rows):
        self.capacity, self.reps, self.rows = capacity, reps, rows
        self.devices = reps * GROUP
        self.images = capacity * self.devices // IMG
        self.short = capacity * self.devices - self.images * IMG
        self.rep, self.member = lax.axis_index("rep"), lax.axis_index("grp")
        low = lax.rem(self.member, 2)
        self.near = self.member + 1 - 2 * low
        self.far = lax.rem(self.member + 2, GROUP)
        self.diagonal = lax.rem(self.near + 2, GROUP)
        self.pair = lax.div(self.member, 2)

    def sharing(self, low, high):
        capacity, short, image = self.capacity, self.short, jnp.int32(IMG)
        start = low * capacity - jnp.minimum(low, short)
        end = high * capacity - jnp.maximum(high - (self.devices - short), 0) - 1
        first = lax.div(start, image) * IMG
        after = (jnp.minimum(lax.div(end, image), self.images - 1) + 1) * IMG
        begin = lax.div(first, jnp.int32(capacity))
        stop = jnp.minimum(
            lax.div(after + short + capacity - 1, jnp.int32(capacity)),
            lax.div(after + capacity - 2, jnp.int32(capacity - 1)),
        )
        return begin, jnp.minimum(stop, self.devices)

    def slots(self, low, high):
        base = self.rep * GROUP
        begin, stop = self.sharing(base + low, base + high)
        return jnp.maximum(begin - base + OWN, 0), jnp.minimum(stop - base + OWN, WINDOW)

    def shares(self, block, group):
        begin, stop = self.sharing(group * GROUP, group * GROUP + GROUP)
        return (group >= 0) & (group < self.reps) & (block >= begin) & (block < stop)

    def block(self, owner):
        return pl.ds(pl.multiple_of(owner * self.rows, self.rows), self.rows)

    def pair_block(self, pair):
        return pl.ds(pl.multiple_of(pair * 2 * self.rows, 2 * self.rows), 2 * self.rows)

    def halving_barrier(self):
        barrier = pltpu.get_barrier_semaphore()
        bits = doublings(self.reps)
        for bit in bits:
            pl.semaphore_signal(
                barrier, inc=1, device_id=(flipped(self.rep, bit), self.member),
                device_id_type=MESH,
            )
        return len(bits)

    def group_barrier(self):
        barrier = pltpu.get_barrier_semaphore()
        for other in (self.near, self.far):
            pl.semaphore_signal(
                barrier, inc=1, device_id=(self.rep, other), device_id_type=MESH
            )
        return barrier, 2

    def wide_barrier(self):
        barrier, count = self.group_barrier()
        count = jnp.int32(count)
        for offset in OFFSETS:
            there = self.rep + offset
            valid = (there >= 0) & (there < self.reps)

            @pl.when(valid)
            def _():
                pl.semaphore_signal(
                    barrier, inc=1, device_id=(there, self.member), device_id_type=MESH
                )

            count = count + jnp.where(valid, 1, 0)
        return barrier, count


def remote(source, target, send, recv, place):
    return pltpu.make_async_remote_copy(
        src_ref=source,
        dst_ref=target,
        send_sem=send,
        recv_sem=recv,
        device_id=place,
        device_id_type=MESH,
    )


class Gather:
    def __init__(self, place, ref, rows, send, recv):
        self.place, self.ref, self.rows, self.send, self.recv = place, ref, rows, send, recv
        self.half = rows // 2

    def copy(self, owner, part, slot, target):
        if part is None:
            piece = self.ref.at[pl.ds(pl.multiple_of(owner * self.rows, self.rows), self.rows), :]
        else:
            start = pl.multiple_of(owner * self.rows + part * self.half, self.half)
            piece = self.ref.at[pl.ds(start, self.half), :]
        return remote(
            piece, piece, self.send.at[slot], self.recv.at[slot], (self.place.rep, target)
        )

    def start(self):
        p = self.place
        for part in range(2):
            self.copy(p.member, part, 1 + part, p.far).start()
        self.copy(p.member, None, 0, p.near).start()

    def wait_near(self):
        p = self.place
        self.copy(p.near, None, 0, p.near).wait_recv()

    def forward(self, part):
        p = self.place
        self.copy(p.far, part, 1 + part, p.far).wait_recv()
        self.copy(p.far, part, 3 + part, p.near).start()

    def wait_rest(self):
        p = self.place
        for part in range(2):
            self.copy(p.diagonal, part, 3 + part, p.near).wait_recv()

    def drain(self):
        p = self.place
        self.copy(p.member, None, 0, p.near).wait_send()
        for part in range(2):
            self.copy(p.member, part, 1 + part, p.far).wait_send()
            self.copy(p.far, part, 3 + part, p.near).wait_send()


class Scatter:
    def __init__(self, place, ref, held, rows, send, recv):
        self.place, self.ref, self.held = place, ref, held
        self.rows, self.send, self.recv = rows, send, recv

    def block(self, owner):
        return pl.ds(pl.multiple_of(owner * self.rows, self.rows), self.rows)

    def ahead(self):
        p = self.place
        return remote(
            self.ref.at[self.block(p.diagonal), :], self.held.at[0],
            self.send.at[0], self.recv.at[0], (p.rep, p.near),
        )

    def own(self):
        p = self.place
        return remote(
            self.ref.at[self.block(p.near), :], self.held.at[1],
            self.send.at[1], self.recv.at[1], (p.rep, p.near),
        )

    def across(self):
        p = self.place
        return remote(
            self.held.at[0], self.held.at[2], self.send.at[2], self.recv.at[2], (p.rep, p.far)
        )

    def pass_on(self):
        p = self.place
        self.ahead().wait_recv()
        self.held[0] = (
            self.ref[self.block(p.far), :].astype(F32) + self.held[0].astype(F32)
        ).astype(BF)
        self.across().start()

    def result(self):
        p = self.place
        self.own().wait_recv()
        total = self.ref[self.block(p.member), :].astype(F32) + self.held[1].astype(F32)
        self.across().wait_recv()
        total = total + self.held[2].astype(F32)
        self.ahead().wait_send()
        self.own().wait_send()
        self.across().wait_send()
        return total


class Exchange:
    def __init__(self, place, view, send, recv):
        self.place, self.view, self.send, self.recv = place, view, send, recv

    def outgoing(self, act):
        p = self.place
        for number, offset in enumerate(OFFSETS):
            begin, stop = p.sharing((p.rep + offset) * GROUP, (p.rep + offset + 1) * GROUP)
            valid = (p.rep + offset >= 0) & (p.rep + offset < p.reps)
            for index in range(GROUP):
                block = p.rep * GROUP + index
                slot_there = OWN - offset * GROUP + index

                @pl.when(valid & (block >= begin) & (block < stop))
                def _():
                    act(
                        remote(
                            self.view(OWN + index),
                            self.view(slot_there),
                            self.send.at[number * GROUP + index],
                            self.recv.at[slot_there],
                            (p.rep + offset, p.member),
                        )
                    )

    def start(self):
        self.outgoing(lambda copy: copy.start())

    def drain(self):
        self.outgoing(lambda copy: copy.wait_send())

    def wait(self):
        p = self.place
        begin, stop = p.slots(0, GROUP)
        for offset in OFFSETS:
            for index in range(GROUP):
                slot = OWN + offset * GROUP + index

                @pl.when((slot >= begin) & (slot < stop))
                def _():
                    remote(
                        self.view(slot), self.view(slot), self.send.at[0], self.recv.at[slot],
                        (p.rep, p.near),
                    ).wait_recv()


def dma(count):
    return [pltpu.SemaphoreType.DMA((count,))] * 2


class Halving:
    def __init__(self, place, levels, deep, bits, send, recv):
        self.place, self.levels, self.deep = place, levels, deep
        self.send, self.recv = send, recv
        self.bits = bits

    def mine(self, step):
        return lax.rem(lax.div(self.place.rep, jnp.int32(self.bits[step])), 2)

    def partner(self, step):
        p = self.place
        return (flipped(p.rep, self.bits[step]), p.member)

    def rows(self, start, count):
        return pl.ds(pl.multiple_of(start * self.deep, self.deep), count * self.deep)

    def firsts(self):
        rest = self.bits[1:]
        for j in range(self.place.reps // 2):
            yield j, sum(bit * ((j >> (len(rest) - 1 - q)) & 1) for q, bit in enumerate(rest))

    def copies(self, step):
        give = 1 - self.mine(step)
        source, target = self.levels[step], self.levels[step + 1]
        if step == 0:
            return [
                remote(
                    source.at[self.rows(give * self.bits[0] + offset, 1), :],
                    target.at[self.rows(j, 1), :],
                    self.send.at[j], self.recv.at[j], self.partner(0),
                )
                for j, offset in self.firsts()
            ]
        half = self.place.reps >> (step + 1)
        slot = self.place.reps // 2 + step - 1
        return [
            remote(
                source.at[self.rows(give * half, half), :], target.at[self.rows(0, half), :],
                self.send.at[slot], self.recv.at[slot], self.partner(step),
            )
        ]

    def start(self, step):
        for copy in self.copies(step):
            copy.start()

    def finish(self, step, out=None):
        copies = self.copies(step)
        mine = self.mine(step)
        source, target = self.levels[step], self.levels[step + 1]
        half = self.place.reps >> (step + 1)
        if step == 0:
            for j, offset in self.firsts():
                copies[j].wait_recv()
                at = self.rows(j, 1)
                kept = source[self.rows(mine * self.bits[0] + offset, 1), :]
                target[at, :] = (target[at, :].astype(F32) + kept.astype(F32)).astype(BF)
            return
        copies[0].wait_recv()
        for j in range(half):
            at = self.rows(j, 1)
            kept = source[self.rows(mine * half + j, 1), :]
            total = target[at, :].astype(F32) + kept.astype(F32)
            if out is None:
                target[at, :] = total.astype(BF)
            else:
                ref, lanes = out
                ref[:, lanes] = total

    def drain(self, step):
        for copy in self.copies(step):
            copy.wait_send()


def orders(reps):
    bits = doublings(reps)
    return bits, bits[1:2] + bits[:1] + bits[2:]


def split(wide):
    cut = -(-wide // 256) * 128
    return slice(0, cut), slice(cut, wide)


def halving_sems(reps):
    return dma(reps // 2 + reps.bit_length() - 2)


def halving_levels(reps, deep, wide, first):
    return [
        pltpu.VMEM(((reps >> s) * deep, lanes.stop - lanes.start), BF)
        for lanes in split(wide)
        for s in range(first, reps.bit_length())
    ]


def grad_chunks(left, right, right_axis, targets, deep, narrow):
    chunk = 128
    width = left.shape[1]

    def body(i, carry):
        at = pl.ds(pl.multiple_of(i * chunk, chunk), chunk)
        if deep == narrow:
            columns = left[:, at]
        else:
            source = lax.broadcasted_iota(jnp.int32, (width, chunk), 0)
            column = lax.broadcasted_iota(jnp.int32, (width, chunk), 1) + i * chunk
            within = column % deep
            picked = (source == (column // deep) * narrow + within) & (within < narrow)
            columns = dot_over(left[...], jnp.where(picked, 1.0, 0.0).astype(BF), 1, 0).astype(BF)
        product = dot_over(columns, right[...], 0, right_axis).astype(BF)
        for target, lanes in zip(targets, split(product.shape[1])):
            target[at, :] = product[:, lanes]
        return carry

    lax.fori_loop(0, targets[0].shape[0] // chunk, body, 0)


def image_codes(place, sizes_ref, kind):
    start = lax.fori_loop(0, place.rep * GROUP, lambda i, n: n + sizes_ref[i], jnp.int32(0))
    index = lax.broadcasted_iota(jnp.int32, (8, place.rows), 1)
    row = lax.broadcasted_iota(jnp.int32, (8, place.rows), 0)
    codes = []
    for b in range(GROUP):
        size = sizes_ref[place.rep * GROUP + b]
        base = lax.div(start, jnp.int32(IMG))
        turn = (base + 1) * IMG - start
        kind_of_image = lax.rem(base + jnp.where(index >= turn, 1, 0), 4)
        live = index < size
        same = kind_of_image == row
        query = jnp.where(same | ~live, 1.0, 0.0)
        key = jnp.where(same & live, 0.0, FAR)
        code = jnp.where(kind == 0, query, key)
        code = jnp.where(row < 4, code, 0.0)
        codes.append(jnp.where(kind == 2, jnp.where(row == 0, 1.0, 0.0), code))
        start = start + size
    return codes


def front_kernel(
    capacity, reps, rows, sizes_ref, tok_ref, cot_ref, gain_ref, shift_ref, w_ref, bias_ref,
    first_ref, own_ref, query_ref, win_ref, cotall_ref,
    xall, sbuf, code, gsend, grecv, csend, crecv, ssend, srecv, ksend, krecv, vsend, vrecv,
):
    p = Place(capacity, reps, rows)
    barrier, count = p.wide_barrier()
    size = sizes_ref[p.rep * GROUP + p.member]
    live = lax.broadcasted_iota(jnp.int32, (capacity, 1), 0) < size
    clean = lambda ref: jnp.where(live, ref[...].astype(F32), 0.0).astype(BF)
    own_ref[...] = jnp.zeros_like(own_ref)
    own_ref[pl.ds(0, capacity), :] = clean(tok_ref)
    xall[p.block(p.member), :] = own_ref[...]
    pl.semaphore_wait(barrier, count)
    tokens = Gather(p, xall, rows, gsend, grecv)
    tokens.start()
    cotall_ref[p.block(p.member), :] = jnp.zeros((rows, tok_ref.shape[1]), BF)
    cotall_ref[pl.ds(pl.multiple_of(p.member * rows, rows), capacity), :] = clean(cot_ref)
    gain, shift = gain_ref[...][None, :], shift_ref[...][None, :]

    def normalize(owner):
        block = p.block(owner)
        normed, _ = norm_parts(xall[block, :].astype(F32))
        first_ref[block, :] = (normed * gain + shift).astype(BF)

    odd = lax.rem(p.member, 2)
    cross = 2 - 2 * odd
    kept = 2 * odd
    kind_of = lambda i: lax.div(3 * p.member + i, GROUP)
    def spot_of(i):
        kind = kind_of(i)
        return jnp.where(kind == 0, 2 * WINDOW, (kind - 1) * WINDOW + OWN)

    gap = jnp.zeros((HD, rows), F32)
    for i in range(3):
        for b, rest in enumerate(image_codes(p, sizes_ref, kind_of(i))):
            at = slice(b * rows, (b + 1) * rows)
            for h in range(GROUP):
                code[i, h * HP : (h + 1) * HP, at] = jnp.concatenate([gap, rest], axis=0)

    def project(i, pair):
        block = first_ref[p.pair_block(pair), :]
        bias = bias_ref[pl.ds(3 * p.member + i, 1), :]
        bias = jnp.transpose(jnp.broadcast_to(bias, (8, bias.shape[1])))[:, 0:1]
        total = dot_over(w_ref[i], block, 1, 1) + bias + code[i, :, p.pair_block(pair)]
        for b in range(2):
            sbuf[i, pair * 2 + b] = total[:, b * rows : (b + 1) * rows].astype(BF)

    def shuffle(i, pair, way, target):
        slot = way * 2 + pair
        return remote(
            sbuf.at[i, pl.ds(pair * 2, 2)],
            win_ref.at[pl.ds(spot_of(i) + pair * 2, 2)],
            ssend.at[slot], srecv.at[slot], (p.rep, target),
        )

    normalize(p.member)
    tokens.wait_near()
    normalize(p.near)
    tokens.forward(0)
    project(cross, p.pair)
    shuffle(cross, p.pair, 0, p.far).start()
    tokens.forward(1)
    project(1, p.pair)
    shuffle(1, p.pair, 1, p.near).start()
    project(kept, p.pair)
    other = 1 - p.pair
    normalize(p.far)
    tokens.wait_rest()
    normalize(p.diagonal)
    project(cross, other)
    shuffle(cross, other, 0, p.far).start()
    project(1, other)
    shuffle(1, other, 1, p.near).start()
    project(kept, other)
    win_ref[pl.ds(spot_of(kept), GROUP)] = sbuf[kept]
    for pair in (p.pair, other):
        shuffle(cross, pair, 0, p.far).wait_recv()
        shuffle(1, pair, 1, p.near).wait_recv()
    keys = Exchange(p, lambda slot: win_ref.at[slot], ksend, krecv)
    values = Exchange(p, lambda slot: win_ref.at[WINDOW + slot], vsend, vrecv)
    keys.start()
    values.start()
    cotangents = Gather(p, cotall_ref, rows, csend, crecv)
    cotangents.start()
    query_ref[...] = win_ref[pl.ds(2 * WINDOW, GROUP)]
    cotangents.wait_near()
    cotangents.forward(0)
    cotangents.forward(1)
    cotangents.wait_rest()
    keys.wait()
    values.wait()
    keys.drain()
    values.drain()
    for pair in (p.pair, other):
        shuffle(cross, pair, 0, p.far).wait_send()
        shuffle(1, pair, 1, p.near).wait_send()
    tokens.drain()
    cotangents.drain()


def joined(view, head, blocks):
    return jnp.concatenate([view(b)[head, :] for b in blocks], axis=1)


def pieces(rows):
    count = max(512 // rows, 1)
    for low in range(0, GROUP, count):
        yield range(low, low + count), slice(low * rows, (low + count) * rows)


def attend_kernel(capacity, reps, rows, sizes_ref, query_ref, win_ref, mixed_ref, lse_ref, acc):
    p = Place(capacity, reps, rows)
    heads = [slice(h * HP, (h + 1) * HP) for h in range(GROUP)]
    for blocks, at in pieces(rows):
        begin, stop = p.slots(blocks[0], blocks[-1] + 1)
        acc[:, at] = jnp.zeros((acc.shape[0], at.stop - at.start), F32)
        queries = [joined(lambda b: query_ref.at[b], head, blocks) for head in heads]

        def attend(slot, tops):
            raws = [dot_over(win_ref[slot, head, :], query, 0, 0) for head, query in zip(heads, queries)]
            news = [
                jnp.maximum(top, jnp.max(raw, axis=0, keepdims=True) * (SCALE * LOG2E))
                for top, raw in zip(tops, raws)
            ]
            powers = [
                jnp.exp2(raw * (SCALE * LOG2E) - new).astype(BF) for raw, new in zip(raws, news)
            ]
            for head, top, new, power in zip(heads, tops, news, powers):
                value = win_ref[WINDOW + slot, head, :]
                acc[head, at] = acc[head, at] * jnp.exp2(top - new) + dot_over(value, power, 1, 0)
            return tuple(news)

        tops = lax.fori_loop(
            begin, stop, attend, tuple(jnp.full((1, at.stop - at.start), 4.0 * FAR, F32) for _ in heads)
        )
        index = lax.broadcasted_iota(jnp.int32, (1, rows), 1)
        live = jnp.concatenate(
            [
                jnp.where(index < sizes_ref[p.rep * GROUP + b], 1.0, 0.0) for b in blocks
            ],
            axis=1,
        )
        for h, head in enumerate(heads):
            whole = acc[h * HP + HD : h * HP + HD + 1, at]
            mixed_ref[head, at] = (acc[head, at] / whole).astype(BF)
            lse_ref[h : h + 1, at] = jnp.where(live > 0.0, tops[h] + jnp.log(whole) * LOG2E, 0.0)


def middle_kernel(
    capacity, reps, rows, deep, tok_ref, cot_ref, query_ref, mixed_ref, lse_ref, wo_ref, wup_ref,
    wdn_ref, upb_ref, outb_ref, gain_ref, shift_ref, downb_ref,
    out_ref, dres_ref, dmix_ref, stats_ref, qwin_ref, up_a, up_b, down_a, down_b, wo_a, wo_b,
    sums_ref, dupb_ref,
    part, part2, second, hidden, dbefore, dresall, dact, dwdn_a, dwdn_b, res_scr, norm_scr, held,
    asend, arecv, bsend, brecv, csend, crecv, dsend, drecv, esend, erecv, qsend, qrecv,
    hsend, hrecv, isend, irecv,
):
    p = Place(capacity, reps, rows)
    barrier, count = p.wide_barrier()
    count = count + p.halving_barrier()
    out_bias, gain, shift, down_bias = (
        ref[...][None, :] for ref in (outb_ref, gain_ref, shift_ref, downb_ref)
    )
    other = 1 - p.pair
    narrow = cot_ref.shape[1] // reps

    def attn_partial(owner):
        part[p.block(owner), :] = dot_over(
            mixed_ref[:, p.block(owner)], wo_ref[...], 0, 0
        ).astype(BF)

    attn_partial(p.diagonal)
    pl.semaphore_wait(barrier, count)
    one = Scatter(p, part, held.at[0], rows, asend, arecv)
    one.ahead().start()
    attn_partial(p.near)
    one.own().start()
    qwin_ref[pl.ds(OWN, GROUP)] = query_ref[...]
    queries = Exchange(p, lambda slot: qwin_ref.at[slot], qsend, qrecv)
    queries.start()
    attn_partial(p.far)
    one.pass_on()
    attn_partial(p.member)
    for pair in (0, 1):
        at = pl.ds(pair * 2 * rows, 2 * rows)
        dact[at, :] = dot_over(cot_ref[at, :], wdn_ref[...], 1, 1)
    resid = tok_ref[...].astype(F32) + one.result() + out_bias
    res_scr[...] = resid
    normed, inverse = norm_parts(resid)
    norm_scr[...] = normed
    second[p.block(p.member), :] = (normed * gain + shift).astype(BF)
    gather = Gather(p, second, rows, bsend, brecv)
    gather.start()

    def mlp(pair):
        at = p.pair_block(pair)
        before = dot_over(second[at, :], wup_ref[...], 1, 1) + upb_ref[pl.ds(p.member, 1), :]
        activated, derivative = gelu_parts(before)
        hidden[at, :] = activated.astype(BF)
        grad = dact[at, :] * derivative
        dact[at, :] = grad
        dbefore[at, :] = grad.astype(BF)
        part2[at, :] = dot_over(dbefore[at, :], wup_ref[...], 1, 0).astype(BF)

    gather.wait_near()
    gather.forward(0)
    mlp(p.pair)
    gather.forward(1)
    two = Scatter(p, part2, held.at[1], rows, csend, crecv)
    two.own().start()
    gather.wait_rest()
    mlp(other)
    two.ahead().start()
    grad_chunks(cot_ref, hidden, 0, (dwdn_a, dwdn_b), deep, narrow)
    order_a, order_b = orders(reps)
    halvings = (
        Halving(p, [dwdn_a, down_a], deep, order_a, hsend, hrecv),
        Halving(p, [dwdn_b, down_b], deep, order_b, isend, irecv),
    )
    for halving in halvings:
        halving.start(0)
    two.pass_on()

    def down(pair):
        at = p.pair_block(pair)
        part[at, :] = dot_over(hidden[at, :], wdn_ref[...], 1, 0).astype(BF)

    down(other)
    down(p.pair)
    three = Scatter(p, part, held.at[2], rows, esend, erecv)
    three.ahead().start()
    three.own().start()
    dsecond = two.result()
    own_cot = cot_ref[p.block(p.member), :].astype(F32)
    normed = norm_scr[...]
    dresid = own_cot + norm_backward(dsecond, normed, inverse, gain)
    dres_ref[...] = dresid
    dresall[p.block(p.member), :] = dresid.astype(BF)
    again = Gather(p, dresall, rows, dsend, drecv)
    again.start()
    three.pass_on()
    dupb_ref[...] = jnp.sum(dact[...], axis=0, keepdims=True)
    for i, term in enumerate((dresid, dsecond * normed, dsecond, own_cot)):
        sums_ref[pl.ds(i, 1), :] = jnp.sum(term, axis=0, keepdims=True)
    again.wait_near()
    again.forward(0)

    def mixed_grad(pair):
        at = p.pair_block(pair)
        dmixed = dot_over(wo_ref[...], dresall[at, :], 1, 1).astype(BF)
        dmix_ref[:, at] = dmixed
        product = dmixed.astype(F32) * mixed_ref[:, at].astype(F32)
        stats_ref[pl.ds(0, GROUP), at] = lse_ref[:, at]
        for h in range(GROUP):
            stats_ref[pl.ds(GROUP + h, 1), at] = jnp.sum(
                product[h * HP : (h + 1) * HP], axis=0, keepdims=True
            )

    grad_chunks(second, dbefore, 0, (up_a, up_b), deep, narrow)
    mixed_grad(p.pair)
    again.forward(1)
    again.wait_rest()
    mixed_grad(other)
    grad_chunks(dresall, mixed_ref, 1, (wo_a, wo_b), deep, narrow)
    out_ref[...] = (res_scr[...] + three.result() + down_bias).astype(BF)
    queries.wait()
    queries.drain()
    for halving in halvings:
        halving.finish(0)
        halving.drain(0)
    gather.drain()
    again.drain()


def back_kernel(
    capacity, reps, rows, deep, win_ref, qwin_ref, dmix_ref, stats_ref, first_ref, w_ref, tok_ref,
    dres_ref, gain_ref, up_a, up_b, down_a, down_b, wo_a, wo_b,
    grad_ref, dbias_ref, sums_ref, dup_out, ddn_out, dwo_out, dwi_out,
    dwin, swin, dq, dv, sbuf, dproj, part, held, *rest,
):
    steps = reps.bit_length() - 1
    scratch = list(rest)
    take = lambda n: [scratch.pop(0) for _ in range(n)]
    up_levels = [[ref] + take(steps) for ref in (up_a, up_b)]
    dn_levels = [[None, ref] + take(steps - 1) for ref in (down_a, down_b)]
    wo_levels = [[ref] + take(steps) for ref in (wo_a, wo_b)]
    wi_levels = [take(steps + 1) for _ in range(2)]
    (ksend, krecv, tsend, trecv, ssend, srecv, rsend, rrecv) = take(8)
    p = Place(capacity, reps, rows)
    barrier, count = p.wide_barrier()
    count = count + p.halving_barrier()
    for b in range(GROUP):
        at = slice(b * rows, (b + 1) * rows)
        dwin[OWN + b] = dmix_ref[:, at]
        swin[OWN + b] = stats_ref[:, at]
    pl.semaphore_wait(barrier, count)
    grads_in = Exchange(p, lambda slot: dwin.at[slot], ksend, krecv)
    stats_in = Exchange(p, lambda slot: swin.at[slot], tsend, trecv)
    grads_in.start()
    stats_in.start()
    down, up, inner, outer = (
        [Halving(p, refs, deep, order, *take(2)) for refs, order in zip(levels, orders(reps))]
        for levels in (dn_levels, up_levels, wi_levels, wo_levels)
    )
    work = [
        [one, first, (out, lanes)]
        for pair, first, out in (
            (down, 1, ddn_out), (up, 0, dup_out), (outer, 0, dwo_out), (inner, 0, dwi_out)
        )
        for one, lanes in zip(pair, split(out.shape[1]))
    ]

    def advance(some):
        for item in some:
            one, step, out = item
            if step < steps:
                one.finish(step, out if step == steps - 1 else None)
                if step + 1 < steps:
                    one.start(step + 1)
                item[1] = step + 1

    for one, step, _ in work[:6]:
        one.start(step)
    heads = [slice(h * HP, (h + 1) * HP) for h in range(GROUP)]
    every = range(GROUP)
    for blocks, at in pieces(rows):
        begin, stop = p.slots(blocks[0], blocks[-1] + 1)
        queries = [joined(lambda b: qwin_ref.at[OWN + b], head, blocks) for head in heads]
        dq[:, at] = jnp.zeros((dq.shape[0], at.stop - at.start), F32)

        def query_grads(slot, carry):
            keys = [win_ref[slot, head, :] for head in heads]
            raws = [dot_over(keys[h], queries[h], 0, 0) for h in every]
            dprobs = [
                dot_over(win_ref[WINDOW + slot, head, :], dmix_ref[head, at], 0, 0) for head in heads
            ]
            dscores = [
                (
                    jnp.exp2(raws[h] * (SCALE * LOG2E) - stats_ref[h : h + 1, at])
                    * (dprobs[h] - stats_ref[GROUP + h : GROUP + h + 1, at])
                ).astype(BF)
                for h in every
            ]
            for h, head in enumerate(heads):
                dq[head, at] += dot_over(keys[h], dscores[h], 1, 0)
            return carry

        lax.fori_loop(begin, stop, query_grads, 0)

    def owner_of(kind):
        c = kind * GROUP + p.member
        return lax.div(c, 3), lax.rem(c, 3)

    high = GROUP * HP

    def part_of(index):
        return pl.ds(pl.multiple_of(index * high, high), high)

    def home(kind):
        owner, index = owner_of(kind)
        return owner, remote(
            sbuf.at[kind], dproj.at[part_of(index), :], ssend.at[kind], srecv.at[index],
            (p.rep, owner),
        )

    def send_home(kind, grads, scale):
        value = grads[...] * scale
        sbuf[kind] = value.astype(BF)
        dbias_ref[:, kind : kind + 1] = jnp.sum(value, axis=1, keepdims=True)
        owner, copy = home(kind)

        @pl.when(owner != p.member)
        def _():
            copy.start()

    send_home(0, dq, SCALE)
    dk = dq
    grads_in.wait()
    stats_in.wait()
    for blocks, at in pieces(rows):
        begin, stop = p.slots(blocks[0], blocks[-1] + 1)
        keys = [joined(lambda b: win_ref.at[OWN + b], head, blocks) for head in heads]
        values = [joined(lambda b: win_ref.at[WINDOW + OWN + b], head, blocks) for head in heads]
        dk[:, at] = jnp.zeros((dk.shape[0], at.stop - at.start), F32)
        dv[:, at] = jnp.zeros((dv.shape[0], at.stop - at.start), F32)

        def key_grads(slot, carry):
            stats = jnp.transpose(swin[slot])
            picked = [qwin_ref[slot, head, :] for head in heads]
            dmixed = [dwin[slot, head, :] for head in heads]
            raws = [dot_over(picked[h], keys[h], 0, 0) for h in every]
            dprobs = [dot_over(dmixed[h], values[h], 0, 0) for h in every]
            probs = [jnp.exp2(raws[h] * (SCALE * LOG2E) - stats[:, h : h + 1]) for h in every]
            dscores = [
                (probs[h] * (dprobs[h] - stats[:, GROUP + h : GROUP + h + 1])).astype(BF)
                for h in every
            ]
            for h, head in enumerate(heads):
                dk[head, at] += dot_over(picked[h], dscores[h], 1, 0)
            for h, head in enumerate(heads):
                dv[head, at] += dot_over(dmixed[h], probs[h].astype(BF), 1, 0)
            return carry

        lax.fori_loop(begin, stop, key_grads, 0)

    send_home(1, dk, SCALE)
    send_home(2, dv, 1.0)
    for kind in range(3):
        owner, index = owner_of(kind)

        @pl.when(owner == p.member)
        def _():
            dproj[part_of(index), :] = sbuf[kind]

    advance(work[:4])
    for index in range(3):
        source = lax.rem(3 * p.member + index, GROUP)

        @pl.when(source != p.member)
        def _():
            remote(
                sbuf.at[0], dproj.at[part_of(index), :], ssend.at[0], srecv.at[index],
                (p.rep, p.near),
            ).wait_recv()

    narrow = first_ref.shape[1] // reps
    grad_chunks(first_ref, dproj, 1, [levels[0] for levels in wi_levels], deep, narrow)
    for one, step, _ in work[6:]:
        one.start(step)

    def partial(owner):
        part[p.block(owner), :] = dot_over(dproj[:, p.block(owner)], w_ref[...], 0, 0).astype(BF)

    scatter = Scatter(p, part, held, rows, rsend, rrecv)
    partial(p.diagonal)
    scatter.ahead().start()
    partial(p.near)
    scatter.own().start()
    partial(p.far)
    scatter.pass_on()
    partial(p.member)
    advance(work[:6])
    normed, inverse = norm_parts(tok_ref[...].astype(F32))
    dfirst = scatter.result()
    for i, term in enumerate((dfirst * normed, dfirst)):
        sums_ref[pl.ds(i, 1), :] = jnp.sum(term, axis=0, keepdims=True)
    grad_ref[...] = dres_ref[...] + norm_backward(dfirst, normed, inverse, gain_ref[...][None, :])
    for _ in range(steps):
        advance(work)
    for kind in range(3):
        owner, copy = home(kind)

        @pl.when(owner != p.member)
        def _():
            copy.wait_send()

    grads_in.drain()
    stats_in.drain()
    for pair, begin in ((down, 1), (up, 0), (inner, 0), (outer, 0)):
        for one in pair:
            for step in range(begin, steps):
                one.drain(step)


def total_kernel(reps, x_ref, o_ref, held, send, recv):
    rep, member = lax.axis_index("rep"), lax.axis_index("grp")
    places = [(rep, flipped(member, bit)) for bit in doublings(GROUP)]
    places += [(flipped(rep, bit), member) for bit in doublings(reps)]
    barrier = pltpu.get_barrier_semaphore()
    for place in places:
        pl.semaphore_signal(barrier, inc=1, device_id=place, device_id_type=MESH)
    pl.semaphore_wait(barrier, len(places))
    o_ref[...] = x_ref[...]
    for slot, place in enumerate(places):
        copy = remote(o_ref, held.at[slot], send.at[slot], recv.at[slot], place)
        copy.start()
        copy.wait()
        o_ref[...] += held[slot]


def call(kernel, number, args, outs, scratch, smem=0, limit=63):
    vmem = pl.BlockSpec(memory_space=pltpu.VMEM)
    smem_spec = pl.BlockSpec(memory_space=pltpu.SMEM)
    linked = {} if number is None else {"collective_id": number, "has_side_effects": True}
    return pl.pallas_call(
        kernel,
        out_shape=[jax.ShapeDtypeStruct(*o) for o in outs],
        in_specs=[smem_spec] * smem + [vmem] * (len(args) - smem),
        out_specs=[vmem] * len(outs),
        scratch_shapes=scratch,
        compiler_params=pltpu.CompilerParams(vmem_limit_bytes=limit * 2**20, **linked),
    )(*args)


def per_device(
    tokens,
    cotangent,
    slice_sizes,
    gain_one,
    shift_one,
    attn_in,
    attn_bias,
    attn_out,
    out_bias,
    gain_two,
    shift_two,
    mlp_up,
    up_bias,
    mlp_down,
    down_bias,
):
    capacity, width = tokens.shape
    reps, groups = lax.axis_size("rep"), lax.axis_size("grp")
    assert groups == GROUP
    rows = -(-capacity // 128) * 128
    all_rows = GROUP * rows
    rep, member = lax.axis_index("rep"), lax.axis_index("grp")
    device = rep * groups + member
    ff_rows = mlp_up.shape[0]
    heads_high = GROUP * HP
    devices = reps * groups
    vm = pltpu.VMEM

    deep = -(-(width // reps) // 16) * 16
    own_count = slice_sizes[device]
    live_col = (jnp.arange(capacity, dtype=jnp.int32) < own_count)[:, None]
    w_in = jnp.pad(
        attn_in.reshape(3, GROUP, HD, width), ((0, 0), (0, 0), (0, HP - HD), (0, 0))
    ).reshape(3, heads_high, width)
    bias = jnp.stack([attn_bias[0], jnp.zeros((width,), F32), attn_bias[1]])
    bias = jnp.pad(
        bias.reshape(3 * GROUP, GROUP, HD), ((0, 0), (0, 0), (0, HP - HD))
    ).reshape(3 * GROUP, heads_high)
    w_out = jnp.pad(
        attn_out.reshape(GROUP, HD, width), ((0, 0), (0, HP - HD), (0, 0))
    ).reshape(heads_high, width)
    place = (capacity, reps, rows)
    window_sems = [
        pltpu.SemaphoreType.DMA((len(OFFSETS) * GROUP,)), pltpu.SemaphoreType.DMA((WINDOW,))
    ]

    first, tok, query, window, cot_all = call(
        functools.partial(front_kernel, *place), 1,
        (slice_sizes, tokens, cotangent, gain_one, shift_one, w_in, bias),
        [((all_rows, width), BF), ((rows, width), BF), ((GROUP, heads_high, rows), BF),
         ((2 * WINDOW + GROUP, heads_high, rows), BF), ((all_rows, width), BF)],
        [vm((all_rows, width), BF), vm((3, GROUP, heads_high, rows), BF),
         vm((3, heads_high, all_rows), F32), *dma(5), *dma(5), *dma(4), *window_sems * 2],
        smem=1,
    )
    mixed, lse = call(
        functools.partial(attend_kernel, *place), None, (slice_sizes, query, window),
        [((heads_high, all_rows), BF), ((GROUP, all_rows), F32)],
        [vm((heads_high, all_rows), F32)],
        smem=1,
    )
    gapped = reps * deep

    def halves(high, wide):
        return [((high, lanes.stop - lanes.start), BF) for lanes in split(wide)]

    out, dresid, dmixed, stats, qwindow, *partials, sums_two, dup = call(
        functools.partial(middle_kernel, *place, deep), 2,
        (tok, cot_all, query, mixed, lse, w_out, mlp_up, mlp_down,
         up_bias.reshape(GROUP, ff_rows), out_bias, gain_two, shift_two, down_bias),
        [((rows, width), BF), ((rows, width), F32), ((heads_high, all_rows), BF),
         ((2 * GROUP, all_rows), F32), ((WINDOW, heads_high, rows), BF), *halves(gapped, ff_rows),
         *halves(gapped // 2, ff_rows), *halves(gapped, heads_high), ((4, width), F32),
         ((1, ff_rows), F32)],
        [vm((all_rows, width), BF)] * 3
        + [vm((all_rows, ff_rows), BF)] * 2
        + [vm((all_rows, width), BF), vm((all_rows, ff_rows), F32), *[vm(*o) for o in halves(gapped, ff_rows)],
           vm((rows, width), F32), vm((rows, width), F32), vm((3, 3, rows, width), BF)]
        + dma(3) + dma(5) + dma(3) + dma(5) + dma(3) + window_sems + halving_sems(reps) * 2,
    )
    input_grad, dbias, sums_one, dmlp_up, dmlp_down, dattn_out, dattn_in = call(
        functools.partial(back_kernel, *place, deep), 3,
        (window, qwindow, dmixed, stats, first, w_in.reshape(3 * heads_high, width), tok, dresid,
         gain_one, *partials),
        [((rows, width), F32), ((heads_high, 3), F32), ((2, width), F32),
         ((deep, ff_rows), F32), ((deep, ff_rows), F32), ((deep, heads_high), F32),
         ((deep, 3 * heads_high), F32)],
        [vm((WINDOW, heads_high, rows), BF), vm((WINDOW, 2 * GROUP, rows), F32)]
        + [vm((heads_high, all_rows), F32)] * 2
        + [vm((3, heads_high, all_rows), BF), vm((3 * heads_high, all_rows), BF)]
        + [vm((all_rows, width), BF), vm((3, rows, width), BF)]
        + halving_levels(reps, deep, ff_rows, 1) + halving_levels(reps, deep, ff_rows, 2)
        + halving_levels(reps, deep, heads_high, 1)
        + halving_levels(reps, deep, 3 * heads_high, 0)
        + window_sems * 2 + dma(3) + dma(3) + halving_sems(reps) * 8,
    )
    narrow = width // reps
    dmlp_up, dmlp_down = dmlp_up[:narrow].T, dmlp_down[:narrow].T

    def without_gaps(grads):
        kinds = grads.shape[1] // heads_high
        return (
            grads[:narrow].T.reshape(kinds, GROUP, HP, narrow)[:, :, :HD]
            .reshape(kinds * GROUP * HD, narrow)
        )

    dattn_out, dattn_in = without_gaps(dattn_out), without_gaps(dattn_in)

    def totals(parts):
        flat = jnp.concatenate([part.reshape(-1) for part in parts])
        lines = -(-flat.shape[0] // 1024) * 8
        flat = jnp.pad(flat, (0, lines * 128 - flat.shape[0])).reshape(lines, 128)
        steps = len(doublings(reps)) + len(doublings(groups))
        [summed] = call(
            functools.partial(total_kernel, reps), 0, (flat,), [(flat.shape, F32)],
            [vm((steps, lines, 128), F32), *dma(steps)], limit=16,
        )
        summed = summed.reshape(-1)
        spot, outs = 0, []
        for part in parts:
            outs.append(summed[spot : spot + part.size].reshape(part.shape))
            spot += part.size
        return outs

    dbias = dbias.T.reshape(3, GROUP, HP)[:, :, :HD].reshape(3, GROUP * HD)
    dattn_bias = lax.dynamic_update_slice_in_dim(
        jnp.zeros((2, width), F32), dbias[0::2], member * GROUP * HD, 1
    )
    dup_bias = lax.dynamic_update_slice_in_dim(
        jnp.zeros(up_bias.shape, F32), dup[0], member * ff_rows, 0
    )
    dgain_one, dshift_one, dattn_bias, dout_bias, dgain_two, dshift_two, dup_bias, ddown_bias = (
        totals(
            (
                sums_one[0], sums_one[1], dattn_bias, sums_two[0], sums_two[1], sums_two[2],
                dup_bias, sums_two[3],
            )
        )
    )
    block_output = jnp.where(live_col, out[:capacity], jnp.zeros((), BF))
    input_grad = jnp.where(live_col, input_grad[:capacity], 0.0)
    return (
        block_output, input_grad, dgain_one, dshift_one, dattn_in, dattn_bias, dattn_out,
        dout_bias, dgain_two, dshift_two, dmlp_up, dup_bias, dmlp_down, ddown_bias,
    )


def solution(mesh):
    rows, rep_grp = P("grp", None), P(("rep", "grp"), None)
    in_specs = (
        rep_grp, rep_grp, P(), P(), P(), rows, P(), rows, P(), P(), P(), rows, P(), rows, P(),
    )
    grads = P("grp", "rep")
    out_specs = (
        rep_grp, rep_grp, P(), P(), grads, P(), grads, P(), P(), P(), grads, P(), grads, P(),
    )
    return jax.shard_map(
        per_device, mesh=mesh, in_specs=in_specs, out_specs=out_specs, check_vma=False
    )
```

```python
import functools

import jax
import jax.numpy as jnp
from jax import lax
from jax.experimental import pallas as pl
from jax.experimental.pallas import tpu as pltpu
from jax.sharding import PartitionSpec as P

H = 16
HD = 72
HP = 80
IMG = 729
GROUP = 4
NEAR_GROUPS = 2
WINDOW = (2 * NEAR_GROUPS + 1) * GROUP
OWN = NEAR_GROUPS * GROUP
OFFSETS = (1, -1, 2, -2)

EPSILON = 1e-06
SQRT_TWO_PI = 0.7978845608028654
CUBIC = 0.044715
FAR = -(2.0**80)
SCALE = HD ** (-0.5)
LOG2E = 1.4426950408889634
BF = jnp.bfloat16
F32 = jnp.float32
MESH = pl.DeviceIdType.MESH


def norm_parts(rows):
    centered = rows - jnp.mean(rows, axis=-1, keepdims=True)
    inverse = lax.rsqrt(jnp.mean(centered * centered, axis=-1, keepdims=True) + EPSILON)
    return centered * inverse, inverse


def norm_backward(dscaled, normed, inverse, gain_row):
    dnormed = dscaled * gain_row
    return inverse * (
        dnormed
        - jnp.mean(dnormed, axis=-1, keepdims=True)
        - normed * jnp.mean(dnormed * normed, axis=-1, keepdims=True)
    )


def gelu_parts(before):
    square = before * before
    tangent = jnp.tanh(SQRT_TWO_PI * before * (1.0 + CUBIC * square))
    half = 0.5 * (1.0 + tangent)
    derivative = half + 0.5 * before * (1.0 - tangent * tangent) * (
        SQRT_TWO_PI + SQRT_TWO_PI * 3.0 * CUBIC * square
    )
    return before * half, derivative


def dot_over(left, right, left_axis, right_axis):
    return lax.dot_general(
        left, right, (((left_axis,), (right_axis,)), ((), ())), preferred_element_type=F32
    )


def flipped(index, bit):
    return index + bit * (1 - 2 * ((index // bit) % 2))


def doublings(count):
    return [1 << i for i in range(count.bit_length() - 1)]


class Place:
    def __init__(self, capacity, reps, rows):
        self.capacity, self.reps, self.rows = capacity, reps, rows
        self.devices = reps * GROUP
        self.images = capacity * self.devices // IMG
        self.short = capacity * self.devices - self.images * IMG
        self.rep, self.member = lax.axis_index("rep"), lax.axis_index("grp")
        low = lax.rem(self.member, 2)
        self.near = self.member + 1 - 2 * low
        self.far = lax.rem(self.member + 2, GROUP)
        self.diagonal = lax.rem(self.near + 2, GROUP)
        self.pair = lax.div(self.member, 2)

    def sharing(self, low, high):
        capacity, short, image = self.capacity, self.short, jnp.int32(IMG)
        start = low * capacity - jnp.minimum(low, short)
        end = high * capacity - jnp.maximum(high - (self.devices - short), 0) - 1
        first = lax.div(start, image) * IMG
        after = (jnp.minimum(lax.div(end, image), self.images - 1) + 1) * IMG
        begin = lax.div(first, jnp.int32(capacity))
        stop = jnp.minimum(
            lax.div(after + short + capacity - 1, jnp.int32(capacity)),
            lax.div(after + capacity - 2, jnp.int32(capacity - 1)),
        )
        return begin, jnp.minimum(stop, self.devices)

    def slots(self, low, high):
        base = self.rep * GROUP
        begin, stop = self.sharing(base + low, base + high)
        return jnp.maximum(begin - base + OWN, 0), jnp.minimum(stop - base + OWN, WINDOW)

    def shares(self, block, group):
        begin, stop = self.sharing(group * GROUP, group * GROUP + GROUP)
        return (group >= 0) & (group < self.reps) & (block >= begin) & (block < stop)

    def block(self, owner):
        return pl.ds(pl.multiple_of(owner * self.rows, self.rows), self.rows)

    def pair_block(self, pair):
        return pl.ds(pl.multiple_of(pair * 2 * self.rows, 2 * self.rows), 2 * self.rows)

    def halving_barrier(self):
        barrier = pltpu.get_barrier_semaphore()
        bits = doublings(self.reps)
        for bit in bits:
            pl.semaphore_signal(
                barrier, inc=1, device_id=(flipped(self.rep, bit), self.member),
                device_id_type=MESH,
            )
        return len(bits)

    def group_barrier(self):
        barrier = pltpu.get_barrier_semaphore()
        for other in (self.near, self.far):
            pl.semaphore_signal(
                barrier, inc=1, device_id=(self.rep, other), device_id_type=MESH
            )
        return barrier, 2

    def wide_barrier(self):
        barrier, count = self.group_barrier()
        count = jnp.int32(count)
        for offset in OFFSETS:
            there = self.rep + offset
            valid = (there >= 0) & (there < self.reps)

            @pl.when(valid)
            def _():
                pl.semaphore_signal(
                    barrier, inc=1, device_id=(there, self.member), device_id_type=MESH
                )

            count = count + jnp.where(valid, 1, 0)
        return barrier, count


def remote(source, target, send, recv, place):
    return pltpu.make_async_remote_copy(
        src_ref=source,
        dst_ref=target,
        send_sem=send,
        recv_sem=recv,
        device_id=place,
        device_id_type=MESH,
    )


class Gather:
    def __init__(self, place, ref, rows, send, recv):
        self.place, self.ref, self.rows, self.send, self.recv = place, ref, rows, send, recv
        self.half = rows // 2

    def copy(self, owner, part, slot, target):
        if part is None:
            piece = self.ref.at[pl.ds(pl.multiple_of(owner * self.rows, self.rows), self.rows), :]
        else:
            start = pl.multiple_of(owner * self.rows + part * self.half, self.half)
            piece = self.ref.at[pl.ds(start, self.half), :]
        return remote(
            piece, piece, self.send.at[slot], self.recv.at[slot], (self.place.rep, target)
        )

    def start(self):
        p = self.place
        for part in range(2):
            self.copy(p.member, part, 1 + part, p.far).start()
        self.copy(p.member, None, 0, p.near).start()

    def wait_near(self):
        p = self.place
        self.copy(p.near, None, 0, p.near).wait_recv()

    def forward(self, part):
        p = self.place
        self.copy(p.far, part, 1 + part, p.far).wait_recv()
        self.copy(p.far, part, 3 + part, p.near).start()

    def wait_rest(self):
        p = self.place
        for part in range(2):
            self.copy(p.diagonal, part, 3 + part, p.near).wait_recv()

    def drain(self):
        p = self.place
        self.copy(p.member, None, 0, p.near).wait_send()
        for part in range(2):
            self.copy(p.member, part, 1 + part, p.far).wait_send()
            self.copy(p.far, part, 3 + part, p.near).wait_send()


class Scatter:
    def __init__(self, place, ref, held, rows, send, recv):
        self.place, self.ref, self.held = place, ref, held
        self.rows, self.send, self.recv = rows, send, recv

    def block(self, owner):
        return pl.ds(pl.multiple_of(owner * self.rows, self.rows), self.rows)

    def ahead(self):
        p = self.place
        return remote(
            self.ref.at[self.block(p.diagonal), :], self.held.at[0],
            self.send.at[0], self.recv.at[0], (p.rep, p.near),
        )

    def own(self):
        p = self.place
        return remote(
            self.ref.at[self.block(p.near), :], self.held.at[1],
            self.send.at[1], self.recv.at[1], (p.rep, p.near),
        )

    def across(self):
        p = self.place
        return remote(
            self.held.at[0], self.held.at[2], self.send.at[2], self.recv.at[2], (p.rep, p.far)
        )

    def pass_on(self):
        p = self.place
        self.ahead().wait_recv()
        self.held[0] = (
            self.ref[self.block(p.far), :].astype(F32) + self.held[0].astype(F32)
        ).astype(BF)
        self.across().start()

    def result(self):
        p = self.place
        self.own().wait_recv()
        total = self.ref[self.block(p.member), :].astype(F32) + self.held[1].astype(F32)
        self.across().wait_recv()
        total = total + self.held[2].astype(F32)
        self.ahead().wait_send()
        self.own().wait_send()
        self.across().wait_send()
        return total


class Exchange:
    def __init__(self, place, view, send, recv):
        self.place, self.view, self.send, self.recv = place, view, send, recv

    def outgoing(self, act):
        p = self.place
        for number, offset in enumerate(OFFSETS):
            begin, stop = p.sharing((p.rep + offset) * GROUP, (p.rep + offset + 1) * GROUP)
            valid = (p.rep + offset >= 0) & (p.rep + offset < p.reps)
            for index in range(GROUP):
                block = p.rep * GROUP + index
                slot_there = OWN - offset * GROUP + index

                @pl.when(valid & (block >= begin) & (block < stop))
                def _():
                    act(
                        remote(
                            self.view(OWN + index),
                            self.view(slot_there),
                            self.send.at[number * GROUP + index],
                            self.recv.at[slot_there],
                            (p.rep + offset, p.member),
                        )
                    )

    def start(self):
        self.outgoing(lambda copy: copy.start())

    def drain(self):
        self.outgoing(lambda copy: copy.wait_send())

    def wait(self):
        p = self.place
        begin, stop = p.slots(0, GROUP)
        for offset in OFFSETS:
            for index in range(GROUP):
                slot = OWN + offset * GROUP + index

                @pl.when((slot >= begin) & (slot < stop))
                def _():
                    remote(
                        self.view(slot), self.view(slot), self.send.at[0], self.recv.at[slot],
                        (p.rep, p.near),
                    ).wait_recv()


def dma(count):
    return [pltpu.SemaphoreType.DMA((count,))] * 2


class Halving:
    def __init__(self, place, levels, deep, bits, send, recv):
        self.place, self.levels, self.deep = place, levels, deep
        self.send, self.recv = send, recv
        self.bits = bits

    def mine(self, step):
        return lax.rem(lax.div(self.place.rep, jnp.int32(self.bits[step])), 2)

    def partner(self, step):
        p = self.place
        return (flipped(p.rep, self.bits[step]), p.member)

    def rows(self, start, count):
        return pl.ds(pl.multiple_of(start * self.deep, self.deep), count * self.deep)

    def firsts(self):
        rest = self.bits[1:]
        for j in range(self.place.reps // 2):
            yield j, sum(bit * ((j >> (len(rest) - 1 - q)) & 1) for q, bit in enumerate(rest))

    def copies(self, step):
        give = 1 - self.mine(step)
        source, target = self.levels[step], self.levels[step + 1]
        if step == 0:
            return [
                remote(
                    source.at[self.rows(give * self.bits[0] + offset, 1), :],
                    target.at[self.rows(j, 1), :],
                    self.send.at[j], self.recv.at[j], self.partner(0),
                )
                for j, offset in self.firsts()
            ]
        half = self.place.reps >> (step + 1)
        slot = self.place.reps // 2 + step - 1
        return [
            remote(
                source.at[self.rows(give * half, half), :], target.at[self.rows(0, half), :],
                self.send.at[slot], self.recv.at[slot], self.partner(step),
            )
        ]

    def start(self, step):
        for copy in self.copies(step):
            copy.start()

    def finish(self, step, out=None):
        copies = self.copies(step)
        mine = self.mine(step)
        source, target = self.levels[step], self.levels[step + 1]
        half = self.place.reps >> (step + 1)
        if step == 0:
            for j, offset in self.firsts():
                copies[j].wait_recv()
                at = self.rows(j, 1)
                kept = source[self.rows(mine * self.bits[0] + offset, 1), :]
                target[at, :] = (target[at, :].astype(F32) + kept.astype(F32)).astype(BF)
            return
        copies[0].wait_recv()
        for j in range(half):
            at = self.rows(j, 1)
            kept = source[self.rows(mine * half + j, 1), :]
            total = target[at, :].astype(F32) + kept.astype(F32)
            if out is None:
                target[at, :] = total.astype(BF)
            else:
                ref, lanes = out
                ref[:, lanes] = total

    def drain(self, step):
        for copy in self.copies(step):
            copy.wait_send()


def orders(reps):
    bits = doublings(reps)
    return bits, bits[1:2] + bits[:1] + bits[2:]


def split(wide, quarters):
    cut = max(wide * quarters // 4 // 128, 1) * 128
    return slice(0, cut), slice(cut, wide)


def halving_sems(reps):
    return dma(reps // 2 + reps.bit_length() - 2)


def halving_levels(reps, deep, wide, quarters, first):
    return [
        pltpu.VMEM(((reps >> s) * deep, lanes.stop - lanes.start), BF)
        for lanes in split(wide, quarters)
        for s in range(first, reps.bit_length())
    ]


def grad_chunks(left, right, right_axis, targets, deep, narrow):
    chunk = 128
    width = left.shape[1]

    def body(i, carry):
        at = pl.ds(pl.multiple_of(i * chunk, chunk), chunk)
        if deep == narrow:
            columns = left[:, at]
        else:
            source = lax.broadcasted_iota(jnp.int32, (width, chunk), 0)
            column = lax.broadcasted_iota(jnp.int32, (width, chunk), 1) + i * chunk
            within = column % deep
            picked = (source == (column // deep) * narrow + within) & (within < narrow)
            columns = dot_over(left[...], jnp.where(picked, 1.0, 0.0).astype(BF), 1, 0).astype(BF)
        product = dot_over(columns, right[...], 0, right_axis).astype(BF)
        cut = targets[0].shape[1]
        targets[0][at, :], targets[1][at, :] = product[:, :cut], product[:, cut:]
        return carry

    lax.fori_loop(0, targets[0].shape[0] // chunk, body, 0)


def image_codes(place, sizes_ref, kind):
    start = lax.fori_loop(0, place.rep * GROUP, lambda i, n: n + sizes_ref[i], jnp.int32(0))
    index = lax.broadcasted_iota(jnp.int32, (8, place.rows), 1)
    row = lax.broadcasted_iota(jnp.int32, (8, place.rows), 0)
    codes = []
    for b in range(GROUP):
        size = sizes_ref[place.rep * GROUP + b]
        base = lax.div(start, jnp.int32(IMG))
        turn = (base + 1) * IMG - start
        kind_of_image = lax.rem(base + jnp.where(index >= turn, 1, 0), 4)
        live = index < size
        same = kind_of_image == row
        query = jnp.where(same | ~live, 1.0, 0.0)
        key = jnp.where(same & live, 0.0, FAR)
        code = jnp.where(kind == 0, query, key)
        code = jnp.where(row < 4, code, 0.0)
        codes.append(jnp.where(kind == 2, jnp.where(row == 0, 1.0, 0.0), code))
        start = start + size
    return codes


def front_kernel(
    capacity, reps, rows, sizes_ref, tok_ref, cot_ref, gain_ref, shift_ref, w_ref, bias_ref,
    first_ref, own_ref, query_ref, win_ref, cotall_ref,
    xall, sbuf, code, gsend, grecv, csend, crecv, ssend, srecv, ksend, krecv, vsend, vrecv,
):
    p = Place(capacity, reps, rows)
    barrier, count = p.wide_barrier()
    size = sizes_ref[p.rep * GROUP + p.member]
    live = lax.broadcasted_iota(jnp.int32, (capacity, 1), 0) < size
    clean = lambda ref: jnp.where(live, ref[...].astype(F32), 0.0).astype(BF)
    own_ref[...] = jnp.zeros_like(own_ref)
    own_ref[pl.ds(0, capacity), :] = clean(tok_ref)
    xall[p.block(p.member), :] = own_ref[...]
    pl.semaphore_wait(barrier, count)
    tokens = Gather(p, xall, rows, gsend, grecv)
    tokens.start()
    cotall_ref[p.block(p.member), :] = jnp.zeros((rows, tok_ref.shape[1]), BF)
    cotall_ref[pl.ds(pl.multiple_of(p.member * rows, rows), capacity), :] = clean(cot_ref)
    gain, shift = gain_ref[...][None, :], shift_ref[...][None, :]

    def normalize(owner):
        block = p.block(owner)
        normed, _ = norm_parts(xall[block, :].astype(F32))
        first_ref[block, :] = (normed * gain + shift).astype(BF)

    odd = lax.rem(p.member, 2)
    cross = 2 - 2 * odd
    kept = 2 * odd
    kind_of = lambda i: lax.div(3 * p.member + i, GROUP)
    def spot_of(i):
        kind = kind_of(i)
        return jnp.where(kind == 0, 2 * WINDOW, (kind - 1) * WINDOW + OWN)

    gap = jnp.zeros((HD, rows), F32)
    for i in range(3):
        for b, rest in enumerate(image_codes(p, sizes_ref, kind_of(i))):
            at = slice(b * rows, (b + 1) * rows)
            for h in range(GROUP):
                code[i, h * HP : (h + 1) * HP, at] = jnp.concatenate([gap, rest], axis=0)

    def project(i, pair):
        block = first_ref[p.pair_block(pair), :]
        bias = bias_ref[pl.ds(3 * p.member + i, 1), :]
        bias = jnp.transpose(jnp.broadcast_to(bias, (8, bias.shape[1])))[:, 0:1]
        total = dot_over(w_ref[i], block, 1, 1) + bias + code[i, :, p.pair_block(pair)]
        for b in range(2):
            sbuf[i, pair * 2 + b] = total[:, b * rows : (b + 1) * rows].astype(BF)

    def shuffle(i, pair, way, target):
        slot = way * 2 + pair
        return remote(
            sbuf.at[i, pl.ds(pair * 2, 2)],
            win_ref.at[pl.ds(spot_of(i) + pair * 2, 2)],
            ssend.at[slot], srecv.at[slot], (p.rep, target),
        )

    normalize(p.member)
    tokens.wait_near()
    normalize(p.near)
    tokens.forward(0)
    project(cross, p.pair)
    shuffle(cross, p.pair, 0, p.far).start()
    tokens.forward(1)
    project(1, p.pair)
    shuffle(1, p.pair, 1, p.near).start()
    project(kept, p.pair)
    other = 1 - p.pair
    normalize(p.far)
    tokens.wait_rest()
    normalize(p.diagonal)
    project(cross, other)
    shuffle(cross, other, 0, p.far).start()
    project(1, other)
    shuffle(1, other, 1, p.near).start()
    project(kept, other)
    win_ref[pl.ds(spot_of(kept), GROUP)] = sbuf[kept]
    for pair in (p.pair, other):
        shuffle(cross, pair, 0, p.far).wait_recv()
        shuffle(1, pair, 1, p.near).wait_recv()
    keys = Exchange(p, lambda slot: win_ref.at[slot], ksend, krecv)
    values = Exchange(p, lambda slot: win_ref.at[WINDOW + slot], vsend, vrecv)
    keys.start()
    values.start()
    cotangents = Gather(p, cotall_ref, rows, csend, crecv)
    cotangents.start()
    query_ref[...] = win_ref[pl.ds(2 * WINDOW, GROUP)]
    cotangents.wait_near()
    cotangents.forward(0)
    cotangents.forward(1)
    cotangents.wait_rest()
    keys.wait()
    values.wait()
    keys.drain()
    values.drain()
    for pair in (p.pair, other):
        shuffle(cross, pair, 0, p.far).wait_send()
        shuffle(1, pair, 1, p.near).wait_send()
    tokens.drain()
    cotangents.drain()


def joined(view, head, blocks):
    return jnp.concatenate([view(b)[head, :] for b in blocks], axis=1)


def pieces(rows):
    count = max(512 // rows, 1)
    for low in range(0, GROUP, count):
        yield range(low, low + count), slice(low * rows, (low + count) * rows)


def attend_kernel(capacity, reps, rows, sizes_ref, query_ref, win_ref, mixed_ref, lse_ref, acc):
    p = Place(capacity, reps, rows)
    heads = [slice(h * HP, (h + 1) * HP) for h in range(GROUP)]
    for blocks, at in pieces(rows):
        begin, stop = p.slots(blocks[0], blocks[-1] + 1)
        acc[:, at] = jnp.zeros((acc.shape[0], at.stop - at.start), F32)
        queries = [joined(lambda b: query_ref.at[b], head, blocks) for head in heads]

        def attend(slot, tops):
            raws = [dot_over(win_ref[slot, head, :], query, 0, 0) for head, query in zip(heads, queries)]
            news = [
                jnp.maximum(top, jnp.max(raw, axis=0, keepdims=True) * (SCALE * LOG2E))
                for top, raw in zip(tops, raws)
            ]
            powers = [
                jnp.exp2(raw * (SCALE * LOG2E) - new).astype(BF) for raw, new in zip(raws, news)
            ]
            for head, top, new, power in zip(heads, tops, news, powers):
                value = win_ref[WINDOW + slot, head, :]
                acc[head, at] = acc[head, at] * jnp.exp2(top - new) + dot_over(value, power, 1, 0)
            return tuple(news)

        tops = lax.fori_loop(
            begin, stop, attend, tuple(jnp.full((1, at.stop - at.start), 4.0 * FAR, F32) for _ in heads)
        )
        index = lax.broadcasted_iota(jnp.int32, (1, rows), 1)
        live = jnp.concatenate(
            [
                jnp.where(index < sizes_ref[p.rep * GROUP + b], 1.0, 0.0) for b in blocks
            ],
            axis=1,
        )
        for h, head in enumerate(heads):
            whole = acc[h * HP + HD : h * HP + HD + 1, at]
            mixed_ref[head, at] = (acc[head, at] / whole).astype(BF)
            lse_ref[h : h + 1, at] = jnp.where(live > 0.0, tops[h] + jnp.log(whole) * LOG2E, 0.0)


def middle_kernel(
    capacity, reps, rows, deep, tok_ref, cot_ref, query_ref, mixed_ref, lse_ref, wo_ref, wup_ref,
    wdn_ref, upb_ref, outb_ref, gain_ref, shift_ref, downb_ref,
    out_ref, dres_ref, dmix_ref, stats_ref, qwin_ref, up_a, up_b, down_a, down_b, wo_a, wo_b,
    sums_ref, dupb_ref,
    part, part2, second, hidden, dbefore, dresall, dact, dwdn_a, dwdn_b, dwup_a, dwup_b, res_scr, norm_scr, held,
    asend, arecv, bsend, brecv, csend, crecv, dsend, drecv, esend, erecv, qsend, qrecv,
    *halving_refs,
):
    p = Place(capacity, reps, rows)
    barrier, count = p.wide_barrier()
    count = count + p.halving_barrier()
    out_bias, gain, shift, down_bias = (
        ref[...][None, :] for ref in (outb_ref, gain_ref, shift_ref, downb_ref)
    )
    other = 1 - p.pair
    narrow = cot_ref.shape[1] // reps

    def attn_partial(owner):
        part[p.block(owner), :] = dot_over(
            mixed_ref[:, p.block(owner)], wo_ref[...], 0, 0
        ).astype(BF)

    attn_partial(p.diagonal)
    pl.semaphore_wait(barrier, count)
    one = Scatter(p, part, held.at[0], rows, asend, arecv)
    one.ahead().start()
    attn_partial(p.near)
    one.own().start()
    qwin_ref[pl.ds(OWN, GROUP)] = query_ref[...]
    queries = Exchange(p, lambda slot: qwin_ref.at[slot], qsend, qrecv)
    queries.start()
    attn_partial(p.far)
    one.pass_on()
    attn_partial(p.member)
    for pair in (0, 1):
        at = pl.ds(pair * 2 * rows, 2 * rows)
        dact[at, :] = dot_over(cot_ref[at, :], wdn_ref[...], 1, 1)
    resid = tok_ref[...].astype(F32) + one.result() + out_bias
    res_scr[...] = resid
    normed, inverse = norm_parts(resid)
    norm_scr[...] = normed
    second[p.block(p.member), :] = (normed * gain + shift).astype(BF)
    gather = Gather(p, second, rows, bsend, brecv)
    gather.start()

    def mlp(pair):
        at = p.pair_block(pair)
        before = dot_over(second[at, :], wup_ref[...], 1, 1) + upb_ref[pl.ds(p.member, 1), :]
        activated, derivative = gelu_parts(before)
        hidden[at, :] = activated.astype(BF)
        grad = dact[at, :] * derivative
        dact[at, :] = grad
        dbefore[at, :] = grad.astype(BF)
        part2[at, :] = dot_over(dbefore[at, :], wup_ref[...], 1, 0).astype(BF)

    gather.wait_near()
    gather.forward(0)
    mlp(p.pair)
    gather.forward(1)
    two = Scatter(p, part2, held.at[1], rows, csend, crecv)
    two.own().start()
    gather.wait_rest()
    mlp(other)
    two.ahead().start()
    grad_chunks(cot_ref, hidden, 0, (dwdn_a, dwdn_b), deep, narrow)
    pairs = ((dwdn_a, down_a), (dwdn_b, down_b), (dwup_a, up_a), (dwup_b, up_b))
    halvings = [
        Halving(p, list(pair), deep, orders(reps)[i % 2], *halving_refs[2 * i : 2 * i + 2])
        for i, pair in enumerate(pairs)
    ]
    for halving in halvings[:2]:
        halving.start(0)
    two.pass_on()
    grad_chunks(second, dbefore, 0, (dwup_a, dwup_b), deep, narrow)
    for halving in halvings[2:]:
        halving.start(0)

    def down(pair):
        at = p.pair_block(pair)
        part[at, :] = dot_over(hidden[at, :], wdn_ref[...], 1, 0).astype(BF)

    dsecond = two.result()
    own_cot = cot_ref[p.block(p.member), :].astype(F32)
    normed = norm_scr[...]
    dresid = own_cot + norm_backward(dsecond, normed, inverse, gain)
    dres_ref[...] = dresid
    dresall[p.block(p.member), :] = dresid.astype(BF)
    again = Gather(p, dresall, rows, dsend, drecv)
    again.start()
    three = Scatter(p, part, held.at[2], rows, esend, erecv)
    down(other)
    three.ahead().start()
    down(p.pair)
    three.own().start()
    dupb_ref[...] = jnp.sum(dact[...], axis=0, keepdims=True)
    for i, term in enumerate((dresid, dsecond * normed, dsecond, own_cot)):
        sums_ref[pl.ds(i, 1), :] = jnp.sum(term, axis=0, keepdims=True)
    again.wait_near()
    again.forward(0)
    three.pass_on()

    def mixed_grad(pair):
        at = p.pair_block(pair)
        dmixed = dot_over(wo_ref[...], dresall[at, :], 1, 1).astype(BF)
        dmix_ref[:, at] = dmixed
        product = dmixed.astype(F32) * mixed_ref[:, at].astype(F32)
        stats_ref[pl.ds(0, GROUP), at] = lse_ref[:, at]
        for h in range(GROUP):
            stats_ref[pl.ds(GROUP + h, 1), at] = jnp.sum(
                product[h * HP : (h + 1) * HP], axis=0, keepdims=True
            )

    mixed_grad(p.pair)
    again.forward(1)
    again.wait_rest()
    mixed_grad(other)
    grad_chunks(dresall, mixed_ref, 1, (wo_a, wo_b), deep, narrow)
    out_ref[...] = (res_scr[...] + three.result() + down_bias).astype(BF)
    queries.wait()
    queries.drain()
    for halving in halvings:
        halving.finish(0)
        halving.drain(0)
    gather.drain()
    again.drain()


def back_kernel(
    capacity, reps, rows, deep, win_ref, qwin_ref, dmix_ref, stats_ref, first_ref, w_ref, tok_ref,
    dres_ref, gain_ref, up_a, up_b, down_a, down_b, wo_a, wo_b,
    grad_ref, dbias_ref, sums_ref, dup_out, ddn_out, dwo_out, dwi_out,
    dwin, swin, dq, dv, sbuf, dproj, part, held, *rest,
):
    steps = reps.bit_length() - 1
    scratch = list(rest)
    take = lambda n: [scratch.pop(0) for _ in range(n)]
    up_levels = [[None, ref] + take(steps - 1) for ref in (up_a, up_b)]
    dn_levels = [[None, ref] + take(steps - 1) for ref in (down_a, down_b)]
    wo_levels = [[ref] + take(steps) for ref in (wo_a, wo_b)]
    wi_levels = [take(steps + 1) for _ in range(2)]
    (ksend, krecv, tsend, trecv, ssend, srecv, rsend, rrecv) = take(8)
    p = Place(capacity, reps, rows)
    barrier, count = p.wide_barrier()
    count = count + p.halving_barrier()
    for b in range(GROUP):
        at = slice(b * rows, (b + 1) * rows)
        dwin[OWN + b] = dmix_ref[:, at]
        swin[OWN + b] = stats_ref[:, at]
    pl.semaphore_wait(barrier, count)
    grads_in = Exchange(p, lambda slot: dwin.at[slot], ksend, krecv)
    stats_in = Exchange(p, lambda slot: swin.at[slot], tsend, trecv)
    grads_in.start()
    stats_in.start()
    down, up, inner, outer = (
        [Halving(p, refs, deep, order, *take(2)) for refs, order in zip(levels, orders(reps))]
        for levels in (dn_levels, up_levels, wi_levels, wo_levels)
    )
    work = [
        [one, first, (out, lanes)]
        for pair, first, quarters, out in (
            (down, 1, 2, ddn_out), (up, 1, 2, dup_out), (outer, 0, 3, dwo_out), (inner, 0, 3, dwi_out)
        )
        for one, lanes in zip(pair, split(out.shape[1], quarters))
    ]

    def advance(some):
        for item in some:
            one, step, out = item
            if step < steps:
                one.finish(step, out if step == steps - 1 else None)
                if step + 1 < steps:
                    one.start(step + 1)
                item[1] = step + 1

    for one, step, _ in work[:6]:
        one.start(step)
    heads = [slice(h * HP, (h + 1) * HP) for h in range(GROUP)]
    every = range(GROUP)
    for blocks, at in pieces(rows):
        begin, stop = p.slots(blocks[0], blocks[-1] + 1)
        queries = [joined(lambda b: qwin_ref.at[OWN + b], head, blocks) for head in heads]
        dq[:, at] = jnp.zeros((dq.shape[0], at.stop - at.start), F32)

        def query_grads(slot, carry):
            keys = [win_ref[slot, head, :] for head in heads]
            raws = [dot_over(keys[h], queries[h], 0, 0) for h in every]
            dprobs = [
                dot_over(win_ref[WINDOW + slot, head, :], dmix_ref[head, at], 0, 0) for head in heads
            ]
            dscores = [
                (
                    jnp.exp2(raws[h] * (SCALE * LOG2E) - stats_ref[h : h + 1, at])
                    * (dprobs[h] - stats_ref[GROUP + h : GROUP + h + 1, at])
                ).astype(BF)
                for h in every
            ]
            for h, head in enumerate(heads):
                dq[head, at] += dot_over(keys[h], dscores[h], 1, 0)
            return carry

        lax.fori_loop(begin, stop, query_grads, 0)

    def owner_of(kind):
        c = kind * GROUP + p.member
        return lax.div(c, 3), lax.rem(c, 3)

    high = GROUP * HP

    def part_of(index):
        return pl.ds(pl.multiple_of(index * high, high), high)

    def home(kind):
        owner, index = owner_of(kind)
        return owner, remote(
            sbuf.at[kind], dproj.at[part_of(index), :], ssend.at[kind], srecv.at[index],
            (p.rep, owner),
        )

    def send_home(kind, grads, scale):
        value = grads[...] * scale
        sbuf[kind] = value.astype(BF)
        dbias_ref[:, kind : kind + 1] = jnp.sum(value, axis=1, keepdims=True)
        owner, copy = home(kind)

        @pl.when(owner != p.member)
        def _():
            copy.start()

    send_home(0, dq, SCALE)
    dk = dq
    grads_in.wait()
    stats_in.wait()
    for blocks, at in pieces(rows):
        begin, stop = p.slots(blocks[0], blocks[-1] + 1)
        keys = [joined(lambda b: win_ref.at[OWN + b], head, blocks) for head in heads]
        values = [joined(lambda b: win_ref.at[WINDOW + OWN + b], head, blocks) for head in heads]
        dk[:, at] = jnp.zeros((dk.shape[0], at.stop - at.start), F32)
        dv[:, at] = jnp.zeros((dv.shape[0], at.stop - at.start), F32)

        def key_grads(slot, carry):
            stats = jnp.transpose(swin[slot])
            picked = [qwin_ref[slot, head, :] for head in heads]
            dmixed = [dwin[slot, head, :] for head in heads]
            raws = [dot_over(picked[h], keys[h], 0, 0) for h in every]
            dprobs = [dot_over(dmixed[h], values[h], 0, 0) for h in every]
            probs = [jnp.exp2(raws[h] * (SCALE * LOG2E) - stats[:, h : h + 1]) for h in every]
            dscores = [
                (probs[h] * (dprobs[h] - stats[:, GROUP + h : GROUP + h + 1])).astype(BF)
                for h in every
            ]
            for h, head in enumerate(heads):
                dk[head, at] += dot_over(picked[h], dscores[h], 1, 0)
            for h, head in enumerate(heads):
                dv[head, at] += dot_over(dmixed[h], probs[h].astype(BF), 1, 0)
            return carry

        lax.fori_loop(begin, stop, key_grads, 0)

    send_home(1, dk, SCALE)
    send_home(2, dv, 1.0)
    for kind in range(3):
        owner, index = owner_of(kind)

        @pl.when(owner == p.member)
        def _():
            dproj[part_of(index), :] = sbuf[kind]

    advance(work[:4])
    for index in range(3):
        source = lax.rem(3 * p.member + index, GROUP)

        @pl.when(source != p.member)
        def _():
            remote(
                sbuf.at[0], dproj.at[part_of(index), :], ssend.at[0], srecv.at[index],
                (p.rep, p.near),
            ).wait_recv()

    narrow = first_ref.shape[1] // reps
    grad_chunks(first_ref, dproj, 1, [levels[0] for levels in wi_levels], deep, narrow)
    for one, step, _ in work[6:]:
        one.start(step)

    def partial(owner):
        part[p.block(owner), :] = dot_over(dproj[:, p.block(owner)], w_ref[...], 0, 0).astype(BF)

    scatter = Scatter(p, part, held, rows, rsend, rrecv)
    partial(p.diagonal)
    scatter.ahead().start()
    partial(p.near)
    scatter.own().start()
    partial(p.far)
    scatter.pass_on()
    partial(p.member)
    advance(work[:6])
    normed, inverse = norm_parts(tok_ref[...].astype(F32))
    dfirst = scatter.result()
    for i, term in enumerate((dfirst * normed, dfirst)):
        sums_ref[pl.ds(i, 1), :] = jnp.sum(term, axis=0, keepdims=True)
    grad_ref[...] = dres_ref[...] + norm_backward(dfirst, normed, inverse, gain_ref[...][None, :])
    for _ in range(steps):
        advance(work)
    for kind in range(3):
        owner, copy = home(kind)

        @pl.when(owner != p.member)
        def _():
            copy.wait_send()

    grads_in.drain()
    stats_in.drain()
    for pair, begin in ((down, 1), (up, 1), (inner, 0), (outer, 0)):
        for one in pair:
            for step in range(begin, steps):
                one.drain(step)


def total_kernel(reps, x_ref, o_ref, held, send, recv):
    rep, member = lax.axis_index("rep"), lax.axis_index("grp")
    places = [(rep, flipped(member, bit)) for bit in doublings(GROUP)]
    places += [(flipped(rep, bit), member) for bit in doublings(reps)]
    barrier = pltpu.get_barrier_semaphore()
    for place in places:
        pl.semaphore_signal(barrier, inc=1, device_id=place, device_id_type=MESH)
    pl.semaphore_wait(barrier, len(places))
    o_ref[...] = x_ref[...]
    for slot, place in enumerate(places):
        copy = remote(o_ref, held.at[slot], send.at[slot], recv.at[slot], place)
        copy.start()
        copy.wait()
        o_ref[...] += held[slot]


def call(kernel, number, args, outs, scratch, smem=0, limit=63):
    vmem = pl.BlockSpec(memory_space=pltpu.VMEM)
    smem_spec = pl.BlockSpec(memory_space=pltpu.SMEM)
    linked = {} if number is None else {"collective_id": number, "has_side_effects": True}
    return pl.pallas_call(
        kernel,
        out_shape=[jax.ShapeDtypeStruct(*o) for o in outs],
        in_specs=[smem_spec] * smem + [vmem] * (len(args) - smem),
        out_specs=[vmem] * len(outs),
        scratch_shapes=scratch,
        compiler_params=pltpu.CompilerParams(vmem_limit_bytes=limit * 2**20, **linked),
    )(*args)


def per_device(
    tokens,
    cotangent,
    slice_sizes,
    gain_one,
    shift_one,
    attn_in,
    attn_bias,
    attn_out,
    out_bias,
    gain_two,
    shift_two,
    mlp_up,
    up_bias,
    mlp_down,
    down_bias,
):
    capacity, width = tokens.shape
    reps, groups = lax.axis_size("rep"), lax.axis_size("grp")
    assert groups == GROUP
    rows = -(-capacity // 128) * 128
    all_rows = GROUP * rows
    rep, member = lax.axis_index("rep"), lax.axis_index("grp")
    device = rep * groups + member
    ff_rows = mlp_up.shape[0]
    heads_high = GROUP * HP
    devices = reps * groups
    vm = pltpu.VMEM

    deep = -(-(width // reps) // 16) * 16
    own_count = slice_sizes[device]
    live_col = (jnp.arange(capacity, dtype=jnp.int32) < own_count)[:, None]
    w_in = jnp.pad(
        attn_in.reshape(3, GROUP, HD, width), ((0, 0), (0, 0), (0, HP - HD), (0, 0))
    ).reshape(3, heads_high, width)
    bias = jnp.stack([attn_bias[0], jnp.zeros((width,), F32), attn_bias[1]])
    bias = jnp.pad(
        bias.reshape(3 * GROUP, GROUP, HD), ((0, 0), (0, 0), (0, HP - HD))
    ).reshape(3 * GROUP, heads_high)
    w_out = jnp.pad(
        attn_out.reshape(GROUP, HD, width), ((0, 0), (0, HP - HD), (0, 0))
    ).reshape(heads_high, width)
    place = (capacity, reps, rows)
    window_sems = [
        pltpu.SemaphoreType.DMA((len(OFFSETS) * GROUP,)), pltpu.SemaphoreType.DMA((WINDOW,))
    ]

    first, tok, query, window, cot_all = call(
        functools.partial(front_kernel, *place), 1,
        (slice_sizes, tokens, cotangent, gain_one, shift_one, w_in, bias),
        [((all_rows, width), BF), ((rows, width), BF), ((GROUP, heads_high, rows), BF),
         ((2 * WINDOW + GROUP, heads_high, rows), BF), ((all_rows, width), BF)],
        [vm((all_rows, width), BF), vm((3, GROUP, heads_high, rows), BF),
         vm((3, heads_high, all_rows), F32), *dma(5), *dma(5), *dma(4), *window_sems * 2],
        smem=1,
    )
    mixed, lse = call(
        functools.partial(attend_kernel, *place), None, (slice_sizes, query, window),
        [((heads_high, all_rows), BF), ((GROUP, all_rows), F32)],
        [vm((heads_high, all_rows), F32)],
        smem=1,
    )
    gapped = reps * deep

    def halves(high, wide, quarters):
        return [((high, lanes.stop - lanes.start), BF) for lanes in split(wide, quarters)]

    out, dresid, dmixed, stats, qwindow, *partials, sums_two, dup = call(
        functools.partial(middle_kernel, *place, deep), 2,
        (tok, cot_all, query, mixed, lse, w_out, mlp_up, mlp_down,
         up_bias.reshape(GROUP, ff_rows), out_bias, gain_two, shift_two, down_bias),
        [((rows, width), BF), ((rows, width), F32), ((heads_high, all_rows), BF),
         ((2 * GROUP, all_rows), F32), ((WINDOW, heads_high, rows), BF), *halves(gapped // 2, ff_rows, 2),
         *halves(gapped // 2, ff_rows, 2), *halves(gapped, heads_high, 3), ((4, width), F32),
         ((1, ff_rows), F32)],
        [vm((all_rows, width), BF)] * 3
        + [vm((all_rows, ff_rows), BF)] * 2
        + [vm((all_rows, width), BF), vm((all_rows, ff_rows), F32), *[vm(*o) for o in halves(gapped, ff_rows, 2) * 2],
           vm((rows, width), F32), vm((rows, width), F32), vm((3, 3, rows, width), BF)]
        + dma(3) + dma(5) + dma(3) + dma(5) + dma(3) + window_sems + halving_sems(reps) * 4,
    )
    input_grad, dbias, sums_one, dmlp_up, dmlp_down, dattn_out, dattn_in = call(
        functools.partial(back_kernel, *place, deep), 3,
        (window, qwindow, dmixed, stats, first, w_in.reshape(3 * heads_high, width), tok, dresid,
         gain_one, *partials),
        [((rows, width), F32), ((heads_high, 3), F32), ((2, width), F32),
         ((deep, ff_rows), F32), ((deep, ff_rows), F32), ((deep, heads_high), F32),
         ((deep, 3 * heads_high), F32)],
        [vm((WINDOW, heads_high, rows), BF), vm((WINDOW, 2 * GROUP, rows), F32)]
        + [vm((heads_high, all_rows), F32)] * 2
        + [vm((3, heads_high, all_rows), BF), vm((3 * heads_high, all_rows), BF)]
        + [vm((all_rows, width), BF), vm((3, rows, width), BF)]
        + halving_levels(reps, deep, ff_rows, 2, 2) * 2
        + halving_levels(reps, deep, heads_high, 3, 1)
        + halving_levels(reps, deep, 3 * heads_high, 3, 0)
        + window_sems * 2 + dma(3) + dma(3) + halving_sems(reps) * 8,
    )
    narrow = width // reps
    dmlp_up, dmlp_down = dmlp_up[:narrow].T, dmlp_down[:narrow].T

    def without_gaps(grads):
        kinds = grads.shape[1] // heads_high
        return (
            grads[:narrow].T.reshape(kinds, GROUP, HP, narrow)[:, :, :HD]
            .reshape(kinds * GROUP * HD, narrow)
        )

    dattn_out, dattn_in = without_gaps(dattn_out), without_gaps(dattn_in)

    def totals(parts):
        flat = jnp.concatenate([part.reshape(-1) for part in parts])
        lines = -(-flat.shape[0] // 1024) * 8
        flat = jnp.pad(flat, (0, lines * 128 - flat.shape[0])).reshape(lines, 128)
        steps = len(doublings(reps)) + len(doublings(groups))
        [summed] = call(
            functools.partial(total_kernel, reps), 0, (flat,), [(flat.shape, F32)],
            [vm((steps, lines, 128), F32), *dma(steps)], limit=16,
        )
        summed = summed.reshape(-1)
        spot, outs = 0, []
        for part in parts:
            outs.append(summed[spot : spot + part.size].reshape(part.shape))
            spot += part.size
        return outs

    dbias = dbias.T.reshape(3, GROUP, HP)[:, :, :HD].reshape(3, GROUP * HD)
    dattn_bias = lax.dynamic_update_slice_in_dim(
        jnp.zeros((2, width), F32), dbias[0::2], member * GROUP * HD, 1
    )
    dup_bias = lax.dynamic_update_slice_in_dim(
        jnp.zeros(up_bias.shape, F32), dup[0], member * ff_rows, 0
    )
    dgain_one, dshift_one, dattn_bias, dout_bias, dgain_two, dshift_two, dup_bias, ddown_bias = (
        totals(
            (
                sums_one[0], sums_one[1], dattn_bias, sums_two[0], sums_two[1], sums_two[2],
                dup_bias, sums_two[3],
            )
        )
    )
    block_output = jnp.where(live_col, out[:capacity], jnp.zeros((), BF))
    input_grad = jnp.where(live_col, input_grad[:capacity], 0.0)
    return (
        block_output, input_grad, dgain_one, dshift_one, dattn_in, dattn_bias, dattn_out,
        dout_bias, dgain_two, dshift_two, dmlp_up, dup_bias, dmlp_down, ddown_bias,
    )


def solution(mesh):
    rows, rep_grp = P("grp", None), P(("rep", "grp"), None)
    in_specs = (
        rep_grp, rep_grp, P(), P(), P(), rows, P(), rows, P(), P(), P(), rows, P(), rows, P(),
    )
    grads = P("grp", "rep")
    out_specs = (
        rep_grp, rep_grp, P(), P(), grads, P(), grads, P(), P(), P(), grads, P(), grads, P(),
    )
    return jax.shard_map(
        per_device, mesh=mesh, in_specs=in_specs, out_specs=out_specs, check_vma=False
    )
```

```python
import functools

import jax
import jax.numpy as jnp
from jax import lax
from jax.experimental import pallas as pl
from jax.experimental.pallas import tpu as pltpu
from jax.sharding import PartitionSpec as P

H = 16
HD = 72
HP = 80
IMG = 729
GROUP = 4
NEAR_GROUPS = 2
WINDOW = (2 * NEAR_GROUPS + 1) * GROUP
OWN = NEAR_GROUPS * GROUP
OFFSETS = (1, -1, 2, -2)

EPSILON = 1e-06
SQRT_TWO_PI = 0.7978845608028654
CUBIC = 0.044715
FAR = -(2.0**80)
SCALE = HD ** (-0.5)
LOG2E = 1.4426950408889634
BF = jnp.bfloat16
F32 = jnp.float32
MESH = pl.DeviceIdType.MESH


def norm_parts(rows):
    centered = rows - jnp.mean(rows, axis=-1, keepdims=True)
    inverse = lax.rsqrt(jnp.mean(centered * centered, axis=-1, keepdims=True) + EPSILON)
    return centered * inverse, inverse


def norm_backward(dscaled, normed, inverse, gain_row):
    dnormed = dscaled * gain_row
    return inverse * (
        dnormed
        - jnp.mean(dnormed, axis=-1, keepdims=True)
        - normed * jnp.mean(dnormed * normed, axis=-1, keepdims=True)
    )


def gelu_parts(before):
    square = before * before
    tangent = jnp.tanh(SQRT_TWO_PI * before * (1.0 + CUBIC * square))
    half = 0.5 * (1.0 + tangent)
    derivative = half + 0.5 * before * (1.0 - tangent * tangent) * (
        SQRT_TWO_PI + SQRT_TWO_PI * 3.0 * CUBIC * square
    )
    return before * half, derivative


def dot_over(left, right, left_axis, right_axis):
    return lax.dot_general(
        left, right, (((left_axis,), (right_axis,)), ((), ())), preferred_element_type=F32
    )


def flipped(index, bit):
    return index + bit * (1 - 2 * ((index // bit) % 2))


def doublings(count):
    return [1 << i for i in range(count.bit_length() - 1)]


class Place:
    def __init__(self, capacity, reps, rows):
        self.capacity, self.reps, self.rows = capacity, reps, rows
        self.devices = reps * GROUP
        self.images = capacity * self.devices // IMG
        self.short = capacity * self.devices - self.images * IMG
        self.rep, self.member = lax.axis_index("rep"), lax.axis_index("grp")
        low = lax.rem(self.member, 2)
        self.near = self.member + 1 - 2 * low
        self.far = lax.rem(self.member + 2, GROUP)
        self.diagonal = lax.rem(self.near + 2, GROUP)
        self.pair = lax.div(self.member, 2)

    def sharing(self, low, high):
        capacity, short, image = self.capacity, self.short, jnp.int32(IMG)
        start = low * capacity - jnp.minimum(low, short)
        end = high * capacity - jnp.maximum(high - (self.devices - short), 0) - 1
        first = lax.div(start, image) * IMG
        after = (jnp.minimum(lax.div(end, image), self.images - 1) + 1) * IMG
        begin = lax.div(first, jnp.int32(capacity))
        stop = jnp.minimum(
            lax.div(after + short + capacity - 1, jnp.int32(capacity)),
            lax.div(after + capacity - 2, jnp.int32(capacity - 1)),
        )
        return begin, jnp.minimum(stop, self.devices)

    def slots(self, low, high):
        base = self.rep * GROUP
        begin, stop = self.sharing(base + low, base + high)
        return jnp.maximum(begin - base + OWN, 0), jnp.minimum(stop - base + OWN, WINDOW)

    def shares(self, block, group):
        begin, stop = self.sharing(group * GROUP, group * GROUP + GROUP)
        return (group >= 0) & (group < self.reps) & (block >= begin) & (block < stop)

    def block(self, owner):
        return pl.ds(pl.multiple_of(owner * self.rows, self.rows), self.rows)

    def pair_block(self, pair):
        return pl.ds(pl.multiple_of(pair * 2 * self.rows, 2 * self.rows), 2 * self.rows)

    def halving_barrier(self):
        barrier = pltpu.get_barrier_semaphore()
        bits = doublings(self.reps)
        for bit in bits:
            pl.semaphore_signal(
                barrier, inc=1, device_id=(flipped(self.rep, bit), self.member),
                device_id_type=MESH,
            )
        return len(bits)

    def group_barrier(self):
        barrier = pltpu.get_barrier_semaphore()
        for other in (self.near, self.far):
            pl.semaphore_signal(
                barrier, inc=1, device_id=(self.rep, other), device_id_type=MESH
            )
        return barrier, 2

    def wide_barrier(self):
        barrier, count = self.group_barrier()
        count = jnp.int32(count)
        for offset in OFFSETS:
            there = self.rep + offset
            valid = (there >= 0) & (there < self.reps)

            @pl.when(valid)
            def _():
                pl.semaphore_signal(
                    barrier, inc=1, device_id=(there, self.member), device_id_type=MESH
                )

            count = count + jnp.where(valid, 1, 0)
        return barrier, count


def remote(source, target, send, recv, place):
    return pltpu.make_async_remote_copy(
        src_ref=source,
        dst_ref=target,
        send_sem=send,
        recv_sem=recv,
        device_id=place,
        device_id_type=MESH,
    )


class Gather:
    def __init__(self, place, ref, rows, send, recv):
        self.place, self.ref, self.rows, self.send, self.recv = place, ref, rows, send, recv
        self.half = rows // 2

    def copy(self, owner, part, slot, target):
        if part is None:
            piece = self.ref.at[pl.ds(pl.multiple_of(owner * self.rows, self.rows), self.rows), :]
        else:
            start = pl.multiple_of(owner * self.rows + part * self.half, self.half)
            piece = self.ref.at[pl.ds(start, self.half), :]
        return remote(
            piece, piece, self.send.at[slot], self.recv.at[slot], (self.place.rep, target)
        )

    def start(self):
        p = self.place
        for part in range(2):
            self.copy(p.member, part, 1 + part, p.far).start()
        self.copy(p.member, None, 0, p.near).start()

    def wait_near(self):
        p = self.place
        self.copy(p.near, None, 0, p.near).wait_recv()

    def forward(self, part):
        p = self.place
        self.copy(p.far, part, 1 + part, p.far).wait_recv()
        self.copy(p.far, part, 3 + part, p.near).start()

    def wait_rest(self):
        p = self.place
        for part in range(2):
            self.copy(p.diagonal, part, 3 + part, p.near).wait_recv()

    def drain(self):
        p = self.place
        self.copy(p.member, None, 0, p.near).wait_send()
        for part in range(2):
            self.copy(p.member, part, 1 + part, p.far).wait_send()
            self.copy(p.far, part, 3 + part, p.near).wait_send()


class Scatter:
    def __init__(self, place, ref, held, rows, send, recv):
        self.place, self.ref, self.held = place, ref, held
        self.rows, self.send, self.recv = rows, send, recv

    def block(self, owner):
        return pl.ds(pl.multiple_of(owner * self.rows, self.rows), self.rows)

    def ahead(self):
        p = self.place
        return remote(
            self.ref.at[self.block(p.diagonal), :], self.held.at[0],
            self.send.at[0], self.recv.at[0], (p.rep, p.near),
        )

    def own(self):
        p = self.place
        return remote(
            self.ref.at[self.block(p.near), :], self.held.at[1],
            self.send.at[1], self.recv.at[1], (p.rep, p.near),
        )

    def across(self):
        p = self.place
        return remote(
            self.held.at[0], self.held.at[2], self.send.at[2], self.recv.at[2], (p.rep, p.far)
        )

    def pass_on(self):
        p = self.place
        self.ahead().wait_recv()
        self.held[0] = (
            self.ref[self.block(p.far), :].astype(F32) + self.held[0].astype(F32)
        ).astype(BF)
        self.across().start()

    def result(self):
        p = self.place
        self.own().wait_recv()
        total = self.ref[self.block(p.member), :].astype(F32) + self.held[1].astype(F32)
        self.across().wait_recv()
        total = total + self.held[2].astype(F32)
        self.ahead().wait_send()
        self.own().wait_send()
        self.across().wait_send()
        return total


class Exchange:
    def __init__(self, place, view, send, recv):
        self.place, self.view, self.send, self.recv = place, view, send, recv

    def outgoing(self, act):
        p = self.place
        for number, offset in enumerate(OFFSETS):
            begin, stop = p.sharing((p.rep + offset) * GROUP, (p.rep + offset + 1) * GROUP)
            valid = (p.rep + offset >= 0) & (p.rep + offset < p.reps)
            for index in range(GROUP):
                block = p.rep * GROUP + index
                slot_there = OWN - offset * GROUP + index

                @pl.when(valid & (block >= begin) & (block < stop))
                def _():
                    act(
                        remote(
                            self.view(OWN + index),
                            self.view(slot_there),
                            self.send.at[number * GROUP + index],
                            self.recv.at[slot_there],
                            (p.rep + offset, p.member),
                        )
                    )

    def start(self):
        self.outgoing(lambda copy: copy.start())

    def drain(self):
        self.outgoing(lambda copy: copy.wait_send())

    def wait(self):
        p = self.place
        begin, stop = p.slots(0, GROUP)
        for offset in OFFSETS:
            for index in range(GROUP):
                slot = OWN + offset * GROUP + index

                @pl.when((slot >= begin) & (slot < stop))
                def _():
                    remote(
                        self.view(slot), self.view(slot), self.send.at[0], self.recv.at[slot],
                        (p.rep, p.near),
                    ).wait_recv()


def dma(count):
    return [pltpu.SemaphoreType.DMA((count,))] * 2


class Halving:
    def __init__(self, place, levels, deep, bits, send, recv):
        self.place, self.levels, self.deep = place, levels, deep
        self.send, self.recv = send, recv
        self.bits = bits

    def mine(self, step):
        return lax.rem(lax.div(self.place.rep, jnp.int32(self.bits[step])), 2)

    def partner(self, step):
        p = self.place
        return (flipped(p.rep, self.bits[step]), p.member)

    def rows(self, start, count):
        return pl.ds(pl.multiple_of(start * self.deep, self.deep), count * self.deep)

    def firsts(self):
        rest = self.bits[1:]
        for j in range(self.place.reps // 2):
            yield j, sum(bit * ((j >> (len(rest) - 1 - q)) & 1) for q, bit in enumerate(rest))

    def copies(self, step):
        give = 1 - self.mine(step)
        source, target = self.levels[step], self.levels[step + 1]
        if step == 0:
            return [
                remote(
                    source.at[self.rows(give * self.bits[0] + offset, 1), :],
                    target.at[self.rows(j, 1), :],
                    self.send.at[j], self.recv.at[j], self.partner(0),
                )
                for j, offset in self.firsts()
            ]
        half = self.place.reps >> (step + 1)
        slot = self.place.reps // 2 + step - 1
        return [
            remote(
                source.at[self.rows(give * half, half), :], target.at[self.rows(0, half), :],
                self.send.at[slot], self.recv.at[slot], self.partner(step),
            )
        ]

    def start(self, step):
        for copy in self.copies(step):
            copy.start()

    def finish(self, step, out=None):
        copies = self.copies(step)
        mine = self.mine(step)
        source, target = self.levels[step], self.levels[step + 1]
        half = self.place.reps >> (step + 1)
        if step == 0:
            for j, offset in self.firsts():
                copies[j].wait_recv()
                at = self.rows(j, 1)
                kept = source[self.rows(mine * self.bits[0] + offset, 1), :]
                target[at, :] = (target[at, :].astype(F32) + kept.astype(F32)).astype(BF)
            return
        copies[0].wait_recv()
        for j in range(half):
            at = self.rows(j, 1)
            kept = source[self.rows(mine * half + j, 1), :]
            total = target[at, :].astype(F32) + kept.astype(F32)
            if out is None:
                target[at, :] = total.astype(BF)
            else:
                ref, lanes = out
                ref[:, lanes] = total

    def drain(self, step):
        for copy in self.copies(step):
            copy.wait_send()


def orders(reps):
    bits = doublings(reps)
    return bits, bits[1:2] + bits[:1] + bits[2:]


def split(wide):
    cut = -(-wide // 256) * 128
    return slice(0, cut), slice(cut, wide)


def halving_sems(reps):
    return dma(reps // 2 + reps.bit_length() - 2)


def halving_levels(reps, deep, wide, first):
    return [
        pltpu.VMEM(((reps >> s) * deep, lanes.stop - lanes.start), BF)
        for lanes in split(wide)
        for s in range(first, reps.bit_length())
    ]


def grad_chunks(left, right, right_axis, targets, deep, narrow):
    chunk = 128
    width = left.shape[1]

    def body(i, carry):
        at = pl.ds(pl.multiple_of(i * chunk, chunk), chunk)
        if deep == narrow:
            columns = left[:, at]
        else:
            source = lax.broadcasted_iota(jnp.int32, (width, chunk), 0)
            column = lax.broadcasted_iota(jnp.int32, (width, chunk), 1) + i * chunk
            within = column % deep
            picked = (source == (column // deep) * narrow + within) & (within < narrow)
            columns = dot_over(left[...], jnp.where(picked, 1.0, 0.0).astype(BF), 1, 0).astype(BF)
        product = dot_over(columns, right[...], 0, right_axis).astype(BF)
        for target, lanes in zip(targets, split(product.shape[1])):
            target[at, :] = product[:, lanes]
        return carry

    lax.fori_loop(0, targets[0].shape[0] // chunk, body, 0)


def image_codes(place, sizes_ref, kind):
    start = lax.fori_loop(0, place.rep * GROUP, lambda i, n: n + sizes_ref[i], jnp.int32(0))
    index = lax.broadcasted_iota(jnp.int32, (8, place.rows), 1)
    row = lax.broadcasted_iota(jnp.int32, (8, place.rows), 0)
    codes = []
    for b in range(GROUP):
        size = sizes_ref[place.rep * GROUP + b]
        base = lax.div(start, jnp.int32(IMG))
        turn = (base + 1) * IMG - start
        kind_of_image = lax.rem(base + jnp.where(index >= turn, 1, 0), 4)
        live = index < size
        same = kind_of_image == row
        query = jnp.where(same | ~live, 1.0, 0.0)
        key = jnp.where(same & live, 0.0, FAR)
        code = jnp.where(kind == 0, query, key)
        code = jnp.where(row < 4, code, 0.0)
        codes.append(jnp.where(kind == 2, jnp.where(row == 0, 1.0, 0.0), code))
        start = start + size
    return codes


def front_kernel(
    capacity, reps, rows, sizes_ref, tok_ref, cot_ref, gain_ref, shift_ref, w_ref, bias_ref,
    first_ref, own_ref, query_ref, win_ref, cotall_ref,
    xall, sbuf, code, gsend, grecv, csend, crecv, ssend, srecv, ksend, krecv, vsend, vrecv,
):
    p = Place(capacity, reps, rows)
    barrier, count = p.wide_barrier()
    size = sizes_ref[p.rep * GROUP + p.member]
    live = lax.broadcasted_iota(jnp.int32, (capacity, 1), 0) < size
    clean = lambda ref: jnp.where(live, ref[...].astype(F32), 0.0).astype(BF)
    own_ref[...] = jnp.zeros_like(own_ref)
    own_ref[pl.ds(0, capacity), :] = clean(tok_ref)
    xall[p.block(p.member), :] = own_ref[...]
    pl.semaphore_wait(barrier, count)
    tokens = Gather(p, xall, rows, gsend, grecv)
    tokens.start()
    cotall_ref[p.block(p.member), :] = jnp.zeros((rows, tok_ref.shape[1]), BF)
    cotall_ref[pl.ds(pl.multiple_of(p.member * rows, rows), capacity), :] = clean(cot_ref)
    gain, shift = gain_ref[...][None, :], shift_ref[...][None, :]

    def normalize(owner):
        block = p.block(owner)
        normed, _ = norm_parts(xall[block, :].astype(F32))
        first_ref[block, :] = (normed * gain + shift).astype(BF)

    odd = lax.rem(p.member, 2)
    cross = 2 - 2 * odd
    kept = 2 * odd
    kind_of = lambda i: lax.div(3 * p.member + i, GROUP)
    def spot_of(i):
        kind = kind_of(i)
        return jnp.where(kind == 0, 2 * WINDOW, (kind - 1) * WINDOW + OWN)

    gap = jnp.zeros((HD, rows), F32)
    for i in range(3):
        for b, rest in enumerate(image_codes(p, sizes_ref, kind_of(i))):
            at = slice(b * rows, (b + 1) * rows)
            for h in range(GROUP):
                code[i, h * HP : (h + 1) * HP, at] = jnp.concatenate([gap, rest], axis=0)

    def project(i, pair):
        block = first_ref[p.pair_block(pair), :]
        bias = bias_ref[pl.ds(3 * p.member + i, 1), :]
        bias = jnp.transpose(jnp.broadcast_to(bias, (8, bias.shape[1])))[:, 0:1]
        total = dot_over(w_ref[i], block, 1, 1) + bias + code[i, :, p.pair_block(pair)]
        for b in range(2):
            sbuf[i, pair * 2 + b] = total[:, b * rows : (b + 1) * rows].astype(BF)

    def shuffle(i, pair, way, target):
        slot = way * 2 + pair
        return remote(
            sbuf.at[i, pl.ds(pair * 2, 2)],
            win_ref.at[pl.ds(spot_of(i) + pair * 2, 2)],
            ssend.at[slot], srecv.at[slot], (p.rep, target),
        )

    normalize(p.member)
    tokens.wait_near()
    normalize(p.near)
    tokens.forward(0)
    project(cross, p.pair)
    shuffle(cross, p.pair, 0, p.far).start()
    tokens.forward(1)
    project(1, p.pair)
    shuffle(1, p.pair, 1, p.near).start()
    project(kept, p.pair)
    other = 1 - p.pair
    normalize(p.far)
    tokens.wait_rest()
    normalize(p.diagonal)
    project(cross, other)
    shuffle(cross, other, 0, p.far).start()
    project(1, other)
    shuffle(1, other, 1, p.near).start()
    project(kept, other)
    win_ref[pl.ds(spot_of(kept), GROUP)] = sbuf[kept]
    for pair in (p.pair, other):
        shuffle(cross, pair, 0, p.far).wait_recv()
        shuffle(1, pair, 1, p.near).wait_recv()
    keys = Exchange(p, lambda slot: win_ref.at[slot], ksend, krecv)
    values = Exchange(p, lambda slot: win_ref.at[WINDOW + slot], vsend, vrecv)
    keys.start()
    values.start()
    cotangents = Gather(p, cotall_ref, rows, csend, crecv)
    cotangents.start()
    query_ref[...] = win_ref[pl.ds(2 * WINDOW, GROUP)]
    cotangents.wait_near()
    cotangents.forward(0)
    cotangents.forward(1)
    cotangents.wait_rest()
    keys.wait()
    values.wait()
    keys.drain()
    values.drain()
    for pair in (p.pair, other):
        shuffle(cross, pair, 0, p.far).wait_send()
        shuffle(1, pair, 1, p.near).wait_send()
    tokens.drain()
    cotangents.drain()


def joined(view, head, blocks):
    return jnp.concatenate([view(b)[head, :] for b in blocks], axis=1)


def pieces(rows):
    count = max(512 // rows, 1)
    for low in range(0, GROUP, count):
        yield range(low, low + count), slice(low * rows, (low + count) * rows)


def attend_kernel(capacity, reps, rows, sizes_ref, query_ref, win_ref, mixed_ref, lse_ref, acc):
    p = Place(capacity, reps, rows)
    heads = [slice(h * HP, (h + 1) * HP) for h in range(GROUP)]
    for blocks, at in pieces(rows):
        begin, stop = p.slots(blocks[0], blocks[-1] + 1)
        acc[:, at] = jnp.zeros((acc.shape[0], at.stop - at.start), F32)
        queries = [joined(lambda b: query_ref.at[b], head, blocks) for head in heads]

        def attend(slot, tops):
            raws = [dot_over(win_ref[slot, head, :], query, 0, 0) for head, query in zip(heads, queries)]
            news = [
                jnp.maximum(top, jnp.max(raw, axis=0, keepdims=True) * (SCALE * LOG2E))
                for top, raw in zip(tops, raws)
            ]
            powers = [
                jnp.exp2(raw * (SCALE * LOG2E) - new).astype(BF) for raw, new in zip(raws, news)
            ]
            for head, top, new, power in zip(heads, tops, news, powers):
                value = win_ref[WINDOW + slot, head, :]
                acc[head, at] = acc[head, at] * jnp.exp2(top - new) + dot_over(value, power, 1, 0)
            return tuple(news)

        tops = lax.fori_loop(
            begin, stop, attend, tuple(jnp.full((1, at.stop - at.start), 4.0 * FAR, F32) for _ in heads)
        )
        index = lax.broadcasted_iota(jnp.int32, (1, rows), 1)
        live = jnp.concatenate(
            [
                jnp.where(index < sizes_ref[p.rep * GROUP + b], 1.0, 0.0) for b in blocks
            ],
            axis=1,
        )
        for h, head in enumerate(heads):
            whole = acc[h * HP + HD : h * HP + HD + 1, at]
            mixed_ref[head, at] = (acc[head, at] / whole).astype(BF)
            lse_ref[h : h + 1, at] = jnp.where(live > 0.0, tops[h] + jnp.log(whole) * LOG2E, 0.0)


def middle_kernel(
    capacity, reps, rows, deep, tok_ref, cot_ref, query_ref, mixed_ref, lse_ref, wo_ref, wup_ref,
    wdn_ref, upb_ref, outb_ref, gain_ref, shift_ref, downb_ref,
    out_ref, dres_ref, dmix_ref, stats_ref, qwin_ref, up_a, up_b, down_a, down_b, wo_a, wo_b,
    sums_ref, dupb_ref,
    part, part2, second, hidden, dbefore, dresall, dact, dwdn_a, dwdn_b, res_scr, norm_scr, held,
    asend, arecv, bsend, brecv, csend, crecv, dsend, drecv, esend, erecv, qsend, qrecv,
    hsend, hrecv, isend, irecv,
):
    p = Place(capacity, reps, rows)
    barrier, count = p.wide_barrier()
    count = count + p.halving_barrier()
    out_bias, gain, shift, down_bias = (
        ref[...][None, :] for ref in (outb_ref, gain_ref, shift_ref, downb_ref)
    )
    other = 1 - p.pair
    narrow = cot_ref.shape[1] // reps

    def attn_partial(owner):
        part[p.block(owner), :] = dot_over(
            mixed_ref[:, p.block(owner)], wo_ref[...], 0, 0
        ).astype(BF)

    attn_partial(p.diagonal)
    pl.semaphore_wait(barrier, count)
    one = Scatter(p, part, held.at[0], rows, asend, arecv)
    one.ahead().start()
    attn_partial(p.near)
    one.own().start()
    qwin_ref[pl.ds(OWN, GROUP)] = query_ref[...]
    queries = Exchange(p, lambda slot: qwin_ref.at[slot], qsend, qrecv)
    queries.start()
    attn_partial(p.far)
    one.pass_on()
    attn_partial(p.member)
    for pair in (0, 1):
        at = pl.ds(pair * 2 * rows, 2 * rows)
        dact[at, :] = dot_over(cot_ref[at, :], wdn_ref[...], 1, 1)
    resid = tok_ref[...].astype(F32) + one.result() + out_bias
    res_scr[...] = resid
    normed, inverse = norm_parts(resid)
    norm_scr[...] = normed
    second[p.block(p.member), :] = (normed * gain + shift).astype(BF)
    gather = Gather(p, second, rows, bsend, brecv)
    gather.start()

    def mlp(pair):
        at = p.pair_block(pair)
        before = dot_over(second[at, :], wup_ref[...], 1, 1) + upb_ref[pl.ds(p.member, 1), :]
        activated, derivative = gelu_parts(before)
        hidden[at, :] = activated.astype(BF)
        grad = dact[at, :] * derivative
        dact[at, :] = grad
        dbefore[at, :] = grad.astype(BF)
        part2[at, :] = dot_over(dbefore[at, :], wup_ref[...], 1, 0).astype(BF)

    gather.wait_near()
    gather.forward(0)
    mlp(p.pair)
    gather.forward(1)
    two = Scatter(p, part2, held.at[1], rows, csend, crecv)
    two.own().start()
    gather.wait_rest()
    mlp(other)
    two.ahead().start()
    grad_chunks(cot_ref, hidden, 0, (dwdn_a, dwdn_b), deep, narrow)
    order_a, order_b = orders(reps)
    halvings = (
        Halving(p, [dwdn_a, down_a], deep, order_a, hsend, hrecv),
        Halving(p, [dwdn_b, down_b], deep, order_b, isend, irecv),
    )
    for halving in halvings:
        halving.start(0)
    two.pass_on()

    def down(pair):
        at = p.pair_block(pair)
        part[at, :] = dot_over(hidden[at, :], wdn_ref[...], 1, 0).astype(BF)

    down(other)
    down(p.pair)
    three = Scatter(p, part, held.at[2], rows, esend, erecv)
    three.ahead().start()
    three.own().start()
    dsecond = two.result()
    own_cot = cot_ref[p.block(p.member), :].astype(F32)
    normed = norm_scr[...]
    dresid = own_cot + norm_backward(dsecond, normed, inverse, gain)
    dres_ref[...] = dresid
    dresall[p.block(p.member), :] = dresid.astype(BF)
    again = Gather(p, dresall, rows, dsend, drecv)
    again.start()
    three.pass_on()
    dupb_ref[...] = jnp.sum(dact[...], axis=0, keepdims=True)
    for i, term in enumerate((dresid, dsecond * normed, dsecond, own_cot)):
        sums_ref[pl.ds(i, 1), :] = jnp.sum(term, axis=0, keepdims=True)
    again.wait_near()
    again.forward(0)

    def mixed_grad(pair):
        at = p.pair_block(pair)
        dmixed = dot_over(wo_ref[...], dresall[at, :], 1, 1).astype(BF)
        dmix_ref[:, at] = dmixed
        product = dmixed.astype(F32) * mixed_ref[:, at].astype(F32)
        stats_ref[pl.ds(0, GROUP), at] = lse_ref[:, at]
        for h in range(GROUP):
            stats_ref[pl.ds(GROUP + h, 1), at] = jnp.sum(
                product[h * HP : (h + 1) * HP], axis=0, keepdims=True
            )

    grad_chunks(second, dbefore, 0, (up_a, up_b), deep, narrow)
    mixed_grad(p.pair)
    again.forward(1)
    again.wait_rest()
    mixed_grad(other)
    grad_chunks(dresall, mixed_ref, 1, (wo_a, wo_b), deep, narrow)
    out_ref[...] = (res_scr[...] + three.result() + down_bias).astype(BF)
    queries.wait()
    queries.drain()
    for halving in halvings:
        halving.finish(0)
        halving.drain(0)
    gather.drain()
    again.drain()


def back_kernel(
    capacity, reps, rows, deep, win_ref, qwin_ref, dmix_ref, stats_ref, first_ref, w_ref, tok_ref,
    dres_ref, gain_ref, up_a, up_b, down_a, down_b, wo_a, wo_b,
    grad_ref, dbias_ref, sums_ref, dup_out, ddn_out, dwo_out, dwi_out,
    dwin, swin, dq, dv, sbuf, dproj, part, held, *rest,
):
    steps = reps.bit_length() - 1
    scratch = list(rest)
    take = lambda n: [scratch.pop(0) for _ in range(n)]
    up_levels = [[ref] + take(steps) for ref in (up_a, up_b)]
    dn_levels = [[None, ref] + take(steps - 1) for ref in (down_a, down_b)]
    wo_levels = [[ref] + take(steps) for ref in (wo_a, wo_b)]
    wi_levels = [take(steps + 1) for _ in range(2)]
    (ksend, krecv, tsend, trecv, ssend, srecv, rsend, rrecv) = take(8)
    p = Place(capacity, reps, rows)
    barrier, count = p.wide_barrier()
    count = count + p.halving_barrier()
    for b in range(GROUP):
        at = slice(b * rows, (b + 1) * rows)
        dwin[OWN + b] = dmix_ref[:, at]
        swin[OWN + b] = stats_ref[:, at]
    pl.semaphore_wait(barrier, count)
    grads_in = Exchange(p, lambda slot: dwin.at[slot], ksend, krecv)
    stats_in = Exchange(p, lambda slot: swin.at[slot], tsend, trecv)
    grads_in.start()
    stats_in.start()
    down, up, inner, outer = (
        [Halving(p, refs, deep, order, *take(2)) for refs, order in zip(levels, orders(reps))]
        for levels in (dn_levels, up_levels, wi_levels, wo_levels)
    )
    work = [
        [one, first, (out, lanes)]
        for pair, first, out in (
            (down, 1, ddn_out), (up, 0, dup_out), (outer, 0, dwo_out), (inner, 0, dwi_out)
        )
        for one, lanes in zip(pair, split(out.shape[1]))
    ]

    def advance(some):
        for item in some:
            one, step, out = item
            if step < steps:
                one.finish(step, out if step == steps - 1 else None)
                if step + 1 < steps:
                    one.start(step + 1)
                item[1] = step + 1

    for one, step, _ in work[:6]:
        one.start(step)
    heads = [slice(h * HP, (h + 1) * HP) for h in range(GROUP)]
    every = range(GROUP)
    for blocks, at in pieces(rows):
        begin, stop = p.slots(blocks[0], blocks[-1] + 1)
        queries = [joined(lambda b: qwin_ref.at[OWN + b], head, blocks) for head in heads]
        dq[:, at] = jnp.zeros((dq.shape[0], at.stop - at.start), F32)

        def query_grads(slot, carry):
            keys = [win_ref[slot, head, :] for head in heads]
            raws = [dot_over(keys[h], queries[h], 0, 0) for h in every]
            dprobs = [
                dot_over(win_ref[WINDOW + slot, head, :], dmix_ref[head, at], 0, 0) for head in heads
            ]
            dscores = [
                (
                    jnp.exp2(raws[h] * (SCALE * LOG2E) - stats_ref[h : h + 1, at])
                    * (dprobs[h] - stats_ref[GROUP + h : GROUP + h + 1, at])
                ).astype(BF)
                for h in every
            ]
            for h, head in enumerate(heads):
                dq[head, at] += dot_over(keys[h], dscores[h], 1, 0)
            return carry

        lax.fori_loop(begin, stop, query_grads, 0)

    def owner_of(kind):
        c = kind * GROUP + p.member
        return lax.div(c, 3), lax.rem(c, 3)

    high = GROUP * HP

    def part_of(index):
        return pl.ds(pl.multiple_of(index * high, high), high)

    def home(kind):
        owner, index = owner_of(kind)
        return owner, remote(
            sbuf.at[kind], dproj.at[part_of(index), :], ssend.at[kind], srecv.at[index],
            (p.rep, owner),
        )

    def send_home(kind, grads, scale):
        value = grads[...] * scale
        sbuf[kind] = value.astype(BF)
        dbias_ref[:, kind : kind + 1] = jnp.sum(value, axis=1, keepdims=True)
        owner, copy = home(kind)

        @pl.when(owner != p.member)
        def _():
            copy.start()

    send_home(0, dq, SCALE)
    dk = dq
    grads_in.wait()
    stats_in.wait()
    for blocks, at in pieces(rows):
        begin, stop = p.slots(blocks[0], blocks[-1] + 1)
        keys = [joined(lambda b: win_ref.at[OWN + b], head, blocks) for head in heads]
        values = [joined(lambda b: win_ref.at[WINDOW + OWN + b], head, blocks) for head in heads]
        dk[:, at] = jnp.zeros((dk.shape[0], at.stop - at.start), F32)
        dv[:, at] = jnp.zeros((dv.shape[0], at.stop - at.start), F32)

        def key_grads(slot, carry):
            stats = jnp.transpose(swin[slot])
            picked = [qwin_ref[slot, head, :] for head in heads]
            dmixed = [dwin[slot, head, :] for head in heads]
            raws = [dot_over(picked[h], keys[h], 0, 0) for h in every]
            dprobs = [dot_over(dmixed[h], values[h], 0, 0) for h in every]
            probs = [jnp.exp2(raws[h] * (SCALE * LOG2E) - stats[:, h : h + 1]) for h in every]
            dscores = [
                (probs[h] * (dprobs[h] - stats[:, GROUP + h : GROUP + h + 1])).astype(BF)
                for h in every
            ]
            for h, head in enumerate(heads):
                dk[head, at] += dot_over(picked[h], dscores[h], 1, 0)
            for h, head in enumerate(heads):
                dv[head, at] += dot_over(dmixed[h], probs[h].astype(BF), 1, 0)
            return carry

        lax.fori_loop(begin, stop, key_grads, 0)

    send_home(1, dk, SCALE)
    send_home(2, dv, 1.0)
    for kind in range(3):
        owner, index = owner_of(kind)

        @pl.when(owner == p.member)
        def _():
            dproj[part_of(index), :] = sbuf[kind]

    advance(work[:4])
    for index in range(3):
        source = lax.rem(3 * p.member + index, GROUP)

        @pl.when(source != p.member)
        def _():
            remote(
                sbuf.at[0], dproj.at[part_of(index), :], ssend.at[0], srecv.at[index],
                (p.rep, p.near),
            ).wait_recv()

    narrow = first_ref.shape[1] // reps
    grad_chunks(first_ref, dproj, 1, [levels[0] for levels in wi_levels], deep, narrow)
    for one, step, _ in work[6:]:
        one.start(step)

    def partial(owner):
        part[p.block(owner), :] = dot_over(dproj[:, p.block(owner)], w_ref[...], 0, 0).astype(BF)

    scatter = Scatter(p, part, held, rows, rsend, rrecv)
    partial(p.diagonal)
    scatter.ahead().start()
    partial(p.near)
    scatter.own().start()
    partial(p.far)
    scatter.pass_on()
    partial(p.member)
    advance(work[:6])
    normed, inverse = norm_parts(tok_ref[...].astype(F32))
    dfirst = scatter.result()
    for i, term in enumerate((dfirst * normed, dfirst)):
        sums_ref[pl.ds(i, 1), :] = jnp.sum(term, axis=0, keepdims=True)
    grad_ref[...] = dres_ref[...] + norm_backward(dfirst, normed, inverse, gain_ref[...][None, :])
    for _ in range(steps):
        advance(work)
    for kind in range(3):
        owner, copy = home(kind)

        @pl.when(owner != p.member)
        def _():
            copy.wait_send()

    grads_in.drain()
    stats_in.drain()
    for pair, begin in ((down, 1), (up, 0), (inner, 0), (outer, 0)):
        for one in pair:
            for step in range(begin, steps):
                one.drain(step)


def total_kernel(reps, x_ref, o_ref, near, wide, send, recv):
    rep, member = lax.axis_index("rep"), lax.axis_index("grp")
    others = [(rep, lax.rem(member + d, GROUP)) for d in range(1, GROUP)]
    peers = [(lax.rem(rep + k, reps), member) for k in range(1, reps)]
    barrier = pltpu.get_barrier_semaphore()
    for place in others + peers:
        pl.semaphore_signal(barrier, inc=1, device_id=place, device_id_type=MESH)
    pl.semaphore_wait(barrier, len(others) + len(peers))
    lines = x_ref.shape[0] // GROUP

    def quarter(owner):
        return pl.ds(pl.multiple_of(owner * lines, lines), lines)

    def run(copies):
        for copy in copies:
            copy.start()
        for copy in copies:
            copy.wait_recv()

    gather = [
        remote(x_ref.at[quarter(place[1]), :], near.at[d], send.at[d], recv.at[d], place)
        for d, place in enumerate(others)
    ]
    run(gather)
    wide[rep] = x_ref[quarter(member), :] + near[0] + near[1] + near[2]
    base = len(others)
    across = [
        remote(wide.at[rep], wide.at[rep], send.at[base + k], recv.at[base + k], place)
        for k, place in enumerate(peers)
    ]
    run(across)
    total = wide[0]
    for r in range(1, reps):
        total = total + wide[r]
    o_ref[quarter(member), :] = total
    base = base + len(peers)
    share = [
        remote(
            o_ref.at[quarter(member), :], o_ref.at[quarter(member), :],
            send.at[base + d], recv.at[base + d], place,
        )
        for d, place in enumerate(others)
    ]
    run(share)
    for copy in gather + across + share:
        copy.wait_send()


def call(kernel, number, args, outs, scratch, smem=0, limit=63):
    vmem = pl.BlockSpec(memory_space=pltpu.VMEM)
    smem_spec = pl.BlockSpec(memory_space=pltpu.SMEM)
    linked = {} if number is None else {"collective_id": number, "has_side_effects": True}
    return pl.pallas_call(
        kernel,
        out_shape=[jax.ShapeDtypeStruct(*o) for o in outs],
        in_specs=[smem_spec] * smem + [vmem] * (len(args) - smem),
        out_specs=[vmem] * len(outs),
        scratch_shapes=scratch,
        compiler_params=pltpu.CompilerParams(vmem_limit_bytes=limit * 2**20, **linked),
    )(*args)


def per_device(
    tokens,
    cotangent,
    slice_sizes,
    gain_one,
    shift_one,
    attn_in,
    attn_bias,
    attn_out,
    out_bias,
    gain_two,
    shift_two,
    mlp_up,
    up_bias,
    mlp_down,
    down_bias,
):
    capacity, width = tokens.shape
    reps, groups = lax.axis_size("rep"), lax.axis_size("grp")
    assert groups == GROUP
    rows = -(-capacity // 128) * 128
    all_rows = GROUP * rows
    rep, member = lax.axis_index("rep"), lax.axis_index("grp")
    device = rep * groups + member
    ff_rows = mlp_up.shape[0]
    heads_high = GROUP * HP
    devices = reps * groups
    vm = pltpu.VMEM

    deep = -(-(width // reps) // 16) * 16
    own_count = slice_sizes[device]
    live_col = (jnp.arange(capacity, dtype=jnp.int32) < own_count)[:, None]
    w_in = jnp.pad(
        attn_in.reshape(3, GROUP, HD, width), ((0, 0), (0, 0), (0, HP - HD), (0, 0))
    ).reshape(3, heads_high, width)
    bias = jnp.stack([attn_bias[0], jnp.zeros((width,), F32), attn_bias[1]])
    bias = jnp.pad(
        bias.reshape(3 * GROUP, GROUP, HD), ((0, 0), (0, 0), (0, HP - HD))
    ).reshape(3 * GROUP, heads_high)
    w_out = jnp.pad(
        attn_out.reshape(GROUP, HD, width), ((0, 0), (0, HP - HD), (0, 0))
    ).reshape(heads_high, width)
    place = (capacity, reps, rows)
    window_sems = [
        pltpu.SemaphoreType.DMA((len(OFFSETS) * GROUP,)), pltpu.SemaphoreType.DMA((WINDOW,))
    ]

    first, tok, query, window, cot_all = call(
        functools.partial(front_kernel, *place), 1,
        (slice_sizes, tokens, cotangent, gain_one, shift_one, w_in, bias),
        [((all_rows, width), BF), ((rows, width), BF), ((GROUP, heads_high, rows), BF),
         ((2 * WINDOW + GROUP, heads_high, rows), BF), ((all_rows, width), BF)],
        [vm((all_rows, width), BF), vm((3, GROUP, heads_high, rows), BF),
         vm((3, heads_high, all_rows), F32), *dma(5), *dma(5), *dma(4), *window_sems * 2],
        smem=1,
    )
    mixed, lse = call(
        functools.partial(attend_kernel, *place), None, (slice_sizes, query, window),
        [((heads_high, all_rows), BF), ((GROUP, all_rows), F32)],
        [vm((heads_high, all_rows), F32)],
        smem=1,
    )
    gapped = reps * deep

    def halves(high, wide):
        return [((high, lanes.stop - lanes.start), BF) for lanes in split(wide)]

    out, dresid, dmixed, stats, qwindow, *partials, sums_two, dup = call(
        functools.partial(middle_kernel, *place, deep), 2,
        (tok, cot_all, query, mixed, lse, w_out, mlp_up, mlp_down,
         up_bias.reshape(GROUP, ff_rows), out_bias, gain_two, shift_two, down_bias),
        [((rows, width), BF), ((rows, width), F32), ((heads_high, all_rows), BF),
         ((2 * GROUP, all_rows), F32), ((WINDOW, heads_high, rows), BF), *halves(gapped, ff_rows),
         *halves(gapped // 2, ff_rows), *halves(gapped, heads_high), ((4, width), F32),
         ((1, ff_rows), F32)],
        [vm((all_rows, width), BF)] * 3
        + [vm((all_rows, ff_rows), BF)] * 2
        + [vm((all_rows, width), BF), vm((all_rows, ff_rows), F32), *[vm(*o) for o in halves(gapped, ff_rows)],
           vm((rows, width), F32), vm((rows, width), F32), vm((3, 3, rows, width), BF)]
        + dma(3) + dma(5) + dma(3) + dma(5) + dma(3) + window_sems + halving_sems(reps) * 2,
    )
    input_grad, dbias, sums_one, dmlp_up, dmlp_down, dattn_out, dattn_in = call(
        functools.partial(back_kernel, *place, deep), 3,
        (window, qwindow, dmixed, stats, first, w_in.reshape(3 * heads_high, width), tok, dresid,
         gain_one, *partials),
        [((rows, width), F32), ((heads_high, 3), F32), ((2, width), F32),
         ((deep, ff_rows), F32), ((deep, ff_rows), F32), ((deep, heads_high), F32),
         ((deep, 3 * heads_high), F32)],
        [vm((WINDOW, heads_high, rows), BF), vm((WINDOW, 2 * GROUP, rows), F32)]
        + [vm((heads_high, all_rows), F32)] * 2
        + [vm((3, heads_high, all_rows), BF), vm((3 * heads_high, all_rows), BF)]
        + [vm((all_rows, width), BF), vm((3, rows, width), BF)]
        + halving_levels(reps, deep, ff_rows, 1) + halving_levels(reps, deep, ff_rows, 2)
        + halving_levels(reps, deep, heads_high, 1)
        + halving_levels(reps, deep, 3 * heads_high, 0)
        + window_sems * 2 + dma(3) + dma(3) + halving_sems(reps) * 8,
    )
    narrow = width // reps
    dmlp_up, dmlp_down = dmlp_up[:narrow].T, dmlp_down[:narrow].T

    def without_gaps(grads):
        kinds = grads.shape[1] // heads_high
        return (
            grads[:narrow].T.reshape(kinds, GROUP, HP, narrow)[:, :, :HD]
            .reshape(kinds * GROUP * HD, narrow)
        )

    dattn_out, dattn_in = without_gaps(dattn_out), without_gaps(dattn_in)

    def totals(parts):
        flat = jnp.concatenate([part.reshape(-1) for part in parts])
        lines = -(-flat.shape[0] // 4096) * 32
        flat = jnp.pad(flat, (0, lines * 128 - flat.shape[0])).reshape(lines, 128)
        copies = 2 * (groups - 1) + reps - 1
        [summed] = call(
            functools.partial(total_kernel, reps), 0, (flat,), [(flat.shape, F32)],
            [vm((groups - 1, lines // groups, 128), F32), vm((reps, lines // groups, 128), F32),
             *dma(copies)], limit=16,
        )
        summed = summed.reshape(-1)
        spot, outs = 0, []
        for part in parts:
            outs.append(summed[spot : spot + part.size].reshape(part.shape))
            spot += part.size
        return outs

    dbias = dbias.T.reshape(3, GROUP, HP)[:, :, :HD].reshape(3, GROUP * HD)
    dattn_bias = lax.dynamic_update_slice_in_dim(
        jnp.zeros((2, width), F32), dbias[0::2], member * GROUP * HD, 1
    )
    dup_bias = lax.dynamic_update_slice_in_dim(
        jnp.zeros(up_bias.shape, F32), dup[0], member * ff_rows, 0
    )
    dgain_one, dshift_one, dattn_bias, dout_bias, dgain_two, dshift_two, dup_bias, ddown_bias = (
        totals(
            (
                sums_one[0], sums_one[1], dattn_bias, sums_two[0], sums_two[1], sums_two[2],
                dup_bias, sums_two[3],
            )
        )
    )
    block_output = jnp.where(live_col, out[:capacity], jnp.zeros((), BF))
    input_grad = jnp.where(live_col, input_grad[:capacity], 0.0)
    return (
        block_output, input_grad, dgain_one, dshift_one, dattn_in, dattn_bias, dattn_out,
        dout_bias, dgain_two, dshift_two, dmlp_up, dup_bias, dmlp_down, ddown_bias,
    )


def solution(mesh):
    rows, rep_grp = P("grp", None), P(("rep", "grp"), None)
    in_specs = (
        rep_grp, rep_grp, P(), P(), P(), rows, P(), rows, P(), P(), P(), rows, P(), rows, P(),
    )
    grads = P("grp", "rep")
    out_specs = (
        rep_grp, rep_grp, P(), P(), grads, P(), grads, P(), P(), P(), grads, P(), grads, P(),
    )
    return jax.shard_map(
        per_device, mesh=mesh, in_specs=in_specs, out_specs=out_specs, check_vma=False
    )
```

```python
import functools

import jax
import jax.numpy as jnp
from jax import lax
from jax.experimental import pallas as pl
from jax.experimental.pallas import tpu as pltpu
from jax.sharding import PartitionSpec as P

H = 16
HD = 72
HP = 80
IMG = 729
GROUP = 4
NEAR_GROUPS = 2
WINDOW = (2 * NEAR_GROUPS + 1) * GROUP
OWN = NEAR_GROUPS * GROUP
OFFSETS = (1, -1, 2, -2)

EPSILON = 1e-06
SQRT_TWO_PI = 0.7978845608028654
CUBIC = 0.044715
FAR = -(2.0**80)
SCALE = HD ** (-0.5)
LOG2E = 1.4426950408889634
BF = jnp.bfloat16
F32 = jnp.float32
MESH = pl.DeviceIdType.MESH


def norm_parts(rows):
    centered = rows - jnp.mean(rows, axis=-1, keepdims=True)
    inverse = lax.rsqrt(jnp.mean(centered * centered, axis=-1, keepdims=True) + EPSILON)
    return centered * inverse, inverse


def norm_backward(dscaled, normed, inverse, gain_row):
    dnormed = dscaled * gain_row
    return inverse * (
        dnormed
        - jnp.mean(dnormed, axis=-1, keepdims=True)
        - normed * jnp.mean(dnormed * normed, axis=-1, keepdims=True)
    )


def gelu_parts(before):
    square = before * before
    tangent = jnp.tanh(SQRT_TWO_PI * before * (1.0 + CUBIC * square))
    half = 0.5 * (1.0 + tangent)
    derivative = half + 0.5 * before * (1.0 - tangent * tangent) * (
        SQRT_TWO_PI + SQRT_TWO_PI * 3.0 * CUBIC * square
    )
    return before * half, derivative


def dot_over(left, right, left_axis, right_axis):
    return lax.dot_general(
        left, right, (((left_axis,), (right_axis,)), ((), ())), preferred_element_type=F32
    )


def flipped(index, bit):
    return index + bit * (1 - 2 * ((index // bit) % 2))


def doublings(count):
    return [1 << i for i in range(count.bit_length() - 1)]


class Place:
    def __init__(self, capacity, reps, rows):
        self.capacity, self.reps, self.rows = capacity, reps, rows
        self.devices = reps * GROUP
        self.images = capacity * self.devices // IMG
        self.short = capacity * self.devices - self.images * IMG
        self.rep, self.member = lax.axis_index("rep"), lax.axis_index("grp")
        low = lax.rem(self.member, 2)
        self.near = self.member + 1 - 2 * low
        self.far = lax.rem(self.member + 2, GROUP)
        self.diagonal = lax.rem(self.near + 2, GROUP)
        self.pair = lax.div(self.member, 2)

    def sharing(self, low, high):
        capacity, short, image = self.capacity, self.short, jnp.int32(IMG)
        start = low * capacity - jnp.minimum(low, short)
        end = high * capacity - jnp.maximum(high - (self.devices - short), 0) - 1
        first = lax.div(start, image) * IMG
        after = (jnp.minimum(lax.div(end, image), self.images - 1) + 1) * IMG
        begin = lax.div(first, jnp.int32(capacity))
        stop = jnp.minimum(
            lax.div(after + short + capacity - 1, jnp.int32(capacity)),
            lax.div(after + capacity - 2, jnp.int32(capacity - 1)),
        )
        return begin, jnp.minimum(stop, self.devices)

    def slots(self, low, high):
        base = self.rep * GROUP
        begin, stop = self.sharing(base + low, base + high)
        return jnp.maximum(begin - base + OWN, 0), jnp.minimum(stop - base + OWN, WINDOW)

    def shares(self, block, group):
        begin, stop = self.sharing(group * GROUP, group * GROUP + GROUP)
        return (group >= 0) & (group < self.reps) & (block >= begin) & (block < stop)

    def block(self, owner):
        return pl.ds(pl.multiple_of(owner * self.rows, self.rows), self.rows)

    def pair_block(self, pair):
        return pl.ds(pl.multiple_of(pair * 2 * self.rows, 2 * self.rows), 2 * self.rows)

    def halving_barrier(self):
        barrier = pltpu.get_barrier_semaphore()
        bits = doublings(self.reps)
        for bit in bits:
            pl.semaphore_signal(
                barrier, inc=1, device_id=(flipped(self.rep, bit), self.member),
                device_id_type=MESH,
            )
        return len(bits)

    def group_barrier(self):
        barrier = pltpu.get_barrier_semaphore()
        for other in (self.near, self.far):
            pl.semaphore_signal(
                barrier, inc=1, device_id=(self.rep, other), device_id_type=MESH
            )
        return barrier, 2

    def wide_barrier(self):
        barrier, count = self.group_barrier()
        count = jnp.int32(count)
        for offset in OFFSETS:
            there = self.rep + offset
            valid = (there >= 0) & (there < self.reps)

            @pl.when(valid)
            def _():
                pl.semaphore_signal(
                    barrier, inc=1, device_id=(there, self.member), device_id_type=MESH
                )

            count = count + jnp.where(valid, 1, 0)
        return barrier, count


def remote(source, target, send, recv, place):
    return pltpu.make_async_remote_copy(
        src_ref=source,
        dst_ref=target,
        send_sem=send,
        recv_sem=recv,
        device_id=place,
        device_id_type=MESH,
    )


class Gather:
    def __init__(self, place, ref, rows, send, recv):
        self.place, self.ref, self.rows, self.send, self.recv = place, ref, rows, send, recv
        self.half = rows // 2

    def copy(self, owner, part, slot, target):
        if part is None:
            piece = self.ref.at[pl.ds(pl.multiple_of(owner * self.rows, self.rows), self.rows), :]
        else:
            start = pl.multiple_of(owner * self.rows + part * self.half, self.half)
            piece = self.ref.at[pl.ds(start, self.half), :]
        return remote(
            piece, piece, self.send.at[slot], self.recv.at[slot], (self.place.rep, target)
        )

    def start(self):
        p = self.place
        for part in range(2):
            self.copy(p.member, part, 1 + part, p.far).start()
        self.copy(p.member, None, 0, p.near).start()

    def wait_near(self):
        p = self.place
        self.copy(p.near, None, 0, p.near).wait_recv()

    def forward(self, part):
        p = self.place
        self.copy(p.far, part, 1 + part, p.far).wait_recv()
        self.copy(p.far, part, 3 + part, p.near).start()

    def wait_rest(self):
        p = self.place
        for part in range(2):
            self.copy(p.diagonal, part, 3 + part, p.near).wait_recv()

    def drain(self):
        p = self.place
        self.copy(p.member, None, 0, p.near).wait_send()
        for part in range(2):
            self.copy(p.member, part, 1 + part, p.far).wait_send()
            self.copy(p.far, part, 3 + part, p.near).wait_send()


class Scatter:
    def __init__(self, place, ref, held, rows, send, recv):
        self.place, self.ref, self.held = place, ref, held
        self.rows, self.send, self.recv = rows, send, recv

    def block(self, owner):
        return pl.ds(pl.multiple_of(owner * self.rows, self.rows), self.rows)

    def ahead(self):
        p = self.place
        return remote(
            self.ref.at[self.block(p.diagonal), :], self.held.at[0],
            self.send.at[0], self.recv.at[0], (p.rep, p.near),
        )

    def own(self):
        p = self.place
        return remote(
            self.ref.at[self.block(p.near), :], self.held.at[1],
            self.send.at[1], self.recv.at[1], (p.rep, p.near),
        )

    def across(self):
        p = self.place
        return remote(
            self.held.at[0], self.held.at[2], self.send.at[2], self.recv.at[2], (p.rep, p.far)
        )

    def pass_on(self):
        p = self.place
        self.ahead().wait_recv()
        self.held[0] = (
            self.ref[self.block(p.far), :].astype(F32) + self.held[0].astype(F32)
        ).astype(BF)
        self.across().start()

    def result(self):
        p = self.place
        self.own().wait_recv()
        total = self.ref[self.block(p.member), :].astype(F32) + self.held[1].astype(F32)
        self.across().wait_recv()
        total = total + self.held[2].astype(F32)
        self.ahead().wait_send()
        self.own().wait_send()
        self.across().wait_send()
        return total


class Exchange:
    def __init__(self, place, view, send, recv):
        self.place, self.view, self.send, self.recv = place, view, send, recv

    def outgoing(self, act):
        p = self.place
        for number, offset in enumerate(OFFSETS):
            begin, stop = p.sharing((p.rep + offset) * GROUP, (p.rep + offset + 1) * GROUP)
            valid = (p.rep + offset >= 0) & (p.rep + offset < p.reps)
            for index in range(GROUP):
                block = p.rep * GROUP + index
                slot_there = OWN - offset * GROUP + index

                @pl.when(valid & (block >= begin) & (block < stop))
                def _():
                    act(
                        remote(
                            self.view(OWN + index),
                            self.view(slot_there),
                            self.send.at[number * GROUP + index],
                            self.recv.at[slot_there],
                            (p.rep + offset, p.member),
                        )
                    )

    def start(self):
        self.outgoing(lambda copy: copy.start())

    def drain(self):
        self.outgoing(lambda copy: copy.wait_send())

    def wait(self):
        p = self.place
        begin, stop = p.slots(0, GROUP)
        for offset in OFFSETS:
            for index in range(GROUP):
                slot = OWN + offset * GROUP + index

                @pl.when((slot >= begin) & (slot < stop))
                def _():
                    remote(
                        self.view(slot), self.view(slot), self.send.at[0], self.recv.at[slot],
                        (p.rep, p.near),
                    ).wait_recv()


def dma(count):
    return [pltpu.SemaphoreType.DMA((count,))] * 2


class Halving:
    def __init__(self, place, levels, deep, bits, send, recv):
        self.place, self.levels, self.deep = place, levels, deep
        self.send, self.recv = send, recv
        self.bits = bits

    def mine(self, step):
        return lax.rem(lax.div(self.place.rep, jnp.int32(self.bits[step])), 2)

    def partner(self, step):
        p = self.place
        return (flipped(p.rep, self.bits[step]), p.member)

    def rows(self, start, count):
        return pl.ds(pl.multiple_of(start * self.deep, self.deep), count * self.deep)

    def firsts(self):
        rest = self.bits[1:]
        for j in range(self.place.reps // 2):
            yield j, sum(bit * ((j >> (len(rest) - 1 - q)) & 1) for q, bit in enumerate(rest))

    def copies(self, step):
        give = 1 - self.mine(step)
        source, target = self.levels[step], self.levels[step + 1]
        if step == 0:
            return [
                remote(
                    source.at[self.rows(give * self.bits[0] + offset, 1), :],
                    target.at[self.rows(j, 1), :],
                    self.send.at[j], self.recv.at[j], self.partner(0),
                )
                for j, offset in self.firsts()
            ]
        half = self.place.reps >> (step + 1)
        slot = self.place.reps // 2 + step - 1
        return [
            remote(
                source.at[self.rows(give * half, half), :], target.at[self.rows(0, half), :],
                self.send.at[slot], self.recv.at[slot], self.partner(step),
            )
        ]

    def start(self, step):
        for copy in self.copies(step):
            copy.start()

    def finish(self, step, out=None):
        copies = self.copies(step)
        mine = self.mine(step)
        source, target = self.levels[step], self.levels[step + 1]
        half = self.place.reps >> (step + 1)
        if step == 0:
            for j, offset in self.firsts():
                copies[j].wait_recv()
                at = self.rows(j, 1)
                kept = source[self.rows(mine * self.bits[0] + offset, 1), :]
                target[at, :] = (target[at, :].astype(F32) + kept.astype(F32)).astype(BF)
            return
        copies[0].wait_recv()
        for j in range(half):
            at = self.rows(j, 1)
            kept = source[self.rows(mine * half + j, 1), :]
            total = target[at, :].astype(F32) + kept.astype(F32)
            if out is None:
                target[at, :] = total.astype(BF)
            else:
                ref, lanes = out
                ref[:, lanes] = total

    def drain(self, step):
        for copy in self.copies(step):
            copy.wait_send()


def orders(reps):
    bits = doublings(reps)
    return bits, bits[1:2] + bits[:1] + bits[2:]


def split(wide):
    cut = -(-wide // 256) * 128
    return slice(0, cut), slice(cut, wide)


def halving_sems(reps):
    return dma(reps // 2 + reps.bit_length() - 2)


def halving_levels(reps, deep, wide, first):
    return [
        pltpu.VMEM(((reps >> s) * deep, lanes.stop - lanes.start), BF)
        for lanes in split(wide)
        for s in range(first, reps.bit_length())
    ]


def grad_chunks(left, right, right_axis, targets, deep, narrow):
    chunk = 128
    width = left.shape[1]

    def body(i, carry):
        at = pl.ds(pl.multiple_of(i * chunk, chunk), chunk)
        if deep == narrow:
            columns = left[:, at]
        else:
            source = lax.broadcasted_iota(jnp.int32, (width, chunk), 0)
            column = lax.broadcasted_iota(jnp.int32, (width, chunk), 1) + i * chunk
            within = column % deep
            picked = (source == (column // deep) * narrow + within) & (within < narrow)
            columns = dot_over(left[...], jnp.where(picked, 1.0, 0.0).astype(BF), 1, 0).astype(BF)
        product = dot_over(columns, right[...], 0, right_axis).astype(BF)
        for target, lanes in zip(targets, split(product.shape[1])):
            target[at, :] = product[:, lanes]
        return carry

    lax.fori_loop(0, targets[0].shape[0] // chunk, body, 0)


def image_codes(place, sizes_ref, kind):
    start = lax.fori_loop(0, place.rep * GROUP, lambda i, n: n + sizes_ref[i], jnp.int32(0))
    index = lax.broadcasted_iota(jnp.int32, (8, place.rows), 1)
    row = lax.broadcasted_iota(jnp.int32, (8, place.rows), 0)
    codes = []
    for b in range(GROUP):
        size = sizes_ref[place.rep * GROUP + b]
        base = lax.div(start, jnp.int32(IMG))
        turn = (base + 1) * IMG - start
        kind_of_image = lax.rem(base + jnp.where(index >= turn, 1, 0), 4)
        live = index < size
        same = kind_of_image == row
        query = jnp.where(same | ~live, 1.0, 0.0)
        key = jnp.where(same & live, 0.0, FAR)
        code = jnp.where(kind == 0, query, key)
        code = jnp.where(row < 4, code, 0.0)
        codes.append(jnp.where(kind == 2, jnp.where(row == 0, 1.0, 0.0), code))
        start = start + size
    return codes


def front_kernel(
    capacity, reps, rows, sizes_ref, tok_ref, cot_ref, gain_ref, shift_ref, w_ref, bias_ref,
    first_ref, own_ref, query_ref, win_ref, cotall_ref,
    xall, sbuf, code, gsend, grecv, csend, crecv, ssend, srecv, ksend, krecv, vsend, vrecv,
):
    p = Place(capacity, reps, rows)
    barrier, count = p.wide_barrier()
    size = sizes_ref[p.rep * GROUP + p.member]
    live = lax.broadcasted_iota(jnp.int32, (capacity, 1), 0) < size
    clean = lambda ref: jnp.where(live, ref[...].astype(F32), 0.0).astype(BF)
    own_ref[...] = jnp.zeros_like(own_ref)
    own_ref[pl.ds(0, capacity), :] = clean(tok_ref)
    xall[p.block(p.member), :] = own_ref[...]
    pl.semaphore_wait(barrier, count)
    tokens = Gather(p, xall, rows, gsend, grecv)
    tokens.start()
    cotall_ref[p.block(p.member), :] = jnp.zeros((rows, tok_ref.shape[1]), BF)
    cotall_ref[pl.ds(pl.multiple_of(p.member * rows, rows), capacity), :] = clean(cot_ref)
    gain, shift = gain_ref[...][None, :], shift_ref[...][None, :]

    def normalize(owner):
        block = p.block(owner)
        normed, _ = norm_parts(xall[block, :].astype(F32))
        first_ref[block, :] = (normed * gain + shift).astype(BF)

    odd = lax.rem(p.member, 2)
    cross = 2 - 2 * odd
    kept = 2 * odd
    kind_of = lambda i: lax.div(3 * p.member + i, GROUP)
    def spot_of(i):
        kind = kind_of(i)
        return jnp.where(kind == 0, 2 * WINDOW, (kind - 1) * WINDOW + OWN)

    gap = jnp.zeros((HD, rows), F32)
    for i in range(3):
        for b, rest in enumerate(image_codes(p, sizes_ref, kind_of(i))):
            at = slice(b * rows, (b + 1) * rows)
            for h in range(GROUP):
                code[i, h * HP : (h + 1) * HP, at] = jnp.concatenate([gap, rest], axis=0)

    def project(i, pair):
        block = first_ref[p.pair_block(pair), :]
        bias = bias_ref[pl.ds(3 * p.member + i, 1), :]
        bias = jnp.transpose(jnp.broadcast_to(bias, (8, bias.shape[1])))[:, 0:1]
        total = dot_over(w_ref[i], block, 1, 1) + bias + code[i, :, p.pair_block(pair)]
        for b in range(2):
            sbuf[i, pair * 2 + b] = total[:, b * rows : (b + 1) * rows].astype(BF)

    def shuffle(i, pair, way, target):
        slot = way * 2 + pair
        return remote(
            sbuf.at[i, pl.ds(pair * 2, 2)],
            win_ref.at[pl.ds(spot_of(i) + pair * 2, 2)],
            ssend.at[slot], srecv.at[slot], (p.rep, target),
        )

    normalize(p.member)
    tokens.wait_near()
    normalize(p.near)
    tokens.forward(0)
    project(cross, p.pair)
    shuffle(cross, p.pair, 0, p.far).start()
    tokens.forward(1)
    project(1, p.pair)
    shuffle(1, p.pair, 1, p.near).start()
    project(kept, p.pair)
    other = 1 - p.pair
    normalize(p.far)
    tokens.wait_rest()
    normalize(p.diagonal)
    project(cross, other)
    shuffle(cross, other, 0, p.far).start()
    project(1, other)
    shuffle(1, other, 1, p.near).start()
    project(kept, other)
    win_ref[pl.ds(spot_of(kept), GROUP)] = sbuf[kept]
    for pair in (p.pair, other):
        shuffle(cross, pair, 0, p.far).wait_recv()
        shuffle(1, pair, 1, p.near).wait_recv()
    keys = Exchange(p, lambda slot: win_ref.at[slot], ksend, krecv)
    values = Exchange(p, lambda slot: win_ref.at[WINDOW + slot], vsend, vrecv)
    keys.start()
    values.start()
    cotangents = Gather(p, cotall_ref, rows, csend, crecv)
    cotangents.start()
    query_ref[...] = win_ref[pl.ds(2 * WINDOW, GROUP)]
    cotangents.wait_near()
    cotangents.forward(0)
    cotangents.forward(1)
    cotangents.wait_rest()
    keys.wait()
    values.wait()
    keys.drain()
    values.drain()
    for pair in (p.pair, other):
        shuffle(cross, pair, 0, p.far).wait_send()
        shuffle(1, pair, 1, p.near).wait_send()
    tokens.drain()
    cotangents.drain()


def joined(view, head, blocks):
    return jnp.concatenate([view(b)[head, :] for b in blocks], axis=1)


def pieces(rows):
    count = max(512 // rows, 1)
    for low in range(0, GROUP, count):
        yield range(low, low + count), slice(low * rows, (low + count) * rows)


def attend_kernel(capacity, reps, rows, sizes_ref, query_ref, win_ref, mixed_ref, lse_ref, acc):
    p = Place(capacity, reps, rows)
    heads = [slice(h * HP, (h + 1) * HP) for h in range(GROUP)]
    for blocks, at in pieces(rows):
        begin, stop = p.slots(blocks[0], blocks[-1] + 1)
        acc[:, at] = jnp.zeros((acc.shape[0], at.stop - at.start), F32)
        queries = [joined(lambda b: query_ref.at[b], head, blocks) for head in heads]

        def attend(slot, tops):
            raws = [dot_over(win_ref[slot, head, :], query, 0, 0) for head, query in zip(heads, queries)]
            news = [
                jnp.maximum(top, jnp.max(raw, axis=0, keepdims=True) * (SCALE * LOG2E))
                for top, raw in zip(tops, raws)
            ]
            powers = [
                jnp.exp2(raw * (SCALE * LOG2E) - new).astype(BF) for raw, new in zip(raws, news)
            ]
            for head, top, new, power in zip(heads, tops, news, powers):
                value = win_ref[WINDOW + slot, head, :]
                acc[head, at] = acc[head, at] * jnp.exp2(top - new) + dot_over(value, power, 1, 0)
            return tuple(news)

        tops = lax.fori_loop(
            begin, stop, attend, tuple(jnp.full((1, at.stop - at.start), 4.0 * FAR, F32) for _ in heads)
        )
        index = lax.broadcasted_iota(jnp.int32, (1, rows), 1)
        live = jnp.concatenate(
            [
                jnp.where(index < sizes_ref[p.rep * GROUP + b], 1.0, 0.0) for b in blocks
            ],
            axis=1,
        )
        for h, head in enumerate(heads):
            whole = acc[h * HP + HD : h * HP + HD + 1, at]
            mixed_ref[head, at] = (acc[head, at] / whole).astype(BF)
            lse_ref[h : h + 1, at] = jnp.where(live > 0.0, tops[h] + jnp.log(whole) * LOG2E, 0.0)


def middle_kernel(
    capacity, reps, rows, deep, tok_ref, cot_ref, query_ref, mixed_ref, lse_ref, wo_ref, wup_ref,
    wdn_ref, upb_ref, outb_ref, gain_ref, shift_ref, downb_ref,
    out_ref, dres_ref, dmix_ref, stats_ref, qwin_ref, up_a, up_b, down_a, down_b, wo_a, wo_b,
    sums_ref, dupb_ref,
    part, part2, second, hidden, dbefore, dresall, dact, dwdn_a, dwdn_b, res_scr, norm_scr, held,
    asend, arecv, bsend, brecv, csend, crecv, dsend, drecv, esend, erecv, qsend, qrecv,
    hsend, hrecv, isend, irecv,
):
    p = Place(capacity, reps, rows)
    barrier, count = p.wide_barrier()
    count = count + p.halving_barrier()
    out_bias, gain, shift, down_bias = (
        ref[...][None, :] for ref in (outb_ref, gain_ref, shift_ref, downb_ref)
    )
    other = 1 - p.pair
    narrow = cot_ref.shape[1] // reps

    def attn_partial(owner):
        part[p.block(owner), :] = dot_over(
            mixed_ref[:, p.block(owner)], wo_ref[...], 0, 0
        ).astype(BF)

    attn_partial(p.diagonal)
    pl.semaphore_wait(barrier, count)
    one = Scatter(p, part, held.at[0], rows, asend, arecv)
    one.ahead().start()
    attn_partial(p.near)
    one.own().start()
    qwin_ref[pl.ds(OWN, GROUP)] = query_ref[...]
    queries = Exchange(p, lambda slot: qwin_ref.at[slot], qsend, qrecv)
    queries.start()
    attn_partial(p.far)
    one.pass_on()
    attn_partial(p.member)
    for pair in (0, 1):
        at = pl.ds(pair * 2 * rows, 2 * rows)
        dact[at, :] = dot_over(cot_ref[at, :], wdn_ref[...], 1, 1)
    resid = tok_ref[...].astype(F32) + one.result() + out_bias
    res_scr[...] = resid
    normed, inverse = norm_parts(resid)
    norm_scr[...] = normed
    second[p.block(p.member), :] = (normed * gain + shift).astype(BF)
    gather = Gather(p, second, rows, bsend, brecv)
    gather.start()

    def mlp(pair):
        at = p.pair_block(pair)
        before = dot_over(second[at, :], wup_ref[...], 1, 1) + upb_ref[pl.ds(p.member, 1), :]
        activated, derivative = gelu_parts(before)
        hidden[at, :] = activated.astype(BF)
        grad = dact[at, :] * derivative
        dact[at, :] = grad
        dbefore[at, :] = grad.astype(BF)
        part2[at, :] = dot_over(dbefore[at, :], wup_ref[...], 1, 0).astype(BF)

    gather.wait_near()
    gather.forward(0)
    mlp(p.pair)
    gather.forward(1)
    two = Scatter(p, part2, held.at[1], rows, csend, crecv)
    two.own().start()
    gather.wait_rest()
    mlp(other)
    two.ahead().start()
    grad_chunks(cot_ref, hidden, 0, (dwdn_a, dwdn_b), deep, narrow)
    order_a, order_b = orders(reps)
    halvings = (
        Halving(p, [dwdn_a, down_a], deep, order_a, hsend, hrecv),
        Halving(p, [dwdn_b, down_b], deep, order_b, isend, irecv),
    )
    for halving in halvings:
        halving.start(0)
    two.pass_on()

    def down(pair):
        at = p.pair_block(pair)
        part[at, :] = dot_over(hidden[at, :], wdn_ref[...], 1, 0).astype(BF)

    down(other)
    down(p.pair)
    three = Scatter(p, part, held.at[2], rows, esend, erecv)
    three.ahead().start()
    three.own().start()
    dsecond = two.result()
    own_cot = cot_ref[p.block(p.member), :].astype(F32)
    normed = norm_scr[...]
    dresid = own_cot + norm_backward(dsecond, normed, inverse, gain)
    dres_ref[...] = dresid
    dresall[p.block(p.member), :] = dresid.astype(BF)
    again = Gather(p, dresall, rows, dsend, drecv)
    again.start()
    three.pass_on()
    dupb_ref[...] = jnp.sum(dact[...], axis=0, keepdims=True)
    for i, term in enumerate((dresid, dsecond * normed, dsecond, own_cot)):
        sums_ref[pl.ds(i, 1), :] = jnp.sum(term, axis=0, keepdims=True)
    again.wait_near()
    again.forward(0)

    def mixed_grad(pair):
        at = p.pair_block(pair)
        dmixed = dot_over(wo_ref[...], dresall[at, :], 1, 1).astype(BF)
        dmix_ref[:, at] = dmixed
        product = dmixed.astype(F32) * mixed_ref[:, at].astype(F32)
        stats_ref[pl.ds(0, GROUP), at] = lse_ref[:, at]
        for h in range(GROUP):
            stats_ref[pl.ds(GROUP + h, 1), at] = jnp.sum(
                product[h * HP : (h + 1) * HP], axis=0, keepdims=True
            )

    grad_chunks(second, dbefore, 0, (up_a, up_b), deep, narrow)
    mixed_grad(p.pair)
    again.forward(1)
    again.wait_rest()
    mixed_grad(other)
    grad_chunks(dresall, mixed_ref, 1, (wo_a, wo_b), deep, narrow)
    out_ref[...] = (res_scr[...] + three.result() + down_bias).astype(BF)
    queries.wait()
    queries.drain()
    for halving in halvings:
        halving.finish(0)
        halving.drain(0)
    gather.drain()
    again.drain()


def back_kernel(
    capacity, reps, rows, deep, win_ref, qwin_ref, dmix_ref, stats_ref, first_ref, w_ref, tok_ref,
    dres_ref, gain_ref, up_a, up_b, down_a, down_b, wo_a, wo_b,
    grad_ref, dbias_ref, sums_ref, dup_out, ddn_out, dwo_out, dwi_out,
    dwin, swin, dq, dv, sbuf, dproj, part, held, *rest,
):
    steps = reps.bit_length() - 1
    scratch = list(rest)
    take = lambda n: [scratch.pop(0) for _ in range(n)]
    up_levels = [[ref] + take(steps) for ref in (up_a, up_b)]
    dn_levels = [[None, ref] + take(steps - 1) for ref in (down_a, down_b)]
    wo_levels = [[ref] + take(steps) for ref in (wo_a, wo_b)]
    wi_levels = [take(steps + 1) for _ in range(2)]
    (ksend, krecv, tsend, trecv, ssend, srecv, rsend, rrecv) = take(8)
    p = Place(capacity, reps, rows)
    barrier, count = p.wide_barrier()
    count = count + p.halving_barrier()
    for b in range(GROUP):
        at = slice(b * rows, (b + 1) * rows)
        dwin[OWN + b] = dmix_ref[:, at]
        swin[OWN + b] = stats_ref[:, at]
    pl.semaphore_wait(barrier, count)
    grads_in = Exchange(p, lambda slot: dwin.at[slot], ksend, krecv)
    stats_in = Exchange(p, lambda slot: swin.at[slot], tsend, trecv)
    grads_in.start()
    stats_in.start()
    down, up, inner, outer = (
        [Halving(p, refs, deep, order, *take(2)) for refs, order in zip(levels, orders(reps))]
        for levels in (dn_levels, up_levels, wi_levels, wo_levels)
    )
    work = [
        [one, first, (out, lanes)]
        for pair, first, out in (
            (down, 1, ddn_out), (up, 0, dup_out), (outer, 0, dwo_out), (inner, 0, dwi_out)
        )
        for one, lanes in zip(pair, split(out.shape[1]))
    ]

    def advance(some):
        for item in some:
            one, step, out = item
            if step < steps:
                one.finish(step, out if step == steps - 1 else None)
                if step + 1 < steps:
                    one.start(step + 1)
                item[1] = step + 1

    for one, step, _ in work[:6]:
        one.start(step)
    heads = [slice(h * HP, (h + 1) * HP) for h in range(GROUP)]
    every = range(GROUP)
    for blocks, at in pieces(rows):
        begin, stop = p.slots(blocks[0], blocks[-1] + 1)
        queries = [joined(lambda b: qwin_ref.at[OWN + b], head, blocks) for head in heads]
        dq[:, at] = jnp.zeros((dq.shape[0], at.stop - at.start), F32)

        def query_grads(slot, carry):
            keys = [win_ref[slot, head, :] for head in heads]
            raws = [dot_over(keys[h], queries[h], 0, 0) for h in every]
            dprobs = [
                dot_over(win_ref[WINDOW + slot, head, :], dmix_ref[head, at], 0, 0) for head in heads
            ]
            dscores = [
                (
                    jnp.exp2(raws[h] * (SCALE * LOG2E) - stats_ref[h : h + 1, at])
                    * (dprobs[h] - stats_ref[GROUP + h : GROUP + h + 1, at])
                ).astype(BF)
                for h in every
            ]
            for h, head in enumerate(heads):
                dq[head, at] += dot_over(keys[h], dscores[h], 1, 0)
            return carry

        lax.fori_loop(begin, stop, query_grads, 0)

    def owner_of(kind):
        c = kind * GROUP + p.member
        return lax.div(c, 3), lax.rem(c, 3)

    high = GROUP * HP

    def part_of(index):
        return pl.ds(pl.multiple_of(index * high, high), high)

    def home(kind):
        owner, index = owner_of(kind)
        return owner, remote(
            sbuf.at[kind], dproj.at[part_of(index), :], ssend.at[kind], srecv.at[index],
            (p.rep, owner),
        )

    def send_home(kind, grads, scale):
        value = grads[...] * scale
        sbuf[kind] = value.astype(BF)
        dbias_ref[:, kind : kind + 1] = jnp.sum(value, axis=1, keepdims=True)
        owner, copy = home(kind)

        @pl.when(owner != p.member)
        def _():
            copy.start()

    send_home(0, dq, SCALE)
    dk = dq
    grads_in.wait()
    stats_in.wait()
    advance(work[:2])
    for blocks, at in pieces(rows):
        begin, stop = p.slots(blocks[0], blocks[-1] + 1)
        keys = [joined(lambda b: win_ref.at[OWN + b], head, blocks) for head in heads]
        values = [joined(lambda b: win_ref.at[WINDOW + OWN + b], head, blocks) for head in heads]
        dk[:, at] = jnp.zeros((dk.shape[0], at.stop - at.start), F32)
        dv[:, at] = jnp.zeros((dv.shape[0], at.stop - at.start), F32)

        def key_grads(slot, carry):
            stats = jnp.transpose(swin[slot])
            picked = [qwin_ref[slot, head, :] for head in heads]
            dmixed = [dwin[slot, head, :] for head in heads]
            raws = [dot_over(picked[h], keys[h], 0, 0) for h in every]
            dprobs = [dot_over(dmixed[h], values[h], 0, 0) for h in every]
            probs = [jnp.exp2(raws[h] * (SCALE * LOG2E) - stats[:, h : h + 1]) for h in every]
            dscores = [
                (probs[h] * (dprobs[h] - stats[:, GROUP + h : GROUP + h + 1])).astype(BF)
                for h in every
            ]
            for h, head in enumerate(heads):
                dk[head, at] += dot_over(picked[h], dscores[h], 1, 0)
            for h, head in enumerate(heads):
                dv[head, at] += dot_over(dmixed[h], probs[h].astype(BF), 1, 0)
            return carry

        lax.fori_loop(begin, stop, key_grads, 0)

    send_home(1, dk, SCALE)
    send_home(2, dv, 1.0)
    for kind in range(3):
        owner, index = owner_of(kind)

        @pl.when(owner == p.member)
        def _():
            dproj[part_of(index), :] = sbuf[kind]

    advance(work[:6])
    for index in range(3):
        source = lax.rem(3 * p.member + index, GROUP)

        @pl.when(source != p.member)
        def _():
            remote(
                sbuf.at[0], dproj.at[part_of(index), :], ssend.at[0], srecv.at[index],
                (p.rep, p.near),
            ).wait_recv()

    narrow = first_ref.shape[1] // reps
    grad_chunks(first_ref, dproj, 1, [levels[0] for levels in wi_levels], deep, narrow)
    for one, step, _ in work[6:]:
        one.start(step)

    def partial(owner):
        part[p.block(owner), :] = dot_over(dproj[:, p.block(owner)], w_ref[...], 0, 0).astype(BF)

    scatter = Scatter(p, part, held, rows, rsend, rrecv)
    partial(p.diagonal)
    scatter.ahead().start()
    partial(p.near)
    scatter.own().start()
    partial(p.far)
    scatter.pass_on()
    partial(p.member)
    advance(work[:6])
    normed, inverse = norm_parts(tok_ref[...].astype(F32))
    dfirst = scatter.result()
    for i, term in enumerate((dfirst * normed, dfirst)):
        sums_ref[pl.ds(i, 1), :] = jnp.sum(term, axis=0, keepdims=True)
    grad_ref[...] = dres_ref[...] + norm_backward(dfirst, normed, inverse, gain_ref[...][None, :])
    for _ in range(steps):
        advance(work)
    for kind in range(3):
        owner, copy = home(kind)

        @pl.when(owner != p.member)
        def _():
            copy.wait_send()

    grads_in.drain()
    stats_in.drain()
    for pair, begin in ((down, 1), (up, 0), (inner, 0), (outer, 0)):
        for one in pair:
            for step in range(begin, steps):
                one.drain(step)


def total_kernel(reps, x_ref, o_ref, near, wide, send, recv):
    rep, member = lax.axis_index("rep"), lax.axis_index("grp")
    others = [(rep, lax.rem(member + d, GROUP)) for d in range(1, GROUP)]
    peers = [(lax.rem(rep + k, reps), member) for k in range(1, reps)]
    barrier = pltpu.get_barrier_semaphore()
    for place in others + peers:
        pl.semaphore_signal(barrier, inc=1, device_id=place, device_id_type=MESH)
    pl.semaphore_wait(barrier, len(others) + len(peers))
    lines = x_ref.shape[0] // GROUP

    def quarter(owner):
        return pl.ds(pl.multiple_of(owner * lines, lines), lines)

    def run(copies):
        for copy in copies:
            copy.start()
        for copy in copies:
            copy.wait_recv()

    gather = [
        remote(x_ref.at[quarter(place[1]), :], near.at[d], send.at[d], recv.at[d], place)
        for d, place in enumerate(others)
    ]
    run(gather)
    wide[rep] = x_ref[quarter(member), :] + near[0] + near[1] + near[2]
    base = len(others)
    across = [
        remote(wide.at[rep], wide.at[rep], send.at[base + k], recv.at[base + k], place)
        for k, place in enumerate(peers)
    ]
    run(across)
    total = wide[0]
    for r in range(1, reps):
        total = total + wide[r]
    o_ref[quarter(member), :] = total
    base = base + len(peers)
    share = [
        remote(
            o_ref.at[quarter(member), :], o_ref.at[quarter(member), :],
            send.at[base + d], recv.at[base + d], place,
        )
        for d, place in enumerate(others)
    ]
    run(share)
    for copy in gather + across + share:
        copy.wait_send()


def call(kernel, number, args, outs, scratch, smem=0, limit=63):
    vmem = pl.BlockSpec(memory_space=pltpu.VMEM)
    smem_spec = pl.BlockSpec(memory_space=pltpu.SMEM)
    linked = {} if number is None else {"collective_id": number, "has_side_effects": True}
    return pl.pallas_call(
        kernel,
        out_shape=[jax.ShapeDtypeStruct(*o) for o in outs],
        in_specs=[smem_spec] * smem + [vmem] * (len(args) - smem),
        out_specs=[vmem] * len(outs),
        scratch_shapes=scratch,
        compiler_params=pltpu.CompilerParams(vmem_limit_bytes=limit * 2**20, **linked),
    )(*args)


def per_device(
    tokens,
    cotangent,
    slice_sizes,
    gain_one,
    shift_one,
    attn_in,
    attn_bias,
    attn_out,
    out_bias,
    gain_two,
    shift_two,
    mlp_up,
    up_bias,
    mlp_down,
    down_bias,
):
    capacity, width = tokens.shape
    reps, groups = lax.axis_size("rep"), lax.axis_size("grp")
    assert groups == GROUP
    rows = -(-capacity // 128) * 128
    all_rows = GROUP * rows
    rep, member = lax.axis_index("rep"), lax.axis_index("grp")
    device = rep * groups + member
    ff_rows = mlp_up.shape[0]
    heads_high = GROUP * HP
    devices = reps * groups
    vm = pltpu.VMEM

    deep = -(-(width // reps) // 16) * 16
    own_count = slice_sizes[device]
    live_col = (jnp.arange(capacity, dtype=jnp.int32) < own_count)[:, None]
    w_in = jnp.pad(
        attn_in.reshape(3, GROUP, HD, width), ((0, 0), (0, 0), (0, HP - HD), (0, 0))
    ).reshape(3, heads_high, width)
    bias = jnp.stack([attn_bias[0], jnp.zeros((width,), F32), attn_bias[1]])
    bias = jnp.pad(
        bias.reshape(3 * GROUP, GROUP, HD), ((0, 0), (0, 0), (0, HP - HD))
    ).reshape(3 * GROUP, heads_high)
    w_out = jnp.pad(
        attn_out.reshape(GROUP, HD, width), ((0, 0), (0, HP - HD), (0, 0))
    ).reshape(heads_high, width)
    place = (capacity, reps, rows)
    window_sems = [
        pltpu.SemaphoreType.DMA((len(OFFSETS) * GROUP,)), pltpu.SemaphoreType.DMA((WINDOW,))
    ]

    first, tok, query, window, cot_all = call(
        functools.partial(front_kernel, *place), 1,
        (slice_sizes, tokens, cotangent, gain_one, shift_one, w_in, bias),
        [((all_rows, width), BF), ((rows, width), BF), ((GROUP, heads_high, rows), BF),
         ((2 * WINDOW + GROUP, heads_high, rows), BF), ((all_rows, width), BF)],
        [vm((all_rows, width), BF), vm((3, GROUP, heads_high, rows), BF),
         vm((3, heads_high, all_rows), F32), *dma(5), *dma(5), *dma(4), *window_sems * 2],
        smem=1,
    )
    mixed, lse = call(
        functools.partial(attend_kernel, *place), None, (slice_sizes, query, window),
        [((heads_high, all_rows), BF), ((GROUP, all_rows), F32)],
        [vm((heads_high, all_rows), F32)],
        smem=1,
    )
    gapped = reps * deep

    def halves(high, wide):
        return [((high, lanes.stop - lanes.start), BF) for lanes in split(wide)]

    out, dresid, dmixed, stats, qwindow, *partials, sums_two, dup = call(
        functools.partial(middle_kernel, *place, deep), 2,
        (tok, cot_all, query, mixed, lse, w_out, mlp_up, mlp_down,
         up_bias.reshape(GROUP, ff_rows), out_bias, gain_two, shift_two, down_bias),
        [((rows, width), BF), ((rows, width), F32), ((heads_high, all_rows), BF),
         ((2 * GROUP, all_rows), F32), ((WINDOW, heads_high, rows), BF), *halves(gapped, ff_rows),
         *halves(gapped // 2, ff_rows), *halves(gapped, heads_high), ((4, width), F32),
         ((1, ff_rows), F32)],
        [vm((all_rows, width), BF)] * 3
        + [vm((all_rows, ff_rows), BF)] * 2
        + [vm((all_rows, width), BF), vm((all_rows, ff_rows), F32), *[vm(*o) for o in halves(gapped, ff_rows)],
           vm((rows, width), F32), vm((rows, width), F32), vm((3, 3, rows, width), BF)]
        + dma(3) + dma(5) + dma(3) + dma(5) + dma(3) + window_sems + halving_sems(reps) * 2,
    )
    input_grad, dbias, sums_one, dmlp_up, dmlp_down, dattn_out, dattn_in = call(
        functools.partial(back_kernel, *place, deep), 3,
        (window, qwindow, dmixed, stats, first, w_in.reshape(3 * heads_high, width), tok, dresid,
         gain_one, *partials),
        [((rows, width), F32), ((heads_high, 3), F32), ((2, width), F32),
         ((deep, ff_rows), F32), ((deep, ff_rows), F32), ((deep, heads_high), F32),
         ((deep, 3 * heads_high), F32)],
        [vm((WINDOW, heads_high, rows), BF), vm((WINDOW, 2 * GROUP, rows), F32)]
        + [vm((heads_high, all_rows), F32)] * 2
        + [vm((3, heads_high, all_rows), BF), vm((3 * heads_high, all_rows), BF)]
        + [vm((all_rows, width), BF), vm((3, rows, width), BF)]
        + halving_levels(reps, deep, ff_rows, 1) + halving_levels(reps, deep, ff_rows, 2)
        + halving_levels(reps, deep, heads_high, 1)
        + halving_levels(reps, deep, 3 * heads_high, 0)
        + window_sems * 2 + dma(3) + dma(3) + halving_sems(reps) * 8,
    )
    narrow = width // reps
    dmlp_up, dmlp_down = dmlp_up[:narrow].T, dmlp_down[:narrow].T

    def without_gaps(grads):
        kinds = grads.shape[1] // heads_high
        return (
            grads[:narrow].T.reshape(kinds, GROUP, HP, narrow)[:, :, :HD]
            .reshape(kinds * GROUP * HD, narrow)
        )

    dattn_out, dattn_in = without_gaps(dattn_out), without_gaps(dattn_in)

    def totals(parts):
        flat = jnp.concatenate([part.reshape(-1) for part in parts])
        lines = -(-flat.shape[0] // 4096) * 32
        flat = jnp.pad(flat, (0, lines * 128 - flat.shape[0])).reshape(lines, 128)
        copies = 2 * (groups - 1) + reps - 1
        [summed] = call(
            functools.partial(total_kernel, reps), 0, (flat,), [(flat.shape, F32)],
            [vm((groups - 1, lines // groups, 128), F32), vm((reps, lines // groups, 128), F32),
             *dma(copies)], limit=16,
        )
        summed = summed.reshape(-1)
        spot, outs = 0, []
        for part in parts:
            outs.append(summed[spot : spot + part.size].reshape(part.shape))
            spot += part.size
        return outs

    dbias = dbias.T.reshape(3, GROUP, HP)[:, :, :HD].reshape(3, GROUP * HD)
    dattn_bias = lax.dynamic_update_slice_in_dim(
        jnp.zeros((2, width), F32), dbias[0::2], member * GROUP * HD, 1
    )
    dup_bias = lax.dynamic_update_slice_in_dim(
        jnp.zeros(up_bias.shape, F32), dup[0], member * ff_rows, 0
    )
    dgain_one, dshift_one, dattn_bias, dout_bias, dgain_two, dshift_two, dup_bias, ddown_bias = (
        totals(
            (
                sums_one[0], sums_one[1], dattn_bias, sums_two[0], sums_two[1], sums_two[2],
                dup_bias, sums_two[3],
            )
        )
    )
    block_output = jnp.where(live_col, out[:capacity], jnp.zeros((), BF))
    input_grad = jnp.where(live_col, input_grad[:capacity], 0.0)
    return (
        block_output, input_grad, dgain_one, dshift_one, dattn_in, dattn_bias, dattn_out,
        dout_bias, dgain_two, dshift_two, dmlp_up, dup_bias, dmlp_down, ddown_bias,
    )


def solution(mesh):
    rows, rep_grp = P("grp", None), P(("rep", "grp"), None)
    in_specs = (
        rep_grp, rep_grp, P(), P(), P(), rows, P(), rows, P(), P(), P(), rows, P(), rows, P(),
    )
    grads = P("grp", "rep")
    out_specs = (
        rep_grp, rep_grp, P(), P(), grads, P(), grads, P(), P(), P(), grads, P(), grads, P(),
    )
    return jax.shard_map(
        per_device, mesh=mesh, in_specs=in_specs, out_specs=out_specs, check_vma=False
    )
```
